128 devices in a mesh: orbits: 4 (over z), rows: 8 (over x, core), cols: 4 (over y).
Axes of the slice: x: 4, y: 4, z: 4, core: 2. Of those that a mesh axis runs over, the one named last changes fastest.
Arguments:
- obs_feat: bfloat16 [524288, 128], P(('orbits', 'rows', 'cols')), may hold values from -6 to 6
- obs_offset: bfloat16 [2, 524288], P(None, ('orbits', 'rows', 'cols')), may hold values from -0.5 to 0.5
- obs_cells: int32 [16, 524288], P(None, ('orbits', 'rows', 'cols')), may hold values from 0 to 255, as said below
- block_tile: int32 [4096], P(('orbits', 'rows', 'cols')), may hold values from 0 to 31, as said below
- block_patch: int32 [4096], P(('orbits', 'rows', 'cols')), may hold values from 0 to 31
- w_embed: bfloat16 [128, 128], replicated, may hold values from -0.5 to 0.5
- b_embed: float32 [128], replicated, may hold values from -3 to 3
- w_proj: bfloat16 [128, 128], replicated, may hold values from -0.5 to 0.5
- b_proj: float32 [128], replicated, may hold values from -3 to 3
- density_weight: float32 [128], replicated, may hold values from -4 to 4
- w_first: bfloat16 [3, 3, 128, 128], replicated, may hold values from -0.1875 to 0.1875
- b_first: float32 [128], replicated, may hold values from -3 to 3
- w_second: bfloat16 [3, 3, 128, 128], replicated, may hold values from -0.1875 to 0.1875
- b_second: float32 [128], replicated, may hold values from -3 to 3
Outputs:
- obs_out: bfloat16 [524288, 128], P(('orbits', 'rows', 'cols'))
- grid_out: bfloat16 [512, 512, 128], P(('orbits', 'rows'), 'cols')
The draws below stay inside these ranges and needn't reach their ends.
Inputs may be any that keep to these rules, and one draw needn't show every extreme that they name: `obs_cells`: column o is a 4 by 4 window of cells of a 8 by 32 patch: entry k is (a + k // 4) * 32 + b + k % 4 with 0 <= a <= 4 and 0 <= b <= 28. `block_tile`: tile t is the grid block of the devices with rows index t // 4 and cols index t % 4. Of the 32 blocks of one device, at most 2 name one tile, so one tile gets at most 64 blocks from the devices of one orbits index.
All inputs are finite; a program needn't handle non-finite values.
Results may differ from the reference program's by a relative error of at most 0.013.
Values may be sent and summed in bfloat16 or wider, within the bound.
A program may use at most 64 MiB of HBM per device.

```python
import jax
import jax.numpy as jnp

C = 128
BLK = 128
KN = 16
PH = 8
PW = 32
NBLK_DEV = 32
SR = 16
TC = 128
TILES = 32
MOST = 2
PATCHES = 32
NBLK = 4096
OBS = 524288
GRID_ROWS = 512
GRID_COLS = 512
N_ROWS = 8


def draw_obs_cells(key, part):
    row_key, col_key = jax.random.split(key)
    anchor_row = jax.random.randint(row_key, (OBS,), 0, PH - 3)
    anchor_col = jax.random.randint(col_key, (OBS,), 0, PW - 3)
    tap_ids = jnp.arange(KN)
    cells = (anchor_row[None, :] + tap_ids[:, None] // 4) * PW + anchor_col[None, :] + tap_ids[:, None] % 4
    return cells.astype(jnp.int32)


def draw_block_tile(key, part):
    devices = NBLK // NBLK_DEV
    groups = devices // TILES
    busiest = jax.random.randint(jax.random.fold_in(key, 11), (groups,), 0, TILES)

    def one_device(device):
        device_key = jax.random.fold_in(key, 1000 + device)
        perm_key, shift_key, shuffle_key = jax.random.split(device_key, 3)
        centre = busiest[device // TILES]
        shuffled = jax.random.permutation(perm_key, TILES - 1)
        others = (centre + 1 + shuffled) % TILES
        shift_count = jax.random.randint(shift_key, (), 0, MOST)
        position = jnp.arange(NBLK_DEV - MOST)
        remaining = others[(position + shift_count) // MOST]
        chosen = jnp.concatenate([jnp.full((MOST,), centre, jnp.int32), remaining.astype(jnp.int32)])
        return chosen[jax.random.permutation(shuffle_key, NBLK_DEV)]
    return jax.vmap(one_device)(jnp.arange(devices)).reshape(NBLK).astype(jnp.int32)


def set_ends(result, own_key, smallest, top_value):
    longest = result.shape.index(max(result.shape))
    spots = []
    for shift in (0, 1):
        where = [jax.random.randint(jax.random.fold_in(own_key, axis), (), 0, length) for axis, length in enumerate(result.shape)]
        where[longest] = (where[longest] + shift) % result.shape[longest]
        spots.append(tuple(where))
    return result.at[spots[0]].set(smallest).at[spots[1]].set(top_value)


def level_of(stream_key, dims, cuts, smallest, high):
    factor_of, own = 1.0, jax.random.fold_in(stream_key, 6)
    for axis_at, blocks in cuts:
        draws = jnp.exp(jax.random.uniform(jax.random.fold_in(own, axis_at), (blocks,), jnp.float32, smallest / len(cuts), high / len(cuts)))
        factor_of = factor_of * jnp.repeat(draws, dims[axis_at] // blocks).reshape([-1 if axis == axis_at else 1 for axis in range(len(dims))])
    return factor_of


def scatter_about(rng, dims, scale, reach, shards=(), kind=jnp.bfloat16):
    array = scale * jax.random.normal(rng, dims, jnp.float32)
    if shards:
        array = array * level_of(rng, dims, shards, -0.22, 0.18)
    return jnp.clip(array, -reach, reach).astype(kind)


def setup_inputs(seed: int = 0) -> dict:
    key_of = jax.random.split(jax.random.key(seed), 15)
    obs_feat = scatter_about(key_of[0], (OBS, C), 1.0, 6.0, ((0, 128),))
    obs_offset = jnp.clip(jax.random.uniform(key_of[1], (2, OBS), jnp.float32, -0.5, 0.5) * level_of(key_of[1], (2, OBS), ((1, 128),), -0.4, 0.0), -0.5, 0.5).astype(jnp.bfloat16)
    obs_cells = draw_obs_cells(jax.random.fold_in(key_of[14], 71), 0)
    block_tile = draw_block_tile(jax.random.fold_in(key_of[14], 71), 0)
    block_patch = set_ends(jax.random.randint(key_of[4], (NBLK,), 0, PATCHES), jax.random.fold_in(key_of[4], 1), 0, PATCHES - 1).astype(jnp.int32)
    w_embed = scatter_about(key_of[5], (C, C), C ** -0.5, 0.5)
    b_embed = scatter_about(key_of[6], (C,), 0.5, 3.0, (), jnp.float32)
    w_proj = scatter_about(key_of[7], (C, C), C ** -0.5, 0.5)
    b_proj = scatter_about(key_of[8], (C,), 0.5, 3.0, (), jnp.float32)
    density_weight = scatter_about(key_of[9], (C,), 1.0, 4.0, (), jnp.float32)
    w_first = scatter_about(key_of[10], (3, 3, C, C), (9 * C) ** -0.5, 0.1875)
    b_first = scatter_about(key_of[11], (C,), 0.5, 3.0, (), jnp.float32)
    w_second = scatter_about(key_of[12], (3, 3, C, C), (9 * C) ** -0.5, 0.1875)
    b_second = scatter_about(key_of[13], (C,), 0.5, 3.0, (), jnp.float32)
    return dict(obs_feat=obs_feat, obs_offset=obs_offset, obs_cells=obs_cells, block_tile=block_tile, block_patch=block_patch, w_embed=w_embed, b_embed=b_embed, w_proj=w_proj, b_proj=b_proj, density_weight=density_weight, w_first=w_first, b_first=b_first, w_second=w_second, b_second=b_second)


inverse_width = 0.5


def kernel_taps(obs_offset):
    offsets = obs_offset.astype(jnp.float32)
    tap_ids = jnp.arange(KN)
    tap_row = (tap_ids // 4).astype(jnp.float32)
    tap_col = (tap_ids % 4).astype(jnp.float32)
    delta_row = tap_row[:, None] - 1.5 - offsets[0][None, :]
    delta_col = tap_col[:, None] - 1.5 - offsets[1][None, :]
    return jnp.exp(-(delta_row * delta_row + delta_col * delta_col) * inverse_width).astype(jnp.bfloat16)


def convolve(padded, weight, bias_vec):
    height = padded.shape[-3] - 2
    breadth = padded.shape[-2] - 2
    channels = padded.shape[-1]
    leading = padded.shape[:-3]
    summed = None
    for row_shift in range(3):
        rows_part = padded[..., row_shift:row_shift + height, :, :]
        stacked = jnp.concatenate([rows_part[..., col_shift:col_shift + breadth, :] for col_shift in range(3)], axis=-1)
        product_term = jnp.dot(stacked.reshape(-1, 3 * channels), weight[row_shift].reshape(3 * channels, channels), preferred_element_type=jnp.float32)
        summed = product_term if summed is None else summed + product_term
    return summed.reshape(leading + (height, breadth, channels)) + bias_vec


def reference(obs_feat, obs_offset, obs_cells, block_tile, block_patch, w_embed, b_embed, w_proj, b_proj, density_weight, w_first, b_first, w_second, b_second):
    hidden = jax.nn.silu(jnp.dot(obs_feat, w_embed, preferred_element_type=jnp.float32) + b_embed).astype(jnp.bfloat16)
    features = (jnp.dot(hidden, w_proj, preferred_element_type=jnp.float32) + b_proj).astype(jnp.bfloat16)
    features_wide = features.astype(jnp.float32)
    kernel = kernel_taps(obs_offset).astype(jnp.float32)
    tile_obs = jnp.repeat(block_tile, BLK).astype(jnp.int32)
    patch_obs = jnp.repeat(block_patch, BLK).astype(jnp.int32)
    tiles_across = GRID_COLS // TC
    patches_across = TC // PW
    tile_row = tile_obs // tiles_across
    tile_col = tile_obs % tiles_across
    patch_row = patch_obs // patches_across
    patch_col = patch_obs % patches_across
    local_row = patch_row[None, :] * PH + obs_cells // PW
    grid_row = ((local_row // SR) * N_ROWS + tile_row[None, :]) * SR + local_row % SR
    grid_col = tile_col[None, :] * TC + patch_col[None, :] * PW + obs_cells % PW
    flat_cell = (grid_row * GRID_COLS + grid_col).astype(jnp.int32)
    spread = jnp.zeros((GRID_ROWS * GRID_COLS, C), jnp.float32)
    density = jnp.zeros((GRID_ROWS * GRID_COLS,), jnp.float32)
    for tap in range(KN):
        spread = spread.at[flat_cell[tap]].add(kernel[tap][:, None] * features_wide)
        density = density.at[flat_cell[tap]].add(kernel[tap])
    grid_in = (spread / jnp.maximum(density, 1.0)[:, None] + density_weight[None, :] * (density / (1.0 + density))[:, None]).astype(jnp.bfloat16)
    grid_in = grid_in.reshape(GRID_ROWS, GRID_COLS, C)
    pads = ((1, 1), (1, 1), (0, 0))
    first = jax.nn.silu(convolve(jnp.pad(grid_in, pads), w_first, b_first)).astype(jnp.bfloat16)
    grid_out = (grid_in.astype(jnp.float32) + convolve(jnp.pad(first, pads), w_second, b_second)).astype(jnp.bfloat16)
    values = grid_out.reshape(GRID_ROWS * GRID_COLS, C)
    reading = jnp.zeros((OBS, C), jnp.float32)
    for tap in range(KN):
        reading = reading + kernel[tap][:, None] * values[flat_cell[tap]].astype(jnp.float32)
    reading = (reading / jnp.sum(kernel, axis=0)[:, None]).astype(jnp.bfloat16)
    obs_out = (features_wide + reading.astype(jnp.float32)).astype(jnp.bfloat16)
    return obs_out, grid_out
```

```python
import functools

import jax
import jax.numpy as jnp
from jax import lax
from jax.experimental import pallas as pl
from jax.experimental.pallas import tpu as pltpu
from jax.sharding import PartitionSpec as P

KN = 16
PH = 8
PW = 32
SR = 16
TC = 128
BLK = 128
C = 128
MOST = 2
PAIR = MOST * BLK + 16
MESH = pl.DeviceIdType.MESH
VMEM = pltpu.VMEM
SMEM = pltpu.SMEM


def plane_device(index, cols):
    return (lax.axis_index("orbits"), index // cols, index % cols)


def plane_barrier(me, tiles, cols):
    barrier = pltpu.get_barrier_semaphore()

    def greet(k, carry):
        pl.semaphore_signal(barrier, inc=1, device_id=plane_device((me + k) % tiles, cols), device_id_type=MESH)
        return carry

    lax.fori_loop(1, tiles, greet, 0)
    pl.semaphore_wait(barrier, tiles - 1)


def window_weights(meta_rows):
    off_r, off_c = meta_rows[0:1], meta_rows[1:2]
    anchor_r, anchor_c = meta_rows[2:3], meta_rows[3:4]
    tap_r = lax.broadcasted_iota(jnp.int32, (PH, BLK), 0).astype(jnp.float32) - anchor_r
    tap_c = lax.broadcasted_iota(jnp.int32, (PW, BLK), 0).astype(jnp.float32) - anchor_c
    delta_r = tap_r - 1.5 - off_r
    delta_c = tap_c - 1.5 - off_c
    weight_r = jnp.where((tap_r >= 0.0) & (tap_r < 4.0), jnp.exp(delta_r * delta_r * -0.5), 0.0)
    weight_c = jnp.where((tap_c >= 0.0) & (tap_c < 4.0), jnp.exp(delta_c * delta_c * -0.5), 0.0)
    return jnp.concatenate([(weight_r[r : r + 1] * weight_c).astype(jnp.bfloat16) for r in range(PH)], axis=0)


def scatter_kernel(
    tiles, cols, blocks, block_ref, patch_ref, feat_ref, off_ref, cells_ref, we_ref, be_ref, wp_ref, bp_ref,
    features_ref, got_ref, send, block_meta, send_sem, recv_sem, own_sem,
):
    me = lax.axis_index("rows") * cols + lax.axis_index("cols")
    plane_barrier(me, tiles, cols)
    group = min(4, blocks)

    def embed(i, carry):
        rows = pl.ds(i * group, group)
        x = feat_ref[rows].reshape(group * BLK, C)
        v = jnp.dot(x, we_ref[...], preferred_element_type=jnp.float32) + be_ref[...]
        hidden = (v / (1.0 + jnp.exp(-v))).astype(jnp.bfloat16)
        out = jnp.dot(hidden, wp_ref[...], preferred_element_type=jnp.float32) + bp_ref[...]
        features_ref[rows] = out.astype(jnp.bfloat16).reshape(group, BLK, C)
        return carry

    lax.fori_loop(0, blocks // group, embed, 0)
    row_id = lax.broadcasted_iota(jnp.int32, (8, BLK), 0)
    for b in range(blocks):
        lanes = slice(b * BLK, (b + 1) * BLK)
        off = off_ref[:, lanes].astype(jnp.float32)
        cell = cells_ref[0:1, lanes]
        meta = jnp.where(row_id == 0, off[0:1], 0.0)
        meta = jnp.where(row_id == 1, off[1:2], meta)
        meta = jnp.where(row_id == 2, (cell >> 5).astype(jnp.float32), meta)
        block_meta[b] = jnp.where(row_id == 3, (cell & 31).astype(jnp.float32), meta)

    def out_copy(t):
        return pltpu.make_async_remote_copy(
            src_ref=send.at[t], dst_ref=got_ref.at[me], send_sem=send_sem.at[t], recv_sem=recv_sem.at[me],
            device_id=plane_device(t, cols), device_id_type=MESH,
        )

    def in_copy(s):
        return pltpu.make_async_remote_copy(
            src_ref=send.at[s], dst_ref=got_ref.at[s], send_sem=send_sem.at[s], recv_sem=recv_sem.at[s],
            device_id=plane_device(s, cols), device_id_type=MESH,
        )

    def pack(t):
        metas = []
        for j in range(MOST):
            slot = t * MOST + j
            block = block_ref[slot]
            patch = jnp.full((8, BLK), patch_ref[slot].astype(jnp.float32))
            send[t, j * BLK : (j + 1) * BLK, :] = features_ref[block]
            meta = block_meta[block]
            meta = jnp.where((row_id == 2) & (patch < 0.0), -100.0, meta)
            metas.append(jnp.where(row_id == 4, patch, meta))
        send[t, MOST * BLK :, :] = jnp.concatenate(metas, axis=0).astype(jnp.bfloat16)

    def start_one(k, carry):
        t = (me + k) % tiles
        pack(t)
        out_copy(t).start()
        return carry

    lax.fori_loop(1, tiles, start_one, 0)
    pack(me)
    own = pltpu.make_async_copy(send.at[me], got_ref.at[me], own_sem)
    own.start()
    own.wait()

    def finish(k, carry):
        out_copy((me + k) % tiles).wait_send()
        in_copy((me + tiles - k) % tiles).wait_recv()
        return carry

    lax.fori_loop(1, tiles, finish, 0)


def spread_kernel(tiles, patches, patch_ref, got_ref, spread_ref, density_ref, acc, density_acc):
    step = pl.program_id(0)

    @pl.when(step == 0)
    def _():
        acc[...] = jnp.zeros_like(acc)
        density_acc[...] = jnp.zeros_like(density_acc)

    metas = got_ref[0, MOST * BLK :, :].astype(jnp.float32)
    ones = jnp.ones((8, BLK), jnp.bfloat16)
    for j in range(MOST):
        patch = patch_ref[step * MOST + j]

        @pl.when(patch >= 0)
        def _():
            matrix = window_weights(metas[8 * j : 8 * j + 8])
            acc[patch] += jnp.dot(matrix, got_ref[0, j * BLK : (j + 1) * BLK, :], preferred_element_type=jnp.float32)
            sums = lax.dot_general(ones, matrix, (((1,), (1,)), ((), ())), preferred_element_type=jnp.float32)
            density_acc[pl.ds(patch, 1), :] += sums[0:1]

    @pl.when(step == tiles - 1)
    def _():
        spread_ref[...] = acc[...].astype(jnp.bfloat16)
        density_ref[...] = density_acc[...].astype(jnp.bfloat16)


def read_kernel(
    tiles, cols, blocks, patch_ref, slot_ref, meta_ref, tile_ref, features_ref,
    out_ref, values_ref, send, got, send_sem, recv_sem,
):
    me = lax.axis_index("rows") * cols + lax.axis_index("cols")
    plane_barrier(me, tiles, cols)
    across = TC // PW
    for p in range(values_ref.shape[0]):
        top, left = p // across * PH, p % across * PW
        values_ref[p] = tile_ref[top : top + PH, left : left + PW, :].reshape(PH * PW, C)
    ones = jnp.ones((PH * PW, C), jnp.bfloat16)

    def pair(t):
        return pl.ds(t * MOST, MOST)

    def out_copy(t):
        return pltpu.make_async_remote_copy(
            src_ref=send.at[pair(t)], dst_ref=got.at[pair(me)], send_sem=send_sem.at[t], recv_sem=recv_sem.at[me],
            device_id=plane_device(t, cols), device_id_type=MESH,
        )

    def in_copy(s):
        return pltpu.make_async_remote_copy(
            src_ref=send.at[pair(s)], dst_ref=got.at[pair(s)], send_sem=send_sem.at[s], recv_sem=recv_sem.at[s],
            device_id=plane_device(s, cols), device_id_type=MESH,
        )

    def read(s, target):
        metas = meta_ref[s].astype(jnp.float32)
        for j in range(MOST):
            rows = metas[8 * j : 8 * j + 8]
            row_id = lax.broadcasted_iota(jnp.int32, (8, BLK), 0)
            rows = jnp.where((row_id == 2) & (rows < 0.0), 0.0, rows)
            matrix = window_weights(rows)
            both = jnp.concatenate([values_ref[patch_ref[s * MOST + j]], ones], axis=1)
            summed = lax.dot_general(matrix, both, (((0,), (0,)), ((), ())), preferred_element_type=jnp.float32)
            target[s * MOST + j] = (summed[:, :C] / summed[:, C:]).astype(jnp.bfloat16)

    def start_one(k, carry):
        s = (me + k) % tiles
        read(s, send)
        out_copy(s).start()
        return carry

    lax.fori_loop(1, tiles, start_one, 0)
    read(me, got)

    def finish(k, carry):
        out_copy((me + k) % tiles).wait_send()
        in_copy((me + tiles - k) % tiles).wait_recv()
        return carry

    lax.fori_loop(1, tiles, finish, 0)

    def combine(b, carry):
        reading = got[slot_ref[b]]
        out_ref[b] = (features_ref[b].astype(jnp.float32) + reading.astype(jnp.float32)).astype(jnp.bfloat16)
        return carry

    lax.fori_loop(0, blocks, combine, 0)


def extended(x, sides, width):
    for axis, dim in sides:
        size, length = (lax.axis_size(axis), x.shape[dim])
        up = [(i, (i + 1) % size) for i in range(size - 1)]
        down = [(j, i) for i, j in up]
        last = lax.slice_in_dim(x, length - width, length, axis=dim)
        initial = lax.slice_in_dim(x, 0, width, axis=dim)
        before = lax.ppermute(last, axis, up)
        after = lax.ppermute(initial, axis, down)
        x = jnp.concatenate([before, x, after], axis=dim)
    return x


def convolve(padded, weight, bias_vec):
    height = padded.shape[-3] - 2
    breadth = padded.shape[-2] - 2
    channels = padded.shape[-1]
    summed = None
    for row_shift in range(3):
        rows_part = padded[row_shift : row_shift + height]
        stacked = jnp.concatenate([rows_part[:, s : s + breadth, :] for s in range(3)], axis=-1)
        term = jnp.dot(
            stacked.reshape(-1, 3 * channels), weight[row_shift].reshape(3 * channels, channels),
            preferred_element_type=jnp.float32,
        )
        summed = term if summed is None else summed + term
    return summed.reshape((height, breadth, channels)) + bias_vec


def patches_to_tile(patches, tile_height, tile_width):
    trailing = patches.shape[2:]
    shaped = patches.reshape((tile_height // PH, tile_width // PW, PH, PW) + trailing)
    axes_order = (0, 2, 1, 3) + tuple(range(4, 4 + len(trailing)))
    return shaped.transpose(axes_order).reshape((tile_height, tile_width) + trailing)


def plain_edges(stripe):
    return extended(stripe, ((("orbits", "rows"), 0), ("cols", 1)), 1)


def local(
    obs_feat, obs_offset, obs_cells, block_tile, block_patch, w_embed, b_embed, w_proj, b_proj, density_weight,
    w_first, b_first, w_second, b_second,
):
    blocks = block_tile.shape[0]
    cols = lax.axis_size("cols")
    tiles = lax.axis_size("rows") * cols
    orbits = lax.axis_size("orbits")
    tile_height = orbits * SR
    patches = tile_height // PH * (TC // PW)
    slots = tiles * MOST

    ids = jnp.arange(blocks, dtype=jnp.int32)
    tile_ids = jnp.arange(tiles, dtype=jnp.int32)
    hit = block_tile[None, :] == tile_ids[:, None]
    lowest = jnp.min(jnp.where(hit, ids[None, :], blocks), axis=1)
    highest = jnp.max(jnp.where(hit, ids[None, :], -1), axis=1)
    block_of_slot = jnp.stack([jnp.where(highest >= 0, lowest, -1), jnp.where(highest > lowest, highest, -1)], axis=1).reshape(slots)
    patch_at = jnp.sum(jnp.where(block_of_slot[:, None] == ids[None, :], block_patch[None, :] + 1, 0), axis=1) - 1
    later = jnp.any((block_tile[:, None] == block_tile[None, :]) & (ids[:, None] > ids[None, :]), axis=1)
    slot_of = block_tile * MOST + later.astype(jnp.int32)

    vm = pl.BlockSpec(memory_space=VMEM)
    sm = pl.BlockSpec(memory_space=SMEM)
    anyspace = pl.BlockSpec(memory_space=pl.ANY)
    features, got = pl.pallas_call(
        functools.partial(scatter_kernel, tiles, cols, blocks),
        grid=(1,),
        out_shape=(
            jax.ShapeDtypeStruct((blocks, BLK, C), jnp.bfloat16),
            jax.ShapeDtypeStruct((tiles, PAIR, C), jnp.bfloat16),
        ),
        in_specs=[sm, sm, vm, vm, pl.BlockSpec((8, blocks * BLK), lambda i: (0, 0)), vm, vm, vm, vm],
        out_specs=(vm, anyspace),
        scratch_shapes=[
            VMEM((tiles, PAIR, C), jnp.bfloat16),
            VMEM((blocks, 8, BLK), jnp.float32),
            pltpu.SemaphoreType.DMA((tiles,)),
            pltpu.SemaphoreType.DMA((tiles,)),
            pltpu.SemaphoreType.DMA,
        ],
        compiler_params=pltpu.CompilerParams(collective_id=0, has_side_effects=True),
        name="embed_and_send",
    )(jnp.maximum(block_of_slot, 0), patch_at, obs_feat.reshape(blocks, BLK, C), obs_offset, obs_cells, w_embed, b_embed[None, :], w_proj, b_proj[None, :])

    got_patch = jnp.stack([got[:, MOST * BLK + 4, 0], got[:, MOST * BLK + 12, 0]], axis=1).astype(jnp.int32).reshape(slots)

    spread, density = pl.pallas_call(
        functools.partial(spread_kernel, tiles, patches),
        grid_spec=pltpu.PrefetchScalarGridSpec(
            num_scalar_prefetch=1,
            grid=(tiles,),
            in_specs=[pl.BlockSpec((1, PAIR, C), lambda i, p: (i, 0, 0))],
            out_specs=(
                pl.BlockSpec((patches, PH * PW, C), lambda i, p: (0, 0, 0)),
                pl.BlockSpec((patches, PH * PW), lambda i, p: (0, 0)),
            ),
            scratch_shapes=[VMEM((patches, PH * PW, C), jnp.float32), VMEM((patches, PH * PW), jnp.float32)],
        ),
        out_shape=(
            jax.ShapeDtypeStruct((patches, PH * PW, C), jnp.bfloat16),
            jax.ShapeDtypeStruct((patches, PH * PW), jnp.bfloat16),
        ),
        name="spread",
    )(got_patch, got)

    spread_tile = patches_to_tile(spread, tile_height, TC)
    density_tile = patches_to_tile(density, tile_height, TC)
    spread_part = lax.psum_scatter(spread_tile, "orbits", scatter_dimension=0, tiled=True).astype(jnp.float32)
    density_part = lax.psum_scatter(density_tile, "orbits", scatter_dimension=0, tiled=True).astype(jnp.float32)
    grid_in = (
        spread_part / jnp.maximum(density_part, 1.0)[..., None]
        + density_weight * (density_part / (1.0 + density_part))[..., None]
    ).astype(jnp.bfloat16)
    first = jax.nn.silu(convolve(plain_edges(grid_in), w_first, b_first)).astype(jnp.bfloat16)
    grid_out = (grid_in.astype(jnp.float32) + convolve(plain_edges(first), w_second, b_second)).astype(jnp.bfloat16)
    full_out = lax.all_gather(grid_out, "orbits", axis=0, tiled=True)

    obs_out = pl.pallas_call(
        functools.partial(read_kernel, tiles, cols, blocks),
        grid=(1,),
        out_shape=jax.ShapeDtypeStruct((blocks, BLK, C), jnp.bfloat16),
        in_specs=[sm, sm, pl.BlockSpec((tiles, 16, C), lambda i: (0, MOST * BLK // 16, 0)), vm, vm],
        out_specs=vm,
        scratch_shapes=[
            VMEM((patches, PH * PW, C), jnp.bfloat16),
            VMEM((slots, BLK, C), jnp.bfloat16),
            VMEM((slots, BLK, C), jnp.bfloat16),
            pltpu.SemaphoreType.DMA((tiles,)),
            pltpu.SemaphoreType.DMA((tiles,)),
        ],
        compiler_params=pltpu.CompilerParams(collective_id=1, has_side_effects=True),
        name="read_and_return",
    )(jnp.maximum(got_patch, 0), slot_of, got, full_out, features)
    return (obs_out.reshape(obs_feat.shape), grid_out)


def solution(mesh):
    spread_out = P(("orbits", "rows", "cols"), None)
    in_specs = (
        spread_out, P(None, ("orbits", "rows", "cols")), P(None, ("orbits", "rows", "cols")),
        P(("orbits", "rows", "cols")), P(("orbits", "rows", "cols")),
        P(), P(), P(), P(), P(), P(), P(), P(), P(),
    )
    out_specs = (spread_out, P(("orbits", "rows"), "cols", None))
    return jax.shard_map(local, mesh=mesh, in_specs=in_specs, out_specs=out_specs, check_vma=False)
```

```python
import functools

import jax
import jax.numpy as jnp
from jax import lax
from jax.experimental import pallas as pl
from jax.experimental.pallas import tpu as pltpu
from jax.sharding import PartitionSpec as P

KN = 16
PH = 8
PW = 32
SR = 16
TC = 128
BLK = 128
C = 128
MOST = 2
CELLS = PH * PW
PATCHES = SR // PH * (TC // PW)
DENS = 2 * PATCHES
PAIR = MOST * BLK + 16
MESH = pl.DeviceIdType.MESH
VMEM = pltpu.VMEM
SMEM = pltpu.SMEM


def plane_device(index, cols):
    return (lax.axis_index("orbits"), index // cols, index % cols)


def plane_barrier(me, tiles, cols):
    barrier = pltpu.get_barrier_semaphore()

    def greet(k, carry):
        pl.semaphore_signal(barrier, inc=1, device_id=plane_device((me + k) % tiles, cols), device_id_type=MESH)
        return carry

    lax.fori_loop(1, tiles, greet, 0)
    pl.semaphore_wait(barrier, tiles - 1)


def window_weights(meta_rows):
    off_r, off_c = meta_rows[0:1], meta_rows[1:2]
    anchor_r, anchor_c = meta_rows[2:3], meta_rows[3:4]
    tap_r = lax.broadcasted_iota(jnp.int32, (PH, BLK), 0).astype(jnp.float32) - anchor_r
    tap_c = lax.broadcasted_iota(jnp.int32, (PW, BLK), 0).astype(jnp.float32) - anchor_c
    delta_r = tap_r - 1.5 - off_r
    delta_c = tap_c - 1.5 - off_c
    weight_r = jnp.where((tap_r >= 0.0) & (tap_r < 4.0), jnp.exp(delta_r * delta_r * -0.5), 0.0)
    weight_c = jnp.where((tap_c >= 0.0) & (tap_c < 4.0), jnp.exp(delta_c * delta_c * -0.5), 0.0)
    return jnp.concatenate([(weight_r[r : r + 1] * weight_c).astype(jnp.bfloat16) for r in range(PH)], axis=0)


def scatter_kernel(
    tiles, cols, blocks, block_ref, patch_ref, feat_ref, off_ref, cells_ref, we_ref, be_ref, wp_ref, bp_ref,
    features_ref, got_ref, send, block_meta, send_sem, recv_sem, own_sem,
):
    me = lax.axis_index("rows") * cols + lax.axis_index("cols")
    plane_barrier(me, tiles, cols)
    group = min(4, blocks)

    def embed(i, carry):
        rows = pl.ds(i * group, group)
        x = feat_ref[rows].reshape(group * BLK, C)
        v = jnp.dot(x, we_ref[...], preferred_element_type=jnp.float32) + be_ref[...]
        hidden = (v / (1.0 + jnp.exp(-v))).astype(jnp.bfloat16)
        out = jnp.dot(hidden, wp_ref[...], preferred_element_type=jnp.float32) + bp_ref[...]
        features_ref[rows] = out.astype(jnp.bfloat16).reshape(group, BLK, C)
        return carry

    lax.fori_loop(0, blocks // group, embed, 0)
    row_id = lax.broadcasted_iota(jnp.int32, (8, BLK), 0)
    for b in range(blocks):
        lanes = slice(b * BLK, (b + 1) * BLK)
        off = off_ref[:, lanes].astype(jnp.float32)
        cell = cells_ref[0:1, lanes]
        meta = jnp.where(row_id == 0, off[0:1], 0.0)
        meta = jnp.where(row_id == 1, off[1:2], meta)
        meta = jnp.where(row_id == 2, (cell >> 5).astype(jnp.float32), meta)
        block_meta[b] = jnp.where(row_id == 3, (cell & 31).astype(jnp.float32), meta)

    def out_copy(t):
        return pltpu.make_async_remote_copy(
            src_ref=send.at[t], dst_ref=got_ref.at[me], send_sem=send_sem.at[t], recv_sem=recv_sem.at[me],
            device_id=plane_device(t, cols), device_id_type=MESH,
        )

    def in_copy(s):
        return pltpu.make_async_remote_copy(
            src_ref=send.at[s], dst_ref=got_ref.at[s], send_sem=send_sem.at[s], recv_sem=recv_sem.at[s],
            device_id=plane_device(s, cols), device_id_type=MESH,
        )

    def pack(t):
        metas = []
        for j in range(MOST):
            slot = t * MOST + j
            block = block_ref[slot]
            patch = jnp.full((8, BLK), patch_ref[slot].astype(jnp.float32))
            send[t, j * BLK : (j + 1) * BLK, :] = features_ref[block]
            meta = block_meta[block]
            meta = jnp.where((row_id == 2) & (patch < 0.0), -100.0, meta)
            metas.append(jnp.where(row_id == 4, patch, meta))
        send[t, MOST * BLK :, :] = jnp.concatenate(metas, axis=0).astype(jnp.bfloat16)

    def start_one(k, carry):
        t = (me + k) % tiles
        pack(t)
        out_copy(t).start()
        return carry

    lax.fori_loop(1, tiles, start_one, 0)
    pack(me)
    own = pltpu.make_async_copy(send.at[me], got_ref.at[me], own_sem)
    own.start()
    own.wait()

    def finish(k, carry):
        out_copy((me + k) % tiles).wait_send()
        in_copy((me + tiles - k) % tiles).wait_recv()
        return carry

    lax.fori_loop(1, tiles, finish, 0)


def spread_kernel(tiles, orbits, group, patch_ref, got_ref, part_ref, acc, density_acc):
    step = pl.program_id(0)

    @pl.when(step == 0)
    def _():
        acc[...] = jnp.zeros_like(acc)
        density_acc[...] = jnp.zeros_like(density_acc)

    ones = jnp.ones((8, BLK), jnp.bfloat16)
    found = []
    for g in range(group):
        metas = got_ref[g, MOST * BLK :, :].astype(jnp.float32)
        for j in range(MOST):
            matrix = window_weights(metas[8 * j : 8 * j + 8])
            spread = jnp.dot(matrix, got_ref[g, j * BLK : (j + 1) * BLK, :], preferred_element_type=jnp.float32)
            sums = lax.dot_general(ones, matrix, (((1,), (1,)), ((), ())), preferred_element_type=jnp.float32)
            found.append((patch_ref[(step * group + g) * MOST + j], spread, sums[0:1]))
    for patch, spread, sums in found:
        acc[patch] += spread
        density_acc[pl.ds(patch, 1), :] += sums

    @pl.when(step == tiles // group - 1)
    def _():
        own = PATCHES
        for z in range(orbits):
            part_ref[z, : own * CELLS, :] = acc[z * own : (z + 1) * own].reshape(own * CELLS, C).astype(jnp.bfloat16)
            sums = density_acc[z * own : (z + 1) * own, :]
            rows = jnp.concatenate([sums[:, :C], sums[:, C:]], axis=0)
            part_ref[z, own * CELLS :, :] = rows.astype(jnp.bfloat16)


def grid_kernel(
    rows, cols, blocks, patch_ref, slot_ref, part_ref, meta_ref, features_ref, dw_ref, w1_ref, b1_ref, w2_ref, b2_ref,
    out_ref, grid_ref,
    relay_in, relay_out, part_in, tile, wide, first, col_out, row_in, col_in, mine, values, send, got,
    ring_send, ring_recv, gather_send, gather_recv, edge_send, edge_recv, send_sem, recv_sem,
):
    z, r, c = lax.axis_index("orbits"), lax.axis_index("rows"), lax.axis_index("cols")
    orbits = 4
    tiles = rows * cols
    stripes = orbits * rows
    me = r * cols + c
    stripe = z * rows + r
    after, before = (z + 1) % orbits, (z + orbits - 1) % orbits
    across = (z + 2) % orbits
    half = PATCHES * CELLS // 2

    def edge_device(up, side):
        other = (stripe + stripes + up) % stripes
        return (other // rows, other % rows, (c + cols + side) % cols)

    edges = ((-1, 0), (1, 0), (-1, -1), (0, -1), (1, -1), (-1, 1), (0, 1), (1, 1))
    barrier = pltpu.get_barrier_semaphore()

    def greet(k, carry):
        pl.semaphore_signal(barrier, inc=1, device_id=plane_device((me + k) % tiles, cols), device_id_type=MESH)
        return carry

    lax.fori_loop(1, tiles, greet, 0)
    for other in (after, before):
        pl.semaphore_signal(barrier, inc=1, device_id=(other, r, c), device_id_type=MESH)
    for up, side in edges:
        pl.semaphore_signal(barrier, inc=1, device_id=edge_device(up, side), device_id_type=MESH)
    pl.semaphore_wait(barrier, tiles - 1 + 2 + len(edges))

    sides = ((0, after, pl.ds(0, half), pl.ds(half, half + DENS)), (1, before, pl.ds(half, half + DENS), pl.ds(0, half)))

    def ring_copy(src, dst, way, step, other):
        return pltpu.make_async_remote_copy(
            src_ref=src, dst_ref=dst, send_sem=ring_send.at[way, step], recv_sem=ring_recv.at[way, step],
            device_id=(other, r, c), device_id_type=MESH,
        )

    ring = []
    for way, other, passed, direct in sides:
        relay = ring_copy(part_ref.at[across, passed], relay_in.at[passed], way, 0, other)
        straight = ring_copy(part_ref.at[other, direct], part_in.at[way, direct], way, 1, other)
        summed = ring_copy(relay_out.at[passed], part_in.at[way, passed], way, 2, other)
        relay.start()
        straight.start()
        ring.append((relay, straight, summed))
    for way, other, passed, direct in sides:
        relay, straight, summed = ring[way]
        relay.wait_recv()
        total = part_ref[other, passed].astype(jnp.float32) + relay_in[passed].astype(jnp.float32)
        relay_out[passed] = total.astype(jnp.bfloat16)
        summed.start()
    for relay, straight, summed in ring:
        straight.wait_recv()
    for relay, straight, summed in ring:
        summed.wait_recv()

    tail = pl.ds(PATCHES * CELLS, DENS)
    parts = jnp.concatenate([part_ref[z, tail], part_in[0, tail], part_in[1, tail]], axis=0)
    picked = lax.broadcasted_iota(jnp.int32, (3 * DENS, DENS * C), 0) % DENS == lax.broadcasted_iota(jnp.int32, (3 * DENS, DENS * C), 1) // C
    density_all = lax.dot_general(
        parts, picked.astype(jnp.bfloat16), (((0,), (0,)), ((), ())), preferred_element_type=jnp.float32
    )
    weight = dw_ref[...]
    wide_patches = TC // PW
    for p in range(PATCHES):
        for h in range(2):
            k = h * PATCHES + p
            density = density_all[:, k * C : (k + 1) * C]
            cells = pl.ds(p * CELLS + h * C, C)
            total = part_ref[z, cells].astype(jnp.float32) + part_in[0, cells].astype(jnp.float32) + part_in[1, cells].astype(jnp.float32)
            value = total / jnp.maximum(density, 1.0) + weight * (density / (1.0 + density))
            top, left = p // wide_patches * PH + h * (PH // 2), p % wide_patches * PW
            tile[top : top + PH // 2, left : left + PW, :] = value.astype(jnp.bfloat16).reshape(PH // 2, PW, C)

    row_id = lax.broadcasted_iota(jnp.int32, (TC, C), 0)

    def exchange(source, turn):
        for i in range(SR):
            col_out[turn, 0, i : i + 1, :] = source[i, 0:1, :]
            col_out[turn, 1, i : i + 1, :] = source[i, TC - 1 : TC, :]
        copies = []
        for e, (up, side) in enumerate(edges):
            if side == 0:
                src, dst = source.at[0 if up < 0 else SR - 1], row_in.at[turn, e]
            else:
                src, dst = col_out.at[turn, 0 if side < 0 else 1], col_in.at[turn, e - 2]
            copies.append(pltpu.make_async_remote_copy(
                src_ref=src, dst_ref=dst, send_sem=edge_send.at[turn, e], recv_sem=edge_recv.at[turn, e],
                device_id=edge_device(up, side), device_id_type=MESH,
            ))
        for copy in copies:
            copy.start()

        def shifts(row, centre):
            centre = centre.astype(jnp.float32)
            wide[row, :, 0:C] = pltpu.roll(centre, 1, 0).astype(jnp.bfloat16)
            wide[row, :, C : 2 * C] = centre.astype(jnp.bfloat16)
            wide[row, :, 2 * C :] = pltpu.roll(centre, TC - 1, 0).astype(jnp.bfloat16)

        for i in range(SR):
            shifts(i + 1, source[i])
        for copy in copies:
            copy.wait_recv()
        from_above, from_below = row_in[turn, 1], row_in[turn, 0]
        shifts(0, jnp.where(stripe > 0, from_above.astype(jnp.float32), 0.0))
        shifts(SR + 1, jnp.where(stripe < stripes - 1, from_below.astype(jnp.float32), 0.0))
        left_open, right_open = c > 0, c < cols - 1
        for first_edge, lanes, at, open_ in ((3, slice(0, C), 0, left_open), (0, slice(2 * C, 3 * C), TC - 1, right_open)):
            above = col_in[turn, first_edge + 2, SR - 1 : SR, :].astype(jnp.float32)
            level = col_in[turn, first_edge + 1].astype(jnp.float32)
            below = col_in[turn, first_edge, 0:1, :].astype(jnp.float32)
            above = jnp.where(open_ & (stripe > 0), above, 0.0)
            level = jnp.where(open_, level, 0.0)
            below = jnp.where(open_ & (stripe < stripes - 1), below, 0.0)
            wide[0, at : at + 1, lanes] = above.astype(jnp.bfloat16)
            wide[SR + 1, at : at + 1, lanes] = below.astype(jnp.bfloat16)
            for i in range(SR):
                wide[i + 1, at : at + 1, lanes] = level[i : i + 1].astype(jnp.bfloat16)
        return copies

    block_rows = 4

    def convolved(i, w_ref, b_ref):
        total = None
        for a in range(3):
            x = wide[pl.ds(i + a, block_rows)].reshape(block_rows * TC, 3 * C)
            term = jnp.dot(x, w_ref[a], preferred_element_type=jnp.float32)
            total = term if total is None else total + term
        return total + b_ref[...]

    edge_copies = exchange(tile, 0)
    for i in range(0, SR, block_rows):
        v = convolved(i, w1_ref, b1_ref)
        v = v / (1.0 + jnp.exp(-v))
        first[i : i + block_rows] = v.astype(jnp.bfloat16).reshape(block_rows, TC, C)
    edge_copies += exchange(first, 1)

    count = PATCHES // 2

    def half_of(owner, h):
        return values.at[pl.ds(owner * PATCHES + h * count, count)]

    def gather_copy(owner, h, way, step, other, src):
        return pltpu.make_async_remote_copy(
            src_ref=src, dst_ref=half_of(owner, h), send_sem=gather_send.at[way, step], recv_sem=gather_recv.at[way, step],
            device_id=(other, r, c), device_id_type=MESH,
        )

    gathers = []
    for h in range(2):
        for i in range(h * PH, (h + 1) * PH, block_rows):
            v = convolved(i, w2_ref, b2_ref).reshape(block_rows, TC, C)
            v = (tile[i : i + block_rows].astype(jnp.float32) + v).astype(jnp.bfloat16)
            grid_ref[i : i + block_rows] = v
            for q in range(wide_patches):
                cells = pl.ds((i - h * PH) * PW, block_rows * PW)
                mine[h * count + q, cells, :] = v[:, q * PW : (q + 1) * PW, :].reshape(block_rows * PW, C)
        for way, other in ((0, after), (1, before)):
            copy = gather_copy(z, h, way, h, other, mine.at[pl.ds(h * count, count)])
            copy.start()
            gathers.append(copy)
    values[pl.ds(z * PATCHES, PATCHES)] = mine[...]
    for way, other, owner in ((0, after, before), (1, before, after)):
        gather_copy(owner, way, way, way, other, half_of(owner, way)).wait_recv()
        copy = gather_copy(owner, way, way, 2, other, half_of(owner, way))
        copy.start()
        gathers.append(copy)
    for way, other, owner in ((0, after, before), (1, before, after)):
        gather_copy(owner, 1 - way, way, 1 - way, other, half_of(owner, 1 - way)).wait_recv()
    for way, other in ((0, after), (1, before)):
        gather_copy(across, way, way, 2, other, half_of(across, way)).wait_recv()

    ones = jnp.ones((CELLS, C), jnp.bfloat16)

    def pair(t):
        return pl.ds(t * MOST, MOST)

    def out_copy(t):
        return pltpu.make_async_remote_copy(
            src_ref=send.at[pair(t)], dst_ref=got.at[pair(me)], send_sem=send_sem.at[t], recv_sem=recv_sem.at[me],
            device_id=plane_device(t, cols), device_id_type=MESH,
        )

    def in_copy(s):
        return pltpu.make_async_remote_copy(
            src_ref=send.at[pair(s)], dst_ref=got.at[pair(s)], send_sem=send_sem.at[s], recv_sem=recv_sem.at[s],
            device_id=plane_device(s, cols), device_id_type=MESH,
        )

    def read(s, target):
        metas = meta_ref[s].astype(jnp.float32)
        for j in range(MOST):
            meta = metas[8 * j : 8 * j + 8]
            meta_id = lax.broadcasted_iota(jnp.int32, (8, BLK), 0)
            meta = jnp.where((meta_id == 2) & (meta < 0.0), 0.0, meta)
            matrix = window_weights(meta)
            both = jnp.concatenate([values[patch_ref[s * MOST + j]], ones], axis=1)
            summed = lax.dot_general(matrix, both, (((0,), (0,)), ((), ())), preferred_element_type=jnp.float32)
            target[s * MOST + j] = (summed[:, :C] / summed[:, C:]).astype(jnp.bfloat16)

    def start_one(k, carry):
        s = (me + k) % tiles
        read(s, send)
        out_copy(s).start()
        return carry

    lax.fori_loop(1, tiles, start_one, 0)
    read(me, got)

    def finish(k, carry):
        out_copy((me + k) % tiles).wait_send()
        in_copy((me + tiles - k) % tiles).wait_recv()
        return carry

    lax.fori_loop(1, tiles, finish, 0)

    def combine(b, carry):
        reading = got[slot_ref[b]]
        out_ref[b] = (features_ref[b].astype(jnp.float32) + reading.astype(jnp.float32)).astype(jnp.bfloat16)
        return carry

    lax.fori_loop(0, blocks, combine, 0)
    for copies in ring:
        for copy in copies:
            copy.wait_send()
    for copy in gathers + edge_copies:
        copy.wait_send()


def local(
    obs_feat, obs_offset, obs_cells, block_tile, block_patch, w_embed, b_embed, w_proj, b_proj, density_weight,
    w_first, b_first, w_second, b_second,
):
    blocks = block_tile.shape[0]
    cols = lax.axis_size("cols")
    tiles = lax.axis_size("rows") * cols
    orbits = lax.axis_size("orbits")
    tile_height = orbits * SR
    patches = tile_height // PH * (TC // PW)
    slots = tiles * MOST

    ids = jnp.arange(blocks, dtype=jnp.int32)
    tile_ids = jnp.arange(tiles, dtype=jnp.int32)
    hit = block_tile[None, :] == tile_ids[:, None]
    lowest = jnp.min(jnp.where(hit, ids[None, :], blocks), axis=1)
    highest = jnp.max(jnp.where(hit, ids[None, :], -1), axis=1)
    block_of_slot = jnp.stack([jnp.where(highest >= 0, lowest, -1), jnp.where(highest > lowest, highest, -1)], axis=1).reshape(slots)
    patch_at = jnp.sum(jnp.where(block_of_slot[:, None] == ids[None, :], block_patch[None, :] + 1, 0), axis=1) - 1
    later = jnp.any((block_tile[:, None] == block_tile[None, :]) & (ids[:, None] > ids[None, :]), axis=1)
    slot_of = block_tile * MOST + later.astype(jnp.int32)

    vm = pl.BlockSpec(memory_space=VMEM)
    sm = pl.BlockSpec(memory_space=SMEM)
    anyspace = pl.BlockSpec(memory_space=pl.ANY)
    features, got = pl.pallas_call(
        functools.partial(scatter_kernel, tiles, cols, blocks),
        grid=(1,),
        out_shape=(
            jax.ShapeDtypeStruct((blocks, BLK, C), jnp.bfloat16),
            jax.ShapeDtypeStruct((tiles, PAIR, C), jnp.bfloat16),
        ),
        in_specs=[sm, sm, vm, vm, pl.BlockSpec((8, blocks * BLK), lambda i: (0, 0)), vm, vm, vm, vm],
        out_specs=(vm, anyspace),
        scratch_shapes=[
            VMEM((tiles, PAIR, C), jnp.bfloat16),
            VMEM((blocks, 8, BLK), jnp.float32),
            pltpu.SemaphoreType.DMA((tiles,)),
            pltpu.SemaphoreType.DMA((tiles,)),
            pltpu.SemaphoreType.DMA,
        ],
        compiler_params=pltpu.CompilerParams(collective_id=0, has_side_effects=True),
        name="embed_and_send",
    )(jnp.maximum(block_of_slot, 0), patch_at, obs_feat.reshape(blocks, BLK, C), obs_offset, obs_cells, w_embed, b_embed[None, :], w_proj, b_proj[None, :])

    got_patch = jnp.stack([got[:, MOST * BLK + 4, 0], got[:, MOST * BLK + 12, 0]], axis=1).astype(jnp.int32).reshape(slots)
    got_patch = jnp.maximum(got_patch, 0)

    group = min(4, tiles)
    rows_out = PATCHES * CELLS + DENS
    part = pl.pallas_call(
        functools.partial(spread_kernel, tiles, orbits, group),
        grid_spec=pltpu.PrefetchScalarGridSpec(
            num_scalar_prefetch=1,
            grid=(tiles // group,),
            in_specs=[pl.BlockSpec((group, PAIR, C), lambda i, p: (i, 0, 0))],
            out_specs=pl.BlockSpec((orbits, rows_out, C), lambda i, p: (0, 0, 0)),
            scratch_shapes=[VMEM((patches, CELLS, C), jnp.float32), VMEM((patches, CELLS), jnp.float32)],
        ),
        out_shape=jax.ShapeDtypeStruct((orbits, rows_out, C), jnp.bfloat16),
        name="spread",
    )(got_patch, got)

    half = PATCHES * CELLS // 2
    bf = jnp.bfloat16
    obs_out, grid_out = pl.pallas_call(
        functools.partial(grid_kernel, tiles // cols, cols, blocks),
        grid=(1,),
        out_shape=(jax.ShapeDtypeStruct((blocks, BLK, C), bf), jax.ShapeDtypeStruct((SR, TC, C), bf)),
        in_specs=[sm, sm, vm, pl.BlockSpec((tiles, 16, C), lambda i: (0, MOST * BLK // 16, 0)), vm, vm, vm, vm, vm, vm],
        out_specs=(vm, vm),
        scratch_shapes=[
            VMEM((rows_out, C), bf),
            VMEM((rows_out, C), bf),
            VMEM((2, rows_out, C), bf),
            VMEM((SR, TC, C), bf),
            VMEM((SR + 2, TC, 3 * C), bf),
            VMEM((SR, TC, C), bf),
            VMEM((2, 2, SR, C), bf),
            VMEM((2, 2, TC, C), bf),
            VMEM((2, 6, SR, C), bf),
            VMEM((PATCHES, CELLS, C), bf),
            VMEM((patches, CELLS, C), bf),
            VMEM((slots, BLK, C), bf),
            VMEM((slots, BLK, C), bf),
            pltpu.SemaphoreType.DMA((2, 3)),
            pltpu.SemaphoreType.DMA((2, 3)),
            pltpu.SemaphoreType.DMA((2, 3)),
            pltpu.SemaphoreType.DMA((2, 3)),
            pltpu.SemaphoreType.DMA((2, 8)),
            pltpu.SemaphoreType.DMA((2, 8)),
            pltpu.SemaphoreType.DMA((tiles,)),
            pltpu.SemaphoreType.DMA((tiles,)),
        ],
        compiler_params=pltpu.CompilerParams(collective_id=1, has_side_effects=True, vmem_limit_bytes=60000000),
        name="grid_and_read",
    )(
        got_patch, slot_of, part, got, features, density_weight[None, :],
        w_first.reshape(3, 3 * C, C), b_first[None, :], w_second.reshape(3, 3 * C, C), b_second[None, :],
    )
    return (obs_out.reshape(obs_feat.shape), grid_out)


def solution(mesh):
    spread_out = P(("orbits", "rows", "cols"), None)
    in_specs = (
        spread_out, P(None, ("orbits", "rows", "cols")), P(None, ("orbits", "rows", "cols")),
        P(("orbits", "rows", "cols")), P(("orbits", "rows", "cols")),
        P(), P(), P(), P(), P(), P(), P(), P(), P(),
    )
    out_specs = (spread_out, P(("orbits", "rows"), "cols", None))
    return jax.shard_map(local, mesh=mesh, in_specs=in_specs, out_specs=out_specs, check_vma=False)
```

```python
import functools

import jax
import jax.numpy as jnp
from jax import lax
from jax.experimental import pallas as pl
from jax.experimental.pallas import tpu as pltpu
from jax.sharding import PartitionSpec as P

PH = 8
PW = 32
SR = 16
TC = 128
BLK = 128
C = 128
HALF = C // 2
MOST = 2
CELLS = PH * PW
FOLD = CELLS // 2
WIDE = TC // PW
PATCHES = SR // PH * WIDE
DENS = 2 * PATCHES
META = 16
ORBITS = 4
MESH = pl.DeviceIdType.MESH
VMEM = pltpu.VMEM
SMEM = pltpu.SMEM
BF = jnp.bfloat16
F32 = jnp.float32


def table_kernel(blocks, slots, tile_ref, patch_ref, block_at, patch_at, rank_of, count):
    def clear(s, carry):
        block_at[s] = 0
        patch_at[s] = -1
        return carry

    def empty(t, carry):
        count[t] = 0
        return carry

    lax.fori_loop(0, slots, clear, 0)
    lax.fori_loop(0, slots // MOST, empty, 0)

    def place(b, carry):
        t = tile_ref[b]
        rank = count[t]
        count[t] = rank + 1
        rank_of[b] = rank
        block_at[t * MOST + rank] = b
        patch_at[t * MOST + rank] = patch_ref[b]
        return carry

    lax.fori_loop(0, blocks, place, 0)


def window_weights(meta_rows):
    off_r, off_c = meta_rows[0:1], meta_rows[1:2]
    anchor_r, anchor_c = meta_rows[2:3], meta_rows[3:4]
    tap_r = lax.broadcasted_iota(jnp.int32, (PH, BLK), 0).astype(F32) - anchor_r
    tap_c = lax.broadcasted_iota(jnp.int32, (PW, BLK), 0).astype(F32) - anchor_c
    delta_r = tap_r - 1.5 - off_r
    delta_c = tap_c - 1.5 - off_c
    weight_r = jnp.where((tap_r >= 0.0) & (tap_r < 4.0), jnp.exp(delta_r * delta_r * -0.5), 0.0)
    weight_c = jnp.where((tap_c >= 0.0) & (tap_c < 4.0), jnp.exp(delta_c * delta_c * -0.5), 0.0)
    return jnp.concatenate([(weight_r[r : r + 1] * weight_c).astype(BF) for r in range(PH)], axis=0)


def swapped(x):
    return pltpu.roll(x.astype(F32), HALF, 1)


def main_kernel(
    rows, cols, blocks,
    block_at, patch_at, tile_of, rank_of,
    feat_ref, off_ref, cells_ref, we_ref, be_ref, wp_ref, bp_ref, dw_ref, w1_ref, b1_ref, w2_ref, b2_ref,
    out_ref, grid_ref,
    features, swapped_features, block_meta, send0, send1, got0, got1, matrices, patch_rows,
    sums0, sums1, density_sums, links, links_smem, density_rows, part0, part1, density_part, relay_in, relay_out, part_in,
    packed, tile, wide, first, col_out, row_in, col_in, mine, values0, values1, values_swapped, back_out, back_in,
    out_send, out_recv, ring_send, ring_recv, edge_send, edge_recv, gather_send, gather_recv, back_send, back_recv, link_sem,
):
    z, r, c = lax.axis_index("orbits"), lax.axis_index("rows"), lax.axis_index("cols")
    tiles = rows * cols
    slots = tiles * MOST
    stripes = ORBITS * rows
    stripe = z * rows + r
    after, before = (z + 1) % ORBITS, (z + ORBITS - 1) % ORBITS
    across = (z + 2) % ORBITS

    def offset_of(j):
        return (j - 1 + tiles // 2) % (tiles - 1) + 1

    def target(j):
        k = offset_of(j)
        return (r + k // cols) % rows, (c + k % cols) % cols

    def source(j):
        k = offset_of(j)
        return (r + rows - k // cols) % rows, (c + cols - k % cols) % cols

    def edge_device(up, side):
        other = (stripe + stripes + up) % stripes
        return (other // rows, other % rows, (c + cols + side) % cols)

    edges = ((-1, 0), (1, 0), (-1, -1), (0, -1), (1, -1), (-1, 1), (0, 1), (1, 1))
    barrier = pltpu.get_barrier_semaphore()

    def greet(j, carry):
        pl.semaphore_signal(barrier, inc=1, device_id=(z, *target(j)), device_id_type=MESH)
        return carry

    lax.fori_loop(1, tiles, greet, 0)
    for other in (after, before):
        pl.semaphore_signal(barrier, inc=1, device_id=(other, r, c), device_id_type=MESH)
    for up, side in edges:
        pl.semaphore_signal(barrier, inc=1, device_id=edge_device(up, side), device_id_type=MESH)

    group = min(4, blocks)
    proj = jnp.concatenate([wp_ref[...], swapped(wp_ref[...]).astype(BF)], axis=1)
    proj_bias = jnp.concatenate([bp_ref[...], jnp.concatenate([bp_ref[:, HALF:], bp_ref[:, :HALF]], axis=1)], axis=1)

    def embed(i, carry):
        at = pl.ds(i * group, group)
        x = feat_ref[at].reshape(group * BLK, C)
        v = jnp.dot(x, we_ref[...], preferred_element_type=F32) + be_ref[...]
        hidden = (v / (1.0 + jnp.exp(-v))).astype(BF)
        both = (jnp.dot(hidden, proj, preferred_element_type=F32) + proj_bias).astype(BF)
        features[at] = both[:, :C].reshape(group, BLK, C)
        swapped_features[at] = both[:, C:].reshape(group, BLK, C)
        return carry

    lax.fori_loop(0, blocks // group, embed, 0)
    row_id = lax.broadcasted_iota(jnp.int32, (8, BLK), 0)
    for b in range(blocks):
        lanes = slice(b * BLK, (b + 1) * BLK)
        off = off_ref[:, lanes].astype(F32)
        cell = cells_ref[0:1, lanes]
        meta = jnp.where(row_id == 0, off[0:1], 0.0)
        meta = jnp.where(row_id == 1, off[1:2], meta)
        meta = jnp.where(row_id == 2, (cell >> 5).astype(F32), meta)
        block_meta[b] = jnp.where(row_id == 3, (cell & 31).astype(F32), meta)

    low_lanes = lax.broadcasted_iota(jnp.int32, (BLK, C), 1) < HALF

    def pack(t, dst0, dst1, j):
        at = [block_at[t * MOST + i] for i in range(MOST)]
        dst0[j, :BLK, :] = jnp.where(low_lanes, features[at[0]], swapped_features[at[1]])
        dst1[j] = jnp.where(low_lanes, swapped_features[at[0]], features[at[1]])
        metas = []
        for i in range(MOST):
            patch = jnp.full((8, BLK), patch_at[t * MOST + i].astype(F32))
            meta = jnp.where((row_id == 2) & (patch < 0.0), -100.0, block_meta[at[i]])
            metas.append(jnp.where(row_id == 4, patch, meta))
        dst0[j, BLK:, :] = jnp.concatenate(metas, axis=0).astype(BF)

    sends, gots = (send0, send1), (got0, got1)

    def out_copy(q, j):
        return pltpu.make_async_remote_copy(
            src_ref=sends[q].at[j], dst_ref=gots[q].at[j], send_sem=out_send.at[q, j], recv_sem=out_recv.at[q, j],
            device_id=(z, *target(j)), device_id_type=MESH,
        )

    pl.semaphore_wait(barrier, tiles - 1 + 2 + len(edges))

    def start_first(j, carry):
        tr, tc = target(j)
        pack(tr * cols + tc, send0, send1, j)
        out_copy(0, j).start()
        return carry

    def start_second(j, carry):
        out_copy(1, j).start()
        return carry

    lax.fori_loop(1, tiles, start_first, 0)
    lax.fori_loop(1, tiles, start_second, 0)
    pack(r * cols + c, got0, got1, 0)

    ones = jnp.ones((8, BLK), BF)
    zero_block = jnp.zeros((BLK, C), BF)
    sums0[0] = jnp.zeros((FOLD, C), F32)
    sums1[0] = jnp.zeros((FOLD, C), F32)
    density_sums[0] = jnp.zeros((8, CELLS), F32)

    def folded(matrix, stream, i):
        other = swapped(stream).astype(BF)
        low, high = (stream, other) if i == 0 else (other, stream)
        right = jnp.concatenate([jnp.where(low_lanes, low, zero_block), jnp.where(low_lanes, zero_block, high)], axis=0)
        left = jnp.concatenate([matrix[:FOLD], matrix[FOLD:]], axis=1)
        return jnp.dot(left, right, preferred_element_type=F32)

    def receive0(j):
        metas = got0[j, BLK:, :].astype(F32)
        stream = got0[j, :BLK, :]
        for i in range(MOST):
            meta = metas[8 * i : 8 * i + 8]
            matrix = window_weights(meta)
            matrices[j * MOST + i] = matrix
            patch_rows[j * MOST + i] = jnp.broadcast_to(meta[4:5], (8, BLK))
            sums0[1 + j * MOST + i] = folded(matrix, stream, i)
            density_sums[1 + j * MOST + i] = lax.dot_general(ones, matrix, (((1,), (1,)), ((), ())), preferred_element_type=F32)

    def step0(p, carry):
        for j in (2 * p, 2 * p + 1):
            out_copy(0, j).wait_recv()
        for j in (2 * p, 2 * p + 1):
            receive0(j)
        return carry

    receive0(0)
    out_copy(0, 1).wait_recv()
    receive0(1)
    lax.fori_loop(1, tiles // 2, step0, 0)

    by_row = jnp.concatenate([patch_rows[s, 0:1, :] for s in range(slots)], axis=0)
    slot_row = lax.broadcasted_iota(jnp.int32, (slots, C), 0)
    lane = lax.broadcasted_iota(jnp.int32, (slots, C), 1)
    by_lane = jnp.sum(jnp.where(slot_row == lane, by_row, 0.0), axis=0, keepdims=True)
    earlier = jnp.max(jnp.where((by_row == by_lane) & (slot_row < lane), slot_row + 1, 0), axis=0, keepdims=True)
    latest = jnp.max(jnp.where(by_row == lane.astype(F32), slot_row + 1, 0), axis=0, keepdims=True)
    link_id = lax.broadcasted_iota(jnp.int32, (8, C), 0)
    ids = jnp.clip(by_lane.astype(jnp.int32), 0, ORBITS * PATCHES - 1)
    links[...] = jnp.where(link_id == 0, earlier, jnp.where(link_id == 1, latest, ids))
    link_copy = pltpu.make_async_copy(links, links_smem, link_sem)
    link_copy.start()
    link_copy.wait()

    def chain(s, carry):
        e = links_smem[0, s]
        sums0[s + 1] = sums0[s + 1] + sums0[e]
        density_sums[s + 1] = density_sums[s + 1] + density_sums[e]
        return carry

    lax.fori_loop(0, slots, chain, 0)

    for p in range(ORBITS * PATCHES):
        at = links_smem[1, p]
        owner, local_patch = p // PATCHES, p % PATCHES
        part0[owner, local_patch * FOLD : (local_patch + 1) * FOLD, :] = sums0[at].astype(BF)
        row = density_sums[at]
        density_rows[owner, local_patch : local_patch + 1, :] = row[0:1, :C]
        density_rows[owner, PATCHES + local_patch : PATCHES + local_patch + 1, :] = row[0:1, C:]
    for owner in range(ORBITS):
        density_part[owner] = density_rows[owner].astype(BF)
        part0[owner, PATCHES * FOLD :, :] = density_part[owner]

    cut = PATCHES * FOLD // 2
    parts = (part0, part1)

    def ring_copy(q, src, dst, way, step, other):
        return pltpu.make_async_remote_copy(
            src_ref=src, dst_ref=dst, send_sem=ring_send.at[q, way, step], recv_sem=ring_recv.at[q, way, step],
            device_id=(other, r, c), device_id_type=MESH,
        )

    def sides(q):
        low, high = pl.ds(0, cut), pl.ds(cut, cut + (DENS if q == 0 else 0))
        return ((0, after, low, high), (1, before, high, low))

    rings = {}

    def ring_start(q):
        rings[q] = []
        for way, other, passed, direct in sides(q):
            relay = ring_copy(q, parts[q].at[across, passed], relay_in.at[q, passed], way, 0, other)
            straight = ring_copy(q, parts[q].at[other, direct], part_in.at[q, way, direct], way, 1, other)
            summed = ring_copy(q, relay_out.at[q, passed], part_in.at[q, way, passed], way, 2, other)
            relay.start()
            straight.start()
            rings[q].append((relay, straight, summed))

    def ring_relay(q):
        for way, other, passed, direct in sides(q):
            relay, straight, summed = rings[q][way]
            relay.wait_recv()
            total = parts[q][other, passed].astype(F32) + relay_in[q, passed].astype(F32)
            relay_out[q, passed] = total.astype(BF)
            summed.start()

    def ring_finish(q):
        for relay, straight, summed in rings[q]:
            straight.wait_recv()
        for relay, straight, summed in rings[q]:
            summed.wait_recv()

    ring_start(0)

    def receive1(j):
        stream = got1[j]
        for i in range(MOST):
            s = j * MOST + i
            sums1[s + 1] = folded(matrices[s], stream, i) + sums1[links_smem[0, s]]

    def step1(p, carry):
        for j in (2 * p, 2 * p + 1):
            out_copy(1, j).wait_recv()
        for j in (2 * p, 2 * p + 1):
            receive1(j)
        return carry

    receive1(0)
    out_copy(1, 1).wait_recv()
    receive1(1)
    middle = max(1, tiles // 4)
    lax.fori_loop(1, middle, step1, 0)
    ring_relay(0)
    lax.fori_loop(middle, tiles // 2, step1, 0)
    for p in range(ORBITS * PATCHES):
        owner, local_patch = p // PATCHES, p % PATCHES
        part1[owner, local_patch * FOLD : (local_patch + 1) * FOLD, :] = sums1[links_smem[1, p]].astype(BF)
    ring_start(1)
    ring_finish(0)

    tail = pl.ds(PATCHES * FOLD, DENS)
    dens_in = jnp.concatenate([part0[z, tail], part_in[0, 0, tail], part_in[0, 1, tail]], axis=0)
    pick_shape = (3 * DENS, DENS * C)
    picked = lax.broadcasted_iota(jnp.int32, pick_shape, 0) % DENS == lax.broadcasted_iota(jnp.int32, pick_shape, 1) // C
    density_all = lax.dot_general(dens_in, picked.astype(BF), (((0,), (0,)), ((), ())), preferred_element_type=F32)
    weight_swapped = jnp.concatenate([dw_ref[:, HALF:], dw_ref[:, :HALF]], axis=1)
    low_row = lax.broadcasted_iota(jnp.int32, (1, C), 1) < HALF
    weights = (jnp.where(low_row, dw_ref[...], weight_swapped), jnp.where(low_row, weight_swapped, dw_ref[...]))

    def grid_value(q, p):
        cells = pl.ds(p * FOLD, FOLD)
        density = jnp.where(
            low_lanes, density_all[:, p * C : (p + 1) * C], density_all[:, (PATCHES + p) * C : (PATCHES + p + 1) * C]
        )
        total = parts[q][z, cells].astype(F32) + part_in[q, 0, cells].astype(F32) + part_in[q, 1, cells].astype(F32)
        return total / jnp.maximum(density, 1.0) + weights[q] * (density / (1.0 + density))

    for p in range(PATCHES):
        packed[p] = grid_value(0, p)
    ring_relay(1)
    ring_finish(1)
    for p in range(PATCHES):
        x0, x1 = packed[p], grid_value(1, p)
        top, left = p // WIDE * PH, p % WIDE * PW
        lower = jnp.where(low_lanes, x0, swapped(x1)).astype(BF)
        upper = jnp.where(low_lanes, swapped(x0), x1).astype(BF)
        tile[top : top + PH // 2, left : left + PW, :] = lower.reshape(PH // 2, PW, C)
        tile[top + PH // 2 : top + PH, left : left + PW, :] = upper.reshape(PH // 2, PW, C)

    def exchange(origin, turn):
        for i in range(SR):
            col_out[turn, 0, i : i + 1, :] = origin[i, 0:1, :]
            col_out[turn, 1, i : i + 1, :] = origin[i, TC - 1 : TC, :]
        copies = []
        for e, (up, side) in enumerate(edges):
            if side == 0:
                src, dst = origin.at[0 if up < 0 else SR - 1], row_in.at[turn, e]
            else:
                src, dst = col_out.at[turn, 0 if side < 0 else 1], col_in.at[turn, e - 2]
            copies.append(pltpu.make_async_remote_copy(
                src_ref=src, dst_ref=dst, send_sem=edge_send.at[turn, e], recv_sem=edge_recv.at[turn, e],
                device_id=edge_device(up, side), device_id_type=MESH,
            ))
        for copy in copies:
            copy.start()

        def shifts(row, centre):
            centre = centre.astype(F32)
            wide[row, :, 0:C] = pltpu.roll(centre, 1, 0).astype(BF)
            wide[row, :, C : 2 * C] = centre.astype(BF)
            wide[row, :, 2 * C :] = pltpu.roll(centre, TC - 1, 0).astype(BF)

        for i in range(SR):
            shifts(i + 1, origin[i])
        for copy in copies:
            copy.wait_recv()
        shifts(0, jnp.where(stripe > 0, row_in[turn, 1].astype(F32), 0.0))
        shifts(SR + 1, jnp.where(stripe < stripes - 1, row_in[turn, 0].astype(F32), 0.0))
        for first_edge, lanes, at, open_ in ((3, slice(0, C), 0, c > 0), (0, slice(2 * C, 3 * C), TC - 1, c < cols - 1)):
            above = col_in[turn, first_edge + 2, SR - 1 : SR, :].astype(F32)
            level = col_in[turn, first_edge + 1].astype(F32)
            below = col_in[turn, first_edge, 0:1, :].astype(F32)
            above = jnp.where(open_ & (stripe > 0), above, 0.0)
            level = jnp.where(open_, level, 0.0)
            below = jnp.where(open_ & (stripe < stripes - 1), below, 0.0)
            wide[0, at : at + 1, lanes] = above.astype(BF)
            wide[SR + 1, at : at + 1, lanes] = below.astype(BF)
            for i in range(SR):
                wide[i + 1, at : at + 1, lanes] = level[i : i + 1].astype(BF)
        return copies

    block_rows = PH // 2

    def convolved(i, w_ref, b_ref):
        total = None
        for a in range(3):
            x = wide[pl.ds(i + a, block_rows)].reshape(block_rows * TC, 3 * C)
            term = jnp.dot(x, w_ref[a], preferred_element_type=F32)
            total = term if total is None else total + term
        return total + b_ref[...]

    edge_copies = exchange(tile, 0)
    for i in range(0, SR, block_rows):
        v = convolved(i, w1_ref, b1_ref)
        first[i : i + block_rows] = (v / (1.0 + jnp.exp(-v))).astype(BF).reshape(block_rows, TC, C)
    edge_copies += exchange(first, 1)

    count = PATCHES // 2
    values = (values0, values1)

    def half_of(q, owner, h):
        return values[q].at[pl.ds(owner * PATCHES + h * count, count)]

    def gather_copy(q, owner, h, way, step, src):
        return pltpu.make_async_remote_copy(
            src_ref=src, dst_ref=half_of(q, owner, h), send_sem=gather_send.at[q, way, step],
            recv_sem=gather_recv.at[q, way, step], device_id=((after, before)[way], r, c), device_id_type=MESH,
        )

    gathers = []

    def gather_start(q, h):
        for way in range(2):
            copy = gather_copy(q, z, h, way, h, mine.at[q, pl.ds(h * count, count)])
            copy.start()
            gathers.append(copy)

    near = (before, after)

    def gather_relay(q):
        for way in range(2):
            gather_copy(q, near[way], way, way, way, half_of(q, near[way], way)).wait_recv()
            copy = gather_copy(q, near[way], way, way, 2, half_of(q, near[way], way))
            copy.start()
            gathers.append(copy)

    def gather_finish(q):
        for way in range(2):
            gather_copy(q, near[way], 1 - way, way, 1 - way, half_of(q, near[way], 1 - way)).wait_recv()
        for way in range(2):
            gather_copy(q, across, way, way, 2, half_of(q, across, way)).wait_recv()

    for h in range(2):
        halves = []
        for i in range(h * PH, (h + 1) * PH, block_rows):
            v = convolved(i, w2_ref, b2_ref).reshape(block_rows, TC, C)
            v = (tile[i : i + block_rows].astype(F32) + v).astype(BF)
            grid_ref[i : i + block_rows] = v
            halves.append(v)
        for w in range(WIDE):
            lower = halves[0][:, w * PW : (w + 1) * PW, :].reshape(FOLD, C)
            upper = halves[1][:, w * PW : (w + 1) * PW, :].reshape(FOLD, C)
            mine[0, h * count + w] = jnp.where(low_lanes, lower, swapped(upper).astype(BF))
            mine[1, h * count + w] = jnp.where(low_lanes, swapped(lower).astype(BF), upper)
        gather_start(0, h)
    for q in range(2):
        values[q][pl.ds(z * PATCHES, PATCHES)] = mine[q]
    gather_relay(0)
    gather_start(1, 0)
    gather_start(1, 1)
    gather_finish(0)

    def swap_values(q):
        def one(p, carry):
            values_swapped[q, p] = swapped(values[q][p]).astype(BF)
            return carry

        lax.fori_loop(0, ORBITS * PATCHES, one, 0)

    one_block = jnp.ones((BLK, C), BF)
    one_low, one_high = jnp.where(low_lanes, one_block, zero_block), jnp.where(low_lanes, zero_block, one_block)

    def read(q, j, target_ref):
        patches = [links_smem[2, j * MOST + i] for i in range(MOST)]
        a, b = patches
        low0 = jnp.where(low_lanes, values[q][a], zero_block)
        low1 = jnp.where(low_lanes, values_swapped[q, a], zero_block)
        high0 = jnp.where(low_lanes, zero_block, values_swapped[q, b])
        high1 = jnp.where(low_lanes, zero_block, values[q][b])
        right = jnp.concatenate([
            jnp.concatenate([low0, one_low], axis=1), jnp.concatenate([low1, one_low], axis=1),
            jnp.concatenate([high0, one_high], axis=1), jnp.concatenate([high1, one_high], axis=1),
        ], axis=0)
        left = jnp.concatenate([matrices[j * MOST], matrices[j * MOST + 1]], axis=0)
        summed = lax.dot_general(left, right, (((0,), (0,)), ((), ())), preferred_element_type=F32)
        total = jnp.where(summed[:, C:] > 0.0, summed[:, C:], 1.0)
        target_ref[q, j] = (summed[:, :C] / total).astype(BF)

    def back_copy(q, j):
        return pltpu.make_async_remote_copy(
            src_ref=back_out.at[q, j], dst_ref=back_in.at[q, j], send_sem=back_send.at[q, j], recv_sem=back_recv.at[q, j],
            device_id=(z, *source(j)), device_id_type=MESH,
        )

    def read_and_send(q):
        def step(j, carry):
            read(q, j, back_out)
            back_copy(q, j).start()
            return carry

        return step

    swap_values(0)
    lax.fori_loop(1, tiles // 2, read_and_send(0), 0)
    gather_relay(1)
    lax.fori_loop(tiles // 2, tiles, read_and_send(0), 0)
    read(0, 0, back_in)
    gather_finish(1)
    swap_values(1)
    lax.fori_loop(1, tiles, read_and_send(1), 0)
    read(1, 0, back_in)

    def arrive(q):
        def step(j, carry):
            back_copy(q, j).wait_recv()
            return carry

        return step

    lax.fori_loop(1, tiles, arrive(0), 0)
    lax.fori_loop(1, tiles, arrive(1), 0)

    def combine(b, carry):
        t = tile_of[b]
        k = (t // cols + rows - r) % rows * cols + (t % cols + cols - c) % cols
        j = jnp.where(k == 0, 0, (k - 1 + tiles - 1 - tiles // 2) % (tiles - 1) + 1)
        is_low = jnp.full((BLK, C), rank_of[b]) == 0
        x0, x1 = back_in[0, j].astype(F32), back_in[1, j].astype(F32)
        lower = jnp.where(is_low, x0, swapped(x0))
        upper = jnp.where(is_low, swapped(x1), x1)
        reading = jnp.where(low_lanes, lower, upper)
        out_ref[b] = (features[b].astype(F32) + reading).astype(BF)
        return carry

    lax.fori_loop(0, blocks, combine, 0)

    def sent(j, carry):
        for q in range(2):
            out_copy(q, j).wait_send()
            back_copy(q, j).wait_send()
        return carry

    lax.fori_loop(1, tiles, sent, 0)
    for q in range(2):
        for copies in rings[q]:
            for copy in copies:
                copy.wait_send()
    for copy in gathers + edge_copies:
        copy.wait_send()


def local(
    obs_feat, obs_offset, obs_cells, block_tile, block_patch, w_embed, b_embed, w_proj, b_proj, density_weight,
    w_first, b_first, w_second, b_second,
):
    blocks = block_tile.shape[0]
    rows, cols = lax.axis_size("rows"), lax.axis_size("cols")
    tiles = rows * cols
    slots = tiles * MOST
    patches = ORBITS * PATCHES

    vm = pl.BlockSpec(memory_space=VMEM)
    sm = pl.BlockSpec(memory_space=SMEM)
    block_at, patch_at, rank_of = pl.pallas_call(
        functools.partial(table_kernel, blocks, slots),
        out_shape=tuple(jax.ShapeDtypeStruct((n,), jnp.int32) for n in (slots, slots, blocks)),
        in_specs=[sm, sm],
        out_specs=(sm, sm, sm),
        scratch_shapes=[SMEM((tiles,), jnp.int32)],
        name="tables",
    )(block_tile, block_patch)

    part_rows = PATCHES * FOLD + DENS
    dma = pltpu.SemaphoreType.DMA
    obs_out, grid_out = pl.pallas_call(
        functools.partial(main_kernel, rows, cols, blocks),
        grid=(1,),
        out_shape=(jax.ShapeDtypeStruct((blocks, BLK, C), BF), jax.ShapeDtypeStruct((SR, TC, C), BF)),
        in_specs=[sm] * 4 + [vm, vm, pl.BlockSpec((8, blocks * BLK), lambda i: (0, 0))] + [vm] * 9,
        out_specs=(vm, vm),
        scratch_shapes=[
            VMEM((blocks, BLK, C), BF),
            VMEM((blocks, BLK, C), BF),
            VMEM((blocks, 8, BLK), F32),
            VMEM((tiles, BLK + META, C), BF),
            VMEM((tiles, BLK, C), BF),
            VMEM((tiles, BLK + META, C), BF),
            VMEM((tiles, BLK, C), BF),
            VMEM((slots, CELLS, BLK), BF),
            VMEM((slots, 8, BLK), F32),
            VMEM((slots + 1, FOLD, C), F32),
            VMEM((slots + 1, FOLD, C), F32),
            VMEM((slots + 1, 8, CELLS), F32),
            VMEM((8, C), jnp.int32),
            SMEM((8, C), jnp.int32),
            VMEM((ORBITS, DENS, C), F32),
            VMEM((ORBITS, part_rows, C), BF),
            VMEM((ORBITS, part_rows, C), BF),
            VMEM((ORBITS, DENS, C), BF),
            VMEM((2, part_rows, C), BF),
            VMEM((2, part_rows, C), BF),
            VMEM((2, 2, part_rows, C), BF),
            VMEM((PATCHES, FOLD, C), F32),
            VMEM((SR, TC, C), BF),
            VMEM((SR + 2, TC, 3 * C), BF),
            VMEM((SR, TC, C), BF),
            VMEM((2, 2, SR, C), BF),
            VMEM((2, 2, TC, C), BF),
            VMEM((2, 6, SR, C), BF),
            VMEM((2, PATCHES, FOLD, C), BF),
            VMEM((patches, FOLD, C), BF),
            VMEM((patches, FOLD, C), BF),
            VMEM((2, patches, FOLD, C), BF),
            VMEM((2, tiles, BLK, C), BF),
            VMEM((2, tiles, BLK, C), BF),
            dma((2, tiles)),
            dma((2, tiles)),
            dma((2, 2, 3)),
            dma((2, 2, 3)),
            dma((2, 8)),
            dma((2, 8)),
            dma((2, 2, 3)),
            dma((2, 2, 3)),
            dma((2, tiles)),
            dma((2, tiles)),
            dma,
        ],
        compiler_params=pltpu.CompilerParams(collective_id=0, has_side_effects=True, vmem_limit_bytes=63000000),
        name="encode",
    )(
        block_at, patch_at, block_tile, rank_of,
        obs_feat.reshape(blocks, BLK, C), obs_offset, obs_cells, w_embed, b_embed[None, :], w_proj, b_proj[None, :],
        density_weight[None, :], w_first.reshape(3, 3 * C, C), b_first[None, :], w_second.reshape(3, 3 * C, C), b_second[None, :],
    )
    return (obs_out.reshape(obs_feat.shape), grid_out)


def solution(mesh):
    by_device = P(("orbits", "rows", "cols"))
    in_specs = (
        P(("orbits", "rows", "cols"), None), P(None, ("orbits", "rows", "cols")), P(None, ("orbits", "rows", "cols")),
        by_device, by_device, P(), P(), P(), P(), P(), P(), P(), P(), P(),
    )
    out_specs = (P(("orbits", "rows", "cols"), None), P(("orbits", "rows"), "cols", None))
    return jax.shard_map(local, mesh=mesh, in_specs=in_specs, out_specs=out_specs, check_vma=False)
```

```python
import functools

import jax
import jax.numpy as jnp
from jax import lax
from jax.experimental import pallas as pl
from jax.experimental.pallas import tpu as pltpu
from jax.sharding import PartitionSpec as P

PH = 8
PW = 32
SR = 16
TC = 128
BLK = 128
C = 128
HALF = C // 2
MOST = 2
CELLS = PH * PW
FOLD = CELLS // 2
WIDE = TC // PW
PATCHES = SR // PH * WIDE
DENS = 2 * PATCHES
META = 8
DEAD = -128.0
ORBITS = 4
MESH = pl.DeviceIdType.MESH
VMEM = pltpu.VMEM
SMEM = pltpu.SMEM
BF = jnp.bfloat16
F32 = jnp.float32


def window_weights(meta_rows):
    off_r, off_c, anchor = meta_rows[0:1], meta_rows[1:2], meta_rows[2:3]
    anchor_r = jnp.floor(anchor * (1.0 / PW))
    anchor_c = anchor - anchor_r * PW
    tap_r = lax.broadcasted_iota(jnp.int32, (PH, BLK), 0).astype(F32) - anchor_r
    tap_c = lax.broadcasted_iota(jnp.int32, (PW, BLK), 0).astype(F32) - anchor_c
    delta_r = tap_r - 1.5 - off_r
    delta_c = tap_c - 1.5 - off_c
    weight_r = jnp.where((tap_r >= 0.0) & (tap_r < 4.0), jnp.exp(delta_r * delta_r * -0.5), 0.0)
    weight_c = jnp.where((tap_c >= 0.0) & (tap_c < 4.0), jnp.exp(delta_c * delta_c * -0.5), 0.0)
    return jnp.concatenate([(weight_r[r : r + 1] * weight_c).astype(BF) for r in range(PH)], axis=0)


def swapped(x):
    return pltpu.roll(x.astype(F32), HALF, 1)


def main_kernel(
    rows, cols, blocks,
    tile_of, tile_row, patch_row, feat_hbm, off_hbm, cells_hbm, w1_hbm, w2_hbm,
    we_ref, be_ref, wp_ref, bp_ref, dw_ref, b1_ref, b2_ref,
    out_ref, grid_ref,
    feat_ref, off_ref, cells_ref, w1_ref, w2_ref, table, table_smem,
    features, swapped_features, block_meta, send0, send1, got0, got1, matrices, patch_rows,
    sums0, sums1, density_sums, links, links_smem, density_rows, part0, part1, density_part, relay_in, relay_out, part_in,
    packed, tile, wide, first, col_out, row_in, col_in, mine, values0, values1, values_swapped, back_out, back0, back1,
    out_send, out_recv, ring_send, ring_recv, edge_send, edge_recv, gather_send, gather_recv, back_send, back_recv, link_sem, load_sem,
):
    z, r, c = lax.axis_index("orbits"), lax.axis_index("rows"), lax.axis_index("cols")
    tiles = rows * cols
    slots = tiles * MOST
    stripes = ORBITS * rows
    stripe = z * rows + r
    after, before = (z + 1) % ORBITS, (z + ORBITS - 1) % ORBITS
    across = (z + 2) % ORBITS

    def offset_of(j):
        return (j - 1 + tiles // 2) % (tiles - 1) + 1

    def target(j):
        k = offset_of(j)
        return (r + k // cols) % rows, (c + k % cols) % cols

    def source(j):
        k = offset_of(j)
        return (r + rows - k // cols) % rows, (c + cols - k % cols) % cols

    def edge_device(up, side):
        other = (stripe + stripes + up) % stripes
        return (other // rows, other % rows, (c + cols + side) % cols)

    edges = ((-1, 0), (1, 0), (-1, -1), (0, -1), (1, -1), (-1, 1), (0, 1), (1, 1))
    barrier = pltpu.get_barrier_semaphore()

    def greet(j, carry):
        pl.semaphore_signal(barrier, inc=1, device_id=(z, *target(j)), device_id_type=MESH)
        return carry

    lax.fori_loop(1, tiles, greet, 0)
    for other in (after, before):
        pl.semaphore_signal(barrier, inc=1, device_id=(other, r, c), device_id_type=MESH)
    for up, side in edges:
        pl.semaphore_signal(barrier, inc=1, device_id=edge_device(up, side), device_id_type=MESH)

    half_blocks = blocks // 2
    loads = [
        pltpu.make_async_copy(feat_hbm.at[pl.ds(0, half_blocks)], feat_ref.at[pl.ds(0, half_blocks)], load_sem.at[0]),
        pltpu.make_async_copy(feat_hbm.at[pl.ds(half_blocks, half_blocks)], feat_ref.at[pl.ds(half_blocks, half_blocks)], load_sem.at[1]),
        pltpu.make_async_copy(off_hbm, off_ref, load_sem.at[2]),
        pltpu.make_async_copy(cells_hbm.at[pl.ds(0, 8)], cells_ref, load_sem.at[3]),
        pltpu.make_async_copy(w1_hbm, w1_ref, load_sem.at[4]),
        pltpu.make_async_copy(w2_hbm, w2_ref, load_sem.at[5]),
    ]
    for load in loads:
        load.start()

    square = (tiles, blocks)
    block_id = lax.broadcasted_iota(jnp.int32, square, 1).astype(F32)
    hit = tile_row[...] == lax.broadcasted_iota(jnp.int32, square, 0)
    lowest = jnp.min(jnp.where(hit, block_id, float(blocks)), axis=1, keepdims=True)
    highest = jnp.max(jnp.where(hit, block_id, -1.0), axis=1, keepdims=True)
    row_patches = patch_row[...].astype(F32)
    patch_low = jnp.max(jnp.where(block_id == lowest, row_patches, -1.0), axis=1, keepdims=True)
    patch_high = jnp.max(jnp.where((block_id == highest) & (highest > lowest), row_patches, -1.0), axis=1, keepdims=True)
    entry = lax.broadcasted_iota(jnp.int32, (tiles, C), 1)
    found = jnp.where(entry == 0, lowest, jnp.where(entry == 1, highest, jnp.where(entry == 2, patch_low, patch_high)))
    found = found.astype(jnp.int32)
    table[...] = jnp.where(entry < 2, jnp.clip(found, 0, blocks - 1), found)
    table_copy = pltpu.make_async_copy(table, table_smem, link_sem.at[1])
    table_copy.start()

    group = min(4, half_blocks)
    proj = jnp.concatenate([wp_ref[...], swapped(wp_ref[...]).astype(BF)], axis=1)
    proj_bias = jnp.concatenate([bp_ref[...], jnp.concatenate([bp_ref[:, HALF:], bp_ref[:, :HALF]], axis=1)], axis=1)

    def embed(i, carry):
        at = pl.ds(i * group, group)
        x = feat_ref[at].reshape(group * BLK, C)
        v = jnp.dot(x, we_ref[...], preferred_element_type=F32) + be_ref[...]
        hidden = (v / (1.0 + jnp.exp(-v))).astype(BF)
        both = (jnp.dot(hidden, proj, preferred_element_type=F32) + proj_bias).astype(BF)
        features[at] = both[:, :C].reshape(group, BLK, C)
        swapped_features[at] = both[:, C:].reshape(group, BLK, C)
        return carry

    loads[0].wait()
    lax.fori_loop(0, half_blocks // group, embed, 0)
    loads[1].wait()
    lax.fori_loop(half_blocks // group, blocks // group, embed, 0)
    loads[2].wait()
    loads[3].wait()
    row_id = lax.broadcasted_iota(jnp.int32, (8, BLK), 0)
    row_kind = row_id % 4
    for b in range(blocks):
        lanes = slice(b * BLK, (b + 1) * BLK)
        off = off_ref[:, lanes].astype(F32)
        meta = jnp.where(row_kind == 0, off[0:1], off[1:2])
        block_meta[b] = jnp.where(row_kind == 2, cells_ref[0:1, lanes].astype(F32), meta)
    table_copy.wait()

    low_lanes = lax.broadcasted_iota(jnp.int32, (BLK, C), 1) < HALF

    def pack(t, dst0, dst1, j):
        at = [table_smem[t, i] for i in range(MOST)]
        dst0[j, :BLK, :] = jnp.where(low_lanes, features[at[0]], swapped_features[at[1]])
        dst1[j] = jnp.where(low_lanes, swapped_features[at[0]], features[at[1]])
        patch = jnp.where(row_id < 4, table_smem[t, 2].astype(F32), table_smem[t, 3].astype(F32))
        meta = jnp.where(row_id < 4, block_meta[at[0]], block_meta[at[1]])
        meta = jnp.where((row_kind == 2) & (patch < 0.0), DEAD, meta)
        dst0[j, BLK:, :] = jnp.where(row_kind == 3, patch, meta).astype(BF)

    sends, gots = (send0, send1), (got0, got1)

    def out_copy(q, j):
        return pltpu.make_async_remote_copy(
            src_ref=sends[q].at[j], dst_ref=gots[q].at[j], send_sem=out_send.at[q, j], recv_sem=out_recv.at[q, j],
            device_id=(z, *target(j)), device_id_type=MESH,
        )

    pl.semaphore_wait(barrier, tiles - 1 + 2 + len(edges))

    def start_first(j, carry):
        tr, tc = target(j)
        pack(tr * cols + tc, send0, send1, j)
        out_copy(0, j).start()
        return carry

    def start_second(j, carry):
        out_copy(1, j).start()
        return carry

    lax.fori_loop(1, tiles, start_first, 0)
    lax.fori_loop(1, tiles, start_second, 0)
    pack(r * cols + c, got0, got1, 0)

    ones = jnp.ones((8, BLK), BF)
    zero_block = jnp.zeros((BLK, C), BF)
    sums0[0] = jnp.zeros((FOLD, C), F32)
    sums1[0] = jnp.zeros((FOLD, C), F32)
    density_sums[0] = jnp.zeros((8, CELLS), F32)

    def folded(matrix, stream, i):
        other = swapped(stream).astype(BF)
        low, high = (stream, other) if i == 0 else (other, stream)
        right = jnp.concatenate([jnp.where(low_lanes, low, zero_block), jnp.where(low_lanes, zero_block, high)], axis=0)
        left = jnp.concatenate([matrix[:FOLD], matrix[FOLD:]], axis=1)
        return jnp.dot(left, right, preferred_element_type=F32)

    def receive0(j):
        metas = got0[j, BLK:, :].astype(F32)
        stream = got0[j, :BLK, :]
        for i in range(MOST):
            meta = metas[4 * i : 4 * i + 4]
            matrix = window_weights(meta)
            matrices[j * MOST + i] = matrix
            patch_rows[j * MOST + i] = jnp.broadcast_to(meta[3:4], (8, BLK))
            sums0[1 + j * MOST + i] = folded(matrix, stream, i)
            density_sums[1 + j * MOST + i] = lax.dot_general(ones, matrix, (((1,), (1,)), ((), ())), preferred_element_type=F32)

    def step0(p, carry):
        for j in (2 * p, 2 * p + 1):
            out_copy(0, j).wait_recv()
        for j in (2 * p, 2 * p + 1):
            receive0(j)
        return carry

    receive0(0)
    out_copy(0, 1).wait_recv()
    receive0(1)
    lax.fori_loop(1, tiles // 2, step0, 0)

    by_row = jnp.concatenate([patch_rows[s, 0:1, :] for s in range(slots)], axis=0)
    slot_row = lax.broadcasted_iota(jnp.int32, (slots, C), 0)
    lane = lax.broadcasted_iota(jnp.int32, (slots, C), 1)
    by_lane = jnp.sum(jnp.where(slot_row == lane, by_row, 0.0), axis=0, keepdims=True)
    earlier = jnp.max(jnp.where((by_row == by_lane) & (slot_row < lane), slot_row + 1, 0), axis=0, keepdims=True)
    latest = jnp.max(jnp.where(by_row == lane.astype(F32), slot_row + 1, 0), axis=0, keepdims=True)
    link_id = lax.broadcasted_iota(jnp.int32, (8, C), 0)
    ids = jnp.clip(by_lane.astype(jnp.int32), 0, ORBITS * PATCHES - 1)
    links[...] = jnp.where(link_id == 0, earlier, jnp.where(link_id == 1, latest, ids))
    link_copy = pltpu.make_async_copy(links, links_smem, link_sem.at[0])
    link_copy.start()
    link_copy.wait()

    def chain(s, carry):
        e = links_smem[0, s]
        sums0[s + 1] = sums0[s + 1] + sums0[e]
        density_sums[s + 1] = density_sums[s + 1] + density_sums[e]
        return carry

    lax.fori_loop(0, slots, chain, 0)

    for p in range(ORBITS * PATCHES):
        at = links_smem[1, p]
        owner, local_patch = p // PATCHES, p % PATCHES
        part0[owner, local_patch * FOLD : (local_patch + 1) * FOLD, :] = sums0[at].astype(BF)
        row = density_sums[at]
        density_rows[owner, local_patch : local_patch + 1, :] = row[0:1, :C]
        density_rows[owner, PATCHES + local_patch : PATCHES + local_patch + 1, :] = row[0:1, C:]
    for owner in range(ORBITS):
        density_part[owner] = density_rows[owner].astype(BF)
        part0[owner, PATCHES * FOLD :, :] = density_part[owner]

    cut = PATCHES * FOLD // 2
    parts = (part0, part1)

    def ring_copy(q, src, dst, way, step, other):
        return pltpu.make_async_remote_copy(
            src_ref=src, dst_ref=dst, send_sem=ring_send.at[q, way, step], recv_sem=ring_recv.at[q, way, step],
            device_id=(other, r, c), device_id_type=MESH,
        )

    def sides(q):
        low, high = pl.ds(0, cut), pl.ds(cut, cut + (DENS if q == 0 else 0))
        return ((0, after, low, high), (1, before, high, low))

    rings = {}

    def ring_start(q):
        rings[q] = []
        for way, other, passed, direct in sides(q):
            relay = ring_copy(q, parts[q].at[across, passed], relay_in.at[q, passed], way, 0, other)
            straight = ring_copy(q, parts[q].at[other, direct], part_in.at[q, way, direct], way, 1, other)
            summed = ring_copy(q, relay_out.at[q, passed], part_in.at[q, way, passed], way, 2, other)
            relay.start()
            straight.start()
            rings[q].append((relay, straight, summed))

    def ring_relay(q):
        for way, other, passed, direct in sides(q):
            relay, straight, summed = rings[q][way]
            relay.wait_recv()
            total = parts[q][other, passed].astype(F32) + relay_in[q, passed].astype(F32)
            relay_out[q, passed] = total.astype(BF)
            summed.start()

    def ring_finish(q):
        for relay, straight, summed in rings[q]:
            straight.wait_recv()
        for relay, straight, summed in rings[q]:
            summed.wait_recv()

    ring_start(0)

    def receive1(j):
        stream = got1[j]
        for i in range(MOST):
            s = j * MOST + i
            sums1[s + 1] = folded(matrices[s], stream, i) + sums1[links_smem[0, s]]

    def step1(p, carry):
        for j in (2 * p, 2 * p + 1):
            out_copy(1, j).wait_recv()
        for j in (2 * p, 2 * p + 1):
            receive1(j)
        return carry

    receive1(0)
    out_copy(1, 1).wait_recv()
    receive1(1)
    middle = max(1, tiles // 4)
    lax.fori_loop(1, middle, step1, 0)
    ring_relay(0)
    lax.fori_loop(middle, tiles // 2, step1, 0)
    for p in range(ORBITS * PATCHES):
        owner, local_patch = p // PATCHES, p % PATCHES
        part1[owner, local_patch * FOLD : (local_patch + 1) * FOLD, :] = sums1[links_smem[1, p]].astype(BF)
    ring_start(1)
    ring_finish(0)

    tail = pl.ds(PATCHES * FOLD, DENS)
    dens_in = jnp.concatenate([part0[z, tail], part_in[0, 0, tail], part_in[0, 1, tail]], axis=0)
    pick_shape = (3 * DENS, DENS * C)
    picked = lax.broadcasted_iota(jnp.int32, pick_shape, 0) % DENS == lax.broadcasted_iota(jnp.int32, pick_shape, 1) // C
    density_all = lax.dot_general(dens_in, picked.astype(BF), (((0,), (0,)), ((), ())), preferred_element_type=F32)
    weight_swapped = jnp.concatenate([dw_ref[:, HALF:], dw_ref[:, :HALF]], axis=1)
    low_row = lax.broadcasted_iota(jnp.int32, (1, C), 1) < HALF
    weights = (jnp.where(low_row, dw_ref[...], weight_swapped), jnp.where(low_row, weight_swapped, dw_ref[...]))

    def grid_value(q, p):
        cells = pl.ds(p * FOLD, FOLD)
        density = jnp.where(
            low_lanes, density_all[:, p * C : (p + 1) * C], density_all[:, (PATCHES + p) * C : (PATCHES + p + 1) * C]
        )
        total = parts[q][z, cells].astype(F32) + part_in[q, 0, cells].astype(F32) + part_in[q, 1, cells].astype(F32)
        return total / jnp.maximum(density, 1.0) + weights[q] * (density / (1.0 + density))

    for p in range(PATCHES):
        packed[p] = grid_value(0, p)
    ring_relay(1)
    ring_finish(1)
    for p in range(PATCHES):
        x0, x1 = packed[p], grid_value(1, p)
        top, left = p // WIDE * PH, p % WIDE * PW
        lower = jnp.where(low_lanes, x0, swapped(x1)).astype(BF)
        upper = jnp.where(low_lanes, swapped(x0), x1).astype(BF)
        tile[top : top + PH // 2, left : left + PW, :] = lower.reshape(PH // 2, PW, C)
        tile[top + PH // 2 : top + PH, left : left + PW, :] = upper.reshape(PH // 2, PW, C)

    def exchange(origin, turn):
        for i in range(SR):
            col_out[turn, 0, i : i + 1, :] = origin[i, 0:1, :]
            col_out[turn, 1, i : i + 1, :] = origin[i, TC - 1 : TC, :]
        copies = []
        for e, (up, side) in enumerate(edges):
            if side == 0:
                src, dst = origin.at[0 if up < 0 else SR - 1], row_in.at[turn, e]
            else:
                src, dst = col_out.at[turn, 0 if side < 0 else 1], col_in.at[turn, e - 2]
            copies.append(pltpu.make_async_remote_copy(
                src_ref=src, dst_ref=dst, send_sem=edge_send.at[turn, e], recv_sem=edge_recv.at[turn, e],
                device_id=edge_device(up, side), device_id_type=MESH,
            ))
        for copy in copies:
            copy.start()

        def shifts(row, centre):
            centre = centre.astype(F32)
            wide[row, :, 0:C] = pltpu.roll(centre, 1, 0).astype(BF)
            wide[row, :, C : 2 * C] = centre.astype(BF)
            wide[row, :, 2 * C :] = pltpu.roll(centre, TC - 1, 0).astype(BF)

        for i in range(SR):
            shifts(i + 1, origin[i])
        for copy in copies:
            copy.wait_recv()
        shifts(0, jnp.where(stripe > 0, row_in[turn, 1].astype(F32), 0.0))
        shifts(SR + 1, jnp.where(stripe < stripes - 1, row_in[turn, 0].astype(F32), 0.0))
        for first_edge, lanes, at, open_ in ((3, slice(0, C), 0, c > 0), (0, slice(2 * C, 3 * C), TC - 1, c < cols - 1)):
            above = col_in[turn, first_edge + 2, SR - 1 : SR, :].astype(F32)
            level = col_in[turn, first_edge + 1].astype(F32)
            below = col_in[turn, first_edge, 0:1, :].astype(F32)
            above = jnp.where(open_ & (stripe > 0), above, 0.0)
            level = jnp.where(open_, level, 0.0)
            below = jnp.where(open_ & (stripe < stripes - 1), below, 0.0)
            wide[0, at : at + 1, lanes] = above.astype(BF)
            wide[SR + 1, at : at + 1, lanes] = below.astype(BF)
            for i in range(SR):
                wide[i + 1, at : at + 1, lanes] = level[i : i + 1].astype(BF)
        return copies

    block_rows = PH // 2

    def convolved(i, w_ref, b_ref):
        total = None
        for a in range(3):
            x = wide[pl.ds(i + a, block_rows)].reshape(block_rows * TC, 3 * C)
            term = jnp.dot(x, w_ref[a], preferred_element_type=F32)
            total = term if total is None else total + term
        return total + b_ref[...]

    edge_copies = exchange(tile, 0)
    loads[4].wait()
    loads[5].wait()
    for i in range(0, SR, block_rows):
        v = convolved(i, w1_ref, b1_ref)
        first[i : i + block_rows] = (v / (1.0 + jnp.exp(-v))).astype(BF).reshape(block_rows, TC, C)
    edge_copies += exchange(first, 1)

    count = PATCHES // 2
    values = (values0, values1)

    def half_of(q, owner, h):
        return values[q].at[pl.ds(owner * PATCHES + h * count, count)]

    def gather_copy(q, owner, h, way, step, src):
        return pltpu.make_async_remote_copy(
            src_ref=src, dst_ref=half_of(q, owner, h), send_sem=gather_send.at[q, way, step],
            recv_sem=gather_recv.at[q, way, step], device_id=((after, before)[way], r, c), device_id_type=MESH,
        )

    gathers = []

    def gather_start(q, h):
        for way in range(2):
            copy = gather_copy(q, z, h, way, h, mine.at[q, pl.ds(h * count, count)])
            copy.start()
            gathers.append(copy)

    near = (before, after)

    def gather_relay(q):
        for way in range(2):
            gather_copy(q, near[way], way, way, way, half_of(q, near[way], way)).wait_recv()
            copy = gather_copy(q, near[way], way, way, 2, half_of(q, near[way], way))
            copy.start()
            gathers.append(copy)

    def gather_finish(q):
        for way in range(2):
            gather_copy(q, near[way], 1 - way, way, 1 - way, half_of(q, near[way], 1 - way)).wait_recv()
        for way in range(2):
            gather_copy(q, across, way, way, 2, half_of(q, across, way)).wait_recv()

    for h in range(2):
        halves = []
        for i in range(h * PH, (h + 1) * PH, block_rows):
            v = convolved(i, w2_ref, b2_ref).reshape(block_rows, TC, C)
            v = (tile[i : i + block_rows].astype(F32) + v).astype(BF)
            grid_ref[i : i + block_rows] = v
            halves.append(v)
        for w in range(WIDE):
            lower = halves[0][:, w * PW : (w + 1) * PW, :].reshape(FOLD, C)
            upper = halves[1][:, w * PW : (w + 1) * PW, :].reshape(FOLD, C)
            mine[0, h * count + w] = jnp.where(low_lanes, lower, swapped(upper).astype(BF))
            mine[1, h * count + w] = jnp.where(low_lanes, swapped(lower).astype(BF), upper)
        gather_start(0, h)
    for q in range(2):
        values[q][pl.ds(z * PATCHES, PATCHES)] = mine[q]
    gather_relay(0)
    gather_start(1, 0)
    gather_start(1, 1)
    gather_finish(0)

    def swap_values(q):
        def one(p, carry):
            values_swapped[q, p] = swapped(values[q][p]).astype(BF)
            return carry

        lax.fori_loop(0, ORBITS * PATCHES, one, 0)

    one_block = jnp.ones((BLK, C), BF)
    one_low, one_high = jnp.where(low_lanes, one_block, zero_block), jnp.where(low_lanes, zero_block, one_block)

    def read(q, j, target_ref):
        patches = [links_smem[2, j * MOST + i] for i in range(MOST)]
        a, b = patches
        low0 = jnp.where(low_lanes, values[q][a], zero_block)
        low1 = jnp.where(low_lanes, values_swapped[q, a], zero_block)
        high0 = jnp.where(low_lanes, zero_block, values_swapped[q, b])
        high1 = jnp.where(low_lanes, zero_block, values[q][b])
        right = jnp.concatenate([
            jnp.concatenate([low0, one_low], axis=1), jnp.concatenate([low1, one_low], axis=1),
            jnp.concatenate([high0, one_high], axis=1), jnp.concatenate([high1, one_high], axis=1),
        ], axis=0)
        left = jnp.concatenate([matrices[j * MOST], matrices[j * MOST + 1]], axis=0)
        summed = lax.dot_general(left, right, (((0,), (0,)), ((), ())), preferred_element_type=F32)
        total = jnp.where(summed[:, C:] > 0.0, summed[:, C:], 1.0)
        target_ref[j] = (summed[:, :C] / total).astype(BF)

    back = (back0, back1)

    def back_copy(q, j):
        return pltpu.make_async_remote_copy(
            src_ref=back_out.at[q, j], dst_ref=back[q].at[j], send_sem=back_send.at[q, j], recv_sem=back_recv.at[q, j],
            device_id=(z, *source(j)), device_id_type=MESH,
        )

    def read_and_send(q):
        def step(j, carry):
            read(q, j, back_out.at[q])
            back_copy(q, j).start()
            return carry

        return step

    swap_values(0)
    lax.fori_loop(1, tiles // 2, read_and_send(0), 0)
    gather_relay(1)
    lax.fori_loop(tiles // 2, tiles, read_and_send(0), 0)
    read(0, 0, back0)
    gather_finish(1)
    swap_values(1)
    lax.fori_loop(1, tiles, read_and_send(1), 0)
    read(1, 0, back1)

    def arrive(q):
        def step(j, carry):
            back_copy(q, j).wait_recv()
            return carry

        return step

    together = min(4, blocks)

    def combine(q):
        def step(i, carry):
            for u in range(together):
                b = i * together + u
                t = tile_of[b]
                k = (t // cols + rows - r) % rows * cols + (t % cols + cols - c) % cols
                j = jnp.where(k == 0, 0, (k - 1 + tiles - 1 - tiles // 2) % (tiles - 1) + 1)
                in_place = jnp.full((BLK, C), (table_smem[t, 0] == b).astype(jnp.int32)) == 1 - q
                x = back[q][j].astype(F32)
                value = (features[b].astype(F32) + jnp.where(in_place, x, swapped(x))).astype(BF)
                out_ref[b] = value if q == 0 else jnp.where(low_lanes, out_ref[b], value)
            return carry

        return step

    for q in range(2):
        lax.fori_loop(1, tiles, arrive(q), 0)
        lax.fori_loop(0, blocks // together, combine(q), 0)

    def sent(j, carry):
        for q in range(2):
            out_copy(q, j).wait_send()
            back_copy(q, j).wait_send()
        return carry

    lax.fori_loop(1, tiles, sent, 0)
    for q in range(2):
        for copies in rings[q]:
            for copy in copies:
                copy.wait_send()
    for copy in gathers + edge_copies:
        copy.wait_send()


def local(
    obs_feat, obs_offset, obs_cells, block_tile, block_patch, w_embed, b_embed, w_proj, b_proj, density_weight,
    w_first, b_first, w_second, b_second,
):
    blocks = block_tile.shape[0]
    rows, cols = lax.axis_size("rows"), lax.axis_size("cols")
    tiles = rows * cols
    slots = tiles * MOST
    patches = ORBITS * PATCHES

    vm = pl.BlockSpec(memory_space=VMEM)
    sm = pl.BlockSpec(memory_space=SMEM)
    part_rows = PATCHES * FOLD + DENS
    dma = pltpu.SemaphoreType.DMA
    obs_out, grid_out = pl.pallas_call(
        functools.partial(main_kernel, rows, cols, blocks),
        grid=(1,),
        out_shape=(jax.ShapeDtypeStruct((blocks, BLK, C), BF), jax.ShapeDtypeStruct((SR, TC, C), BF)),
        in_specs=[sm, vm, vm] + [pl.BlockSpec(memory_space=pl.ANY)] * 5 + [vm] * 7,
        out_specs=(vm, vm),
        scratch_shapes=[
            VMEM((blocks, BLK, C), BF),
            VMEM((2, blocks * BLK), BF),
            VMEM((8, blocks * BLK), jnp.int32),
            VMEM((3, 3 * C, C), BF),
            VMEM((3, 3 * C, C), BF),
            VMEM((tiles, C), jnp.int32),
            SMEM((tiles, C), jnp.int32),
            VMEM((blocks, BLK, C), BF),
            VMEM((blocks, BLK, C), BF),
            VMEM((blocks, 8, BLK), F32),
            VMEM((tiles, BLK + META, C), BF),
            VMEM((tiles, BLK, C), BF),
            VMEM((tiles, BLK + META, C), BF),
            VMEM((tiles, BLK, C), BF),
            VMEM((slots, CELLS, BLK), BF),
            VMEM((slots, 8, BLK), F32),
            VMEM((slots + 1, FOLD, C), F32),
            VMEM((slots + 1, FOLD, C), F32),
            VMEM((slots + 1, 8, CELLS), F32),
            VMEM((8, C), jnp.int32),
            SMEM((8, C), jnp.int32),
            VMEM((ORBITS, DENS, C), F32),
            VMEM((ORBITS, part_rows, C), BF),
            VMEM((ORBITS, part_rows, C), BF),
            VMEM((ORBITS, DENS, C), BF),
            VMEM((2, part_rows, C), BF),
            VMEM((2, part_rows, C), BF),
            VMEM((2, 2, part_rows, C), BF),
            VMEM((PATCHES, FOLD, C), F32),
            VMEM((SR, TC, C), BF),
            VMEM((SR + 2, TC, 3 * C), BF),
            VMEM((SR, TC, C), BF),
            VMEM((2, 2, SR, C), BF),
            VMEM((2, 2, TC, C), BF),
            VMEM((2, 6, SR, C), BF),
            VMEM((2, PATCHES, FOLD, C), BF),
            VMEM((patches, FOLD, C), BF),
            VMEM((patches, FOLD, C), BF),
            VMEM((2, patches, FOLD, C), BF),
            VMEM((2, tiles, BLK, C), BF),
            VMEM((tiles, BLK, C), BF),
            VMEM((tiles, BLK, C), BF),
            dma((2, tiles)),
            dma((2, tiles)),
            dma((2, 2, 3)),
            dma((2, 2, 3)),
            dma((2, 8)),
            dma((2, 8)),
            dma((2, 2, 3)),
            dma((2, 2, 3)),
            dma((2, tiles)),
            dma((2, tiles)),
            dma((2,)),
            dma((6,)),
        ],
        compiler_params=pltpu.CompilerParams(collective_id=0, has_side_effects=True, vmem_limit_bytes=63000000),
        name="encode",
    )(
        block_tile, block_tile[None, :], block_patch[None, :], obs_feat.reshape(blocks, BLK, C), obs_offset, obs_cells,
        w_first.reshape(3, 3 * C, C), w_second.reshape(3, 3 * C, C), w_embed, b_embed[None, :], w_proj, b_proj[None, :],
        density_weight[None, :], b_first[None, :], b_second[None, :],
    )
    return (obs_out.reshape(obs_feat.shape), grid_out)


def solution(mesh):
    by_device = P(("orbits", "rows", "cols"))
    in_specs = (
        P(("orbits", "rows", "cols"), None), P(None, ("orbits", "rows", "cols")), P(None, ("orbits", "rows", "cols")),
        by_device, by_device, P(), P(), P(), P(), P(), P(), P(), P(), P(),
    )
    out_specs = (P(("orbits", "rows", "cols"), None), P(("orbits", "rows"), "cols", None))
    return jax.shard_map(local, mesh=mesh, in_specs=in_specs, out_specs=out_specs, check_vma=False)
```

```python
import functools

import jax
import jax.numpy as jnp
from jax import lax
from jax.experimental import pallas as pl
from jax.experimental.pallas import tpu as pltpu
from jax.sharding import PartitionSpec as P

PH = 8
PW = 32
SR = 16
TC = 128
BLK = 128
C = 128
HALF = C // 2
MOST = 2
CELLS = PH * PW
FOLD = CELLS // 2
WIDE = TC // PW
PATCHES = SR // PH * WIDE
DENS = 2 * PATCHES
META = 8
DEAD = -128.0
ORBITS = 4
MESH = pl.DeviceIdType.MESH
VMEM = pltpu.VMEM
SMEM = pltpu.SMEM
BF = jnp.bfloat16
F32 = jnp.float32


def window_weights(meta_rows):
    off_r, off_c, anchor = meta_rows[0:1], meta_rows[1:2], meta_rows[2:3]
    anchor_r = jnp.floor(anchor * (1.0 / PW))
    anchor_c = anchor - anchor_r * PW
    tap_r = lax.broadcasted_iota(jnp.int32, (PH, BLK), 0).astype(F32) - anchor_r
    tap_c = lax.broadcasted_iota(jnp.int32, (PW, BLK), 0).astype(F32) - anchor_c
    delta_r = tap_r - 1.5 - off_r
    delta_c = tap_c - 1.5 - off_c
    weight_r = jnp.where((tap_r >= 0.0) & (tap_r < 4.0), jnp.exp(delta_r * delta_r * -0.5), 0.0)
    weight_c = jnp.where((tap_c >= 0.0) & (tap_c < 4.0), jnp.exp(delta_c * delta_c * -0.5), 0.0)
    return jnp.concatenate([(weight_r[r : r + 1] * weight_c).astype(BF) for r in range(PH)], axis=0)


def swapped(x):
    return pltpu.roll(x.astype(F32), HALF, 1)


def main_kernel(
    rows, cols, blocks,
    tile_of, tile_row, patch_row, feat_hbm, off_hbm, cells_hbm, w1_hbm, w2_hbm,
    we_ref, be_ref, wp_ref, bp_ref, dw_ref, b1_ref, b2_ref,
    out_hbm, grid_hbm,
    out_ref, grid_ref, feat_ref, off_ref, cells_ref, w1_ref, w2_ref, table, table_smem,
    features, swapped_features, block_meta, send0, send1, got0, got1, matrices, patch_rows,
    turned, inverse, sums0, sums1, density_sums, links, links_smem, density_rows, part0, part1, density_part, relay_in, relay_out, part_in,
    packed, tile, wide, first, side_in, side_first, col_out, row_in, col_in, mine, values0, values1, values_swapped, back_out, back0, back1,
    out_send, out_recv, ring_send, ring_recv, edge_send, edge_recv, gather_send, gather_recv, back_send, back_recv, link_sem, load_sem, store_sem, grid_sem,
):
    z, r, c = lax.axis_index("orbits"), lax.axis_index("rows"), lax.axis_index("cols")
    tiles = rows * cols
    slots = tiles * MOST
    stripes = ORBITS * rows
    stripe = z * rows + r
    after, before = (z + 1) % ORBITS, (z + ORBITS - 1) % ORBITS
    across = (z + 2) % ORBITS

    def offset_of(j):
        return (j - 1 + tiles // 2) % (tiles - 1) + 1

    def target(j):
        k = offset_of(j)
        return (r + k // cols) % rows, (c + k % cols) % cols

    def source(j):
        k = offset_of(j)
        return (r + rows - k // cols) % rows, (c + cols - k % cols) % cols

    def edge_device(up, side):
        other = (stripe + stripes + up) % stripes
        return (other // rows, other % rows, (c + cols + side) % cols)

    edges = ((-1, 0), (1, 0), (-1, -1), (0, -1), (1, -1), (-1, 1), (0, 1), (1, 1))
    barrier = pltpu.get_barrier_semaphore()

    def greet(j, carry):
        pl.semaphore_signal(barrier, inc=1, device_id=(z, *target(j)), device_id_type=MESH)
        return carry

    lax.fori_loop(1, tiles, greet, 0)
    for other in (after, before):
        pl.semaphore_signal(barrier, inc=1, device_id=(other, r, c), device_id_type=MESH)
    for up, side in edges:
        pl.semaphore_signal(barrier, inc=1, device_id=edge_device(up, side), device_id_type=MESH)

    half_blocks = blocks // 2
    loads = [
        pltpu.make_async_copy(feat_hbm.at[pl.ds(0, half_blocks)], feat_ref.at[pl.ds(0, half_blocks)], load_sem.at[0]),
        pltpu.make_async_copy(feat_hbm.at[pl.ds(half_blocks, half_blocks)], feat_ref.at[pl.ds(half_blocks, half_blocks)], load_sem.at[1]),
        pltpu.make_async_copy(off_hbm, off_ref, load_sem.at[2]),
        pltpu.make_async_copy(cells_hbm.at[pl.ds(0, 8)], cells_ref, load_sem.at[3]),
        pltpu.make_async_copy(w1_hbm, w1_ref, load_sem.at[4]),
        pltpu.make_async_copy(w2_hbm, w2_ref, load_sem.at[5]),
    ]
    for load in loads:
        load.start()

    square = (tiles, blocks)
    block_id = lax.broadcasted_iota(jnp.int32, square, 1).astype(F32)
    hit = tile_row[...] == lax.broadcasted_iota(jnp.int32, square, 0)
    lowest = jnp.min(jnp.where(hit, block_id, float(blocks)), axis=1, keepdims=True)
    highest = jnp.max(jnp.where(hit, block_id, -1.0), axis=1, keepdims=True)
    row_patches = patch_row[...].astype(F32)
    patch_low = jnp.max(jnp.where(block_id == lowest, row_patches, -1.0), axis=1, keepdims=True)
    patch_high = jnp.max(jnp.where((block_id == highest) & (highest > lowest), row_patches, -1.0), axis=1, keepdims=True)
    entry = lax.broadcasted_iota(jnp.int32, (tiles, C), 1)
    found = jnp.where(entry == 0, lowest, jnp.where(entry == 1, highest, jnp.where(entry == 2, patch_low, patch_high)))
    found = found.astype(jnp.int32)
    table[...] = jnp.where(entry < 2, jnp.clip(found, 0, blocks - 1), found)
    table_copy = pltpu.make_async_copy(table, table_smem, link_sem.at[1])
    table_copy.start()

    group = min(4, half_blocks)
    proj = jnp.concatenate([wp_ref[...], swapped(wp_ref[...]).astype(BF)], axis=1)
    proj_bias = jnp.concatenate([bp_ref[...], jnp.concatenate([bp_ref[:, HALF:], bp_ref[:, :HALF]], axis=1)], axis=1)

    def embed(i, carry):
        at = pl.ds(i * group, group)
        x = feat_ref[at].reshape(group * BLK, C)
        v = jnp.dot(x, we_ref[...], preferred_element_type=F32) + be_ref[...]
        hidden = (v / (1.0 + jnp.exp(-v))).astype(BF)
        both = (jnp.dot(hidden, proj, preferred_element_type=F32) + proj_bias).astype(BF)
        features[at] = both[:, :C].reshape(group, BLK, C)
        swapped_features[at] = both[:, C:].reshape(group, BLK, C)
        return carry

    loads[0].wait()
    lax.fori_loop(0, half_blocks // group, embed, 0)
    loads[1].wait()
    lax.fori_loop(half_blocks // group, blocks // group, embed, 0)
    loads[2].wait()
    loads[3].wait()
    row_id = lax.broadcasted_iota(jnp.int32, (8, BLK), 0)
    row_kind = row_id % 4
    for b in range(blocks):
        lanes = slice(b * BLK, (b + 1) * BLK)
        off = off_ref[:, lanes].astype(F32)
        meta = jnp.where(row_kind == 0, off[0:1], off[1:2])
        block_meta[b] = jnp.where(row_kind == 2, cells_ref[0:1, lanes].astype(F32), meta)
    table_copy.wait()

    low_lanes = lax.broadcasted_iota(jnp.int32, (BLK, C), 1) < HALF

    def pack(t, dst0, dst1, j):
        at = [table_smem[t, i] for i in range(MOST)]
        dst0[j, :BLK, :] = jnp.where(low_lanes, features[at[0]], swapped_features[at[1]])
        dst1[j] = jnp.where(low_lanes, swapped_features[at[0]], features[at[1]])
        patch = jnp.where(row_id < 4, table_smem[t, 2].astype(F32), table_smem[t, 3].astype(F32))
        meta = jnp.where(row_id < 4, block_meta[at[0]], block_meta[at[1]])
        meta = jnp.where((row_kind == 2) & (patch < 0.0), DEAD, meta)
        dst0[j, BLK:, :] = jnp.where(row_kind == 3, patch, meta).astype(BF)

    sends, gots = (send0, send1), (got0, got1)

    def out_copy(q, j):
        return pltpu.make_async_remote_copy(
            src_ref=sends[q].at[j], dst_ref=gots[q].at[j], send_sem=out_send.at[q, j], recv_sem=out_recv.at[q, j],
            device_id=(z, *target(j)), device_id_type=MESH,
        )

    pl.semaphore_wait(barrier, tiles - 1 + 2 + len(edges))

    def start_first(j, carry):
        tr, tc = target(j)
        pack(tr * cols + tc, send0, send1, j)
        out_copy(0, j).start()
        return carry

    def start_second(j, carry):
        out_copy(1, j).start()
        return carry

    lax.fori_loop(1, tiles, start_first, 0)
    lax.fori_loop(1, tiles, start_second, 0)
    pack(r * cols + c, got0, got1, 0)

    ones = jnp.ones((8, BLK), BF)
    zero_block = jnp.zeros((BLK, C), BF)
    sums0[0] = jnp.zeros((FOLD, C), F32)
    sums1[0] = jnp.zeros((FOLD, C), F32)
    density_sums[0] = jnp.zeros((8, CELLS), F32)

    def folded(matrix, stream, i):
        other = swapped(stream).astype(BF)
        low, high = (stream, other) if i == 0 else (other, stream)
        right = jnp.concatenate([jnp.where(low_lanes, low, zero_block), jnp.where(low_lanes, zero_block, high)], axis=0)
        left = jnp.concatenate([matrix[:FOLD], matrix[FOLD:]], axis=1)
        return jnp.dot(left, right, preferred_element_type=F32)

    def receive0(j):
        metas = got0[j, BLK:, :].astype(F32)
        stream = got0[j, :BLK, :]
        for i in range(MOST):
            meta = metas[4 * i : 4 * i + 4]
            matrix = window_weights(meta)
            matrices[j * MOST + i] = matrix
            patch_rows[j * MOST + i] = jnp.broadcast_to(meta[3:4], (8, BLK))
            sums0[1 + j * MOST + i] = folded(matrix, stream, i)
            density_sums[1 + j * MOST + i] = lax.dot_general(ones, matrix, (((1,), (1,)), ((), ())), preferred_element_type=F32)

    unroll = min(4, tiles // 2)

    def step0(p, carry):
        for u in range(unroll):
            out_copy(0, p * unroll + u).wait_recv()
        for u in range(unroll):
            receive0(p * unroll + u)
        return carry

    for u in range(1, unroll):
        out_copy(0, u).wait_recv()
    for u in range(unroll):
        receive0(u)
    lax.fori_loop(1, tiles // unroll, step0, 0)

    by_row = jnp.concatenate([patch_rows[s, 0:1, :] for s in range(slots)], axis=0)
    slot_row = lax.broadcasted_iota(jnp.int32, (slots, C), 0)
    lane = lax.broadcasted_iota(jnp.int32, (slots, C), 1)
    by_lane = jnp.sum(jnp.where(slot_row == lane, by_row, 0.0), axis=0, keepdims=True)
    earlier = jnp.max(jnp.where((by_row == by_lane) & (slot_row < lane), slot_row + 1, 0), axis=0, keepdims=True)
    latest = jnp.max(jnp.where(by_row == lane.astype(F32), slot_row + 1, 0), axis=0, keepdims=True)
    link_id = lax.broadcasted_iota(jnp.int32, (8, C), 0)
    ids = jnp.clip(by_lane.astype(jnp.int32), 0, ORBITS * PATCHES - 1)
    links[...] = jnp.where(link_id == 0, earlier, jnp.where(link_id == 1, latest, ids))
    link_copy = pltpu.make_async_copy(links, links_smem, link_sem.at[0])
    link_copy.start()
    link_copy.wait()

    def chain(s, carry):
        e = links_smem[0, s]
        sums0[s + 1] = sums0[s + 1] + sums0[e]
        density_sums[s + 1] = density_sums[s + 1] + density_sums[e]
        return carry

    lax.fori_loop(0, slots, chain, 0)

    for p in range(ORBITS * PATCHES):
        at = links_smem[1, p]
        owner, local_patch = p // PATCHES, p % PATCHES
        part0[owner, local_patch * FOLD : (local_patch + 1) * FOLD, :] = sums0[at].astype(BF)
        row = density_sums[at]
        density_rows[owner, local_patch : local_patch + 1, :] = row[0:1, :C]
        density_rows[owner, PATCHES + local_patch : PATCHES + local_patch + 1, :] = row[0:1, C:]
    for owner in range(ORBITS):
        density_part[owner] = density_rows[owner].astype(BF)
        part0[owner, PATCHES * FOLD :, :] = density_part[owner]

    cut = PATCHES * FOLD // 2
    parts = (part0, part1)

    def ring_copy(q, src, dst, way, step, other):
        return pltpu.make_async_remote_copy(
            src_ref=src, dst_ref=dst, send_sem=ring_send.at[q, way, step], recv_sem=ring_recv.at[q, way, step],
            device_id=(other, r, c), device_id_type=MESH,
        )

    def sides(q):
        low, high = pl.ds(0, cut), pl.ds(cut, cut + (DENS if q == 0 else 0))
        return ((0, after, low, high), (1, before, high, low))

    rings = {}

    def ring_start(q, which):
        if q not in rings:
            rings[q] = []
            for way, other, passed, direct in sides(q):
                relay = ring_copy(q, parts[q].at[across, passed], relay_in.at[q, passed], way, 0, other)
                straight = ring_copy(q, parts[q].at[other, direct], part_in.at[q, way, direct], way, 1, other)
                summed = ring_copy(q, relay_out.at[q, passed], part_in.at[q, way, passed], way, 2, other)
                rings[q].append((relay, straight, summed))
        for relay, straight, summed in rings[q]:
            (relay if which == "relay" else straight).start()

    def ring_relay(q):
        for way, other, passed, direct in sides(q):
            relay, straight, summed = rings[q][way]
            relay.wait_recv()
            total = parts[q][other, passed].astype(F32) + relay_in[q, passed].astype(F32)
            relay_out[q, passed] = total.astype(BF)
            summed.start()

    def ring_finish(q):
        for relay, straight, summed in rings[q]:
            straight.wait_recv()
        for relay, straight, summed in rings[q]:
            summed.wait_recv()

    ring_start(0, "relay")
    ring_start(0, "straight")

    def receive1(j):
        stream = got1[j]
        for i in range(MOST):
            s = j * MOST + i
            sums1[s + 1] = folded(matrices[s], stream, i) + sums1[links_smem[0, s]]

    def step1(p, carry):
        for j in (2 * p, 2 * p + 1):
            out_copy(1, j).wait_recv()
        for j in (2 * p, 2 * p + 1):
            receive1(j)
        return carry

    receive1(0)
    out_copy(1, 1).wait_recv()
    receive1(1)
    middle = max(1, tiles // 4)
    lax.fori_loop(1, middle, step1, 0)
    ring_relay(0)
    lax.fori_loop(middle, tiles // 2, step1, 0)
    def fill_part1(owner):
        for p in range(PATCHES):
            part1[owner, p * FOLD : (p + 1) * FOLD, :] = sums1[links_smem[1, owner * PATCHES + p]].astype(BF)

    fill_part1(across)
    ring_start(1, "relay")
    fill_part1(after)
    fill_part1(before)
    ring_start(1, "straight")
    fill_part1(z)
    ring_finish(0)

    zero_lanes = jnp.zeros((CELLS, C), BF)
    one_cells = jnp.ones((CELLS, C), BF)
    cell_low = lax.broadcasted_iota(jnp.int32, (CELLS, C), 1) < HALF
    one_pair = jnp.concatenate([jnp.where(cell_low, one_cells, zero_lanes), jnp.where(cell_low, zero_lanes, one_cells)], axis=0)

    def prepare(j, carry):
        turned[j] = jnp.concatenate([matrices[j * MOST].T, matrices[j * MOST + 1].T], axis=1)
        total = jnp.dot(turned[j], one_pair, preferred_element_type=F32)
        inverse[j] = 1.0 / jnp.where(total > 0.0, total, 1.0)
        return carry

    quarter = max(1, tiles // 4)

    tail = pl.ds(PATCHES * FOLD, DENS)
    dens_in = jnp.concatenate([part0[z, tail], part_in[0, 0, tail], part_in[0, 1, tail]], axis=0)
    pick_shape = (3 * DENS, DENS * C)
    picked = lax.broadcasted_iota(jnp.int32, pick_shape, 0) % DENS == lax.broadcasted_iota(jnp.int32, pick_shape, 1) // C
    density_all = lax.dot_general(dens_in, picked.astype(BF), (((0,), (0,)), ((), ())), preferred_element_type=F32)
    weight_swapped = jnp.concatenate([dw_ref[:, HALF:], dw_ref[:, :HALF]], axis=1)
    low_row = lax.broadcasted_iota(jnp.int32, (1, C), 1) < HALF
    weights = (jnp.where(low_row, dw_ref[...], weight_swapped), jnp.where(low_row, weight_swapped, dw_ref[...]))

    def grid_value(q, p):
        cells = pl.ds(p * FOLD, FOLD)
        density = jnp.where(
            low_lanes, density_all[:, p * C : (p + 1) * C], density_all[:, (PATCHES + p) * C : (PATCHES + p + 1) * C]
        )
        total = parts[q][z, cells].astype(F32) + part_in[q, 0, cells].astype(F32) + part_in[q, 1, cells].astype(F32)
        return total / jnp.maximum(density, 1.0) + weights[q] * (density / (1.0 + density))

    for p in range(PATCHES):
        packed[p] = grid_value(0, p)
    lax.fori_loop(0, quarter, prepare, 0)
    ring_relay(1)
    lax.fori_loop(quarter, 2 * quarter, prepare, 0)
    ring_finish(1)
    for p in range(PATCHES):
        x0, x1 = packed[p], grid_value(1, p)
        top, left = p // WIDE * PH, p % WIDE * PW
        lower = jnp.where(low_lanes, x0, swapped(x1)).astype(BF)
        upper = jnp.where(low_lanes, swapped(x0), x1).astype(BF)
        tile[top : top + PH // 2, left : left + PW, :] = lower.reshape(PH // 2, PW, C)
        tile[top + PH // 2 : top + PH, left : left + PW, :] = upper.reshape(PH // 2, PW, C)

    for i in range(SR):
        for k in range(2):
            col_out[0, k, i : i + 1, :] = tile[i, k : k + 1, :]
            col_out[1, k, i : i + 1, :] = tile[i, TC - 2 + k : TC - 1 + k, :]
    edge_copies = []
    for e, (up, side) in enumerate(edges):
        if side == 0:
            src, dst = tile.at[pl.ds(0 if up < 0 else SR - 2, 2)], row_in.at[e]
        else:
            src, dst = col_out.at[0 if side < 0 else 1], col_in.at[e - 2]
        edge_copies.append(pltpu.make_async_remote_copy(
            src_ref=src, dst_ref=dst, send_sem=edge_send.at[e], recv_sem=edge_recv.at[e],
            device_id=edge_device(up, side), device_id_type=MESH,
        ))
    for copy in edge_copies:
        copy.start()

    def shifts(row, centre):
        centre = centre.astype(F32)
        wide[row, :, 0:C] = pltpu.roll(centre, 1, 0).astype(BF)
        wide[row, :, C : 2 * C] = centre.astype(BF)
        wide[row, :, 2 * C :] = pltpu.roll(centre, TC - 1, 0).astype(BF)

    def convolved(i, height, w_ref, b_ref):
        total = None
        for a in range(3):
            x = wide[pl.ds(i + a, height)].reshape(height * TC, 3 * C)
            term = jnp.dot(x, w_ref[a], preferred_element_type=F32)
            total = term if total is None else total + term
        return total + b_ref[...]

    def silu(v):
        return v / (1.0 + jnp.exp(-v))

    for i in range(SR):
        shifts(i + 2, tile[i])
    loads[4].wait()
    loads[5].wait()
    for copy in edge_copies:
        copy.wait_recv()
    has_above, has_below = stripe > 0, stripe < stripes - 1
    for k in range(2):
        shifts(k, jnp.where(has_above, row_in[1, k].astype(F32), 0.0))
        shifts(SR + 2 + k, jnp.where(has_below, row_in[0, k].astype(F32), 0.0))
    for s, (first_edge, open_) in enumerate(((3, c > 0), (0, c < cols - 1))):
        own_at, own_lanes = (0, slice(2 * C, 3 * C)) if s == 0 else (TC - 1, slice(0, C))
        side_in[s, 2 : SR + 2, own_lanes] = col_out[s, s].astype(F32)
        for k in range(2):
            side_in[s, k : k + 1, own_lanes] = jnp.where(has_above, row_in[1, k, own_at : own_at + 1, :].astype(F32), 0.0)
            side_in[s, SR + 2 + k : SR + 3 + k, own_lanes] = jnp.where(has_below, row_in[0, k, own_at : own_at + 1, :].astype(F32), 0.0)
            lanes = slice((k + s) * C, (k + s + 1) * C)
            above = col_in[first_edge + 2, k].astype(F32)[SR - 2 :]
            below = col_in[first_edge, k].astype(F32)[:2]
            side_in[s, 0:2, lanes] = jnp.where(open_ & has_above, above, 0.0)
            side_in[s, 2 : SR + 2, lanes] = jnp.where(open_, col_in[first_edge + 1, k].astype(F32), 0.0)
            side_in[s, SR + 2 : SR + 4, lanes] = jnp.where(open_ & has_below, below, 0.0)
    for i in range(SR + 4):
        wide[i, 0:1, 0:C] = side_in[0, i : i + 1, C : 2 * C].astype(BF)
        wide[i, TC - 1 : TC, 2 * C :] = side_in[1, i : i + 1, C : 2 * C].astype(BF)

    tall = 6
    for i in range(0, SR + 2, tall):
        first[i : i + tall] = silu(convolved(i, tall, w1_ref, b1_ref)).astype(BF).reshape(tall, TC, C)
    side_row = lax.broadcasted_iota(jnp.int32, (SR + 2, C), 0)
    inside = ((side_row > 0) | has_above) & ((side_row < SR + 1) | has_below)
    for s, open_ in enumerate((c > 0, c < cols - 1)):
        total = None
        for a in range(3):
            term = jnp.dot(side_in[s, a : a + SR + 2, :].astype(BF), w1_ref[a], preferred_element_type=F32)
            total = term if total is None else total + term
        side_first[s, 0 : SR + 2, :] = jnp.where(inside & open_, silu(total + b1_ref[...]), 0.0)
    for i in range(SR + 2):
        row = first[i].astype(F32)
        if i == 0:
            row = jnp.where(has_above, row, 0.0)
        if i == SR + 1:
            row = jnp.where(has_below, row, 0.0)
        shifts(i, row)
    for i in range(SR + 2):
        wide[i, 0:1, 0:C] = side_first[0, i : i + 1, :].astype(BF)
        wide[i, TC - 1 : TC, 2 * C :] = side_first[1, i : i + 1, :].astype(BF)
    block_rows = PH // 2

    count = PATCHES // 2
    values = (values0, values1)

    def half_of(q, owner, h):
        return values[q].at[pl.ds(owner * PATCHES + h * count, count)]

    def gather_copy(q, owner, h, way, step, src):
        return pltpu.make_async_remote_copy(
            src_ref=src, dst_ref=half_of(q, owner, h), send_sem=gather_send.at[q, way, step],
            recv_sem=gather_recv.at[q, way, step], device_id=((after, before)[way], r, c), device_id_type=MESH,
        )

    gathers = []

    def gather_start(q, h):
        for way in range(2):
            copy = gather_copy(q, z, h, way, h, mine.at[q, pl.ds(h * count, count)])
            copy.start()
            gathers.append(copy)

    near = (before, after)

    def gather_relay(q):
        for way in range(2):
            gather_copy(q, near[way], way, way, way, half_of(q, near[way], way)).wait_recv()
            copy = gather_copy(q, near[way], way, way, 2, half_of(q, near[way], way))
            copy.start()
            gathers.append(copy)

    def gather_finish(q):
        for way in range(2):
            gather_copy(q, near[way], 1 - way, way, 1 - way, half_of(q, near[way], 1 - way)).wait_recv()
        for way in range(2):
            gather_copy(q, across, way, way, 2, half_of(q, across, way)).wait_recv()

    for h in range(2):
        halves, others = [], []
        for i in range(h * PH, (h + 1) * PH, block_rows):
            v = convolved(i, block_rows, w2_ref, b2_ref).reshape(block_rows, TC, C)
            v = (tile[i : i + block_rows].astype(F32) + v).astype(BF)
            grid_ref[i : i + block_rows] = v
            halves.append(v)
        for w in range(WIDE):
            lower = halves[0][:, w * PW : (w + 1) * PW, :].reshape(FOLD, C)
            upper = halves[1][:, w * PW : (w + 1) * PW, :].reshape(FOLD, C)
            mine[0, h * count + w] = jnp.where(low_lanes, lower, swapped(upper).astype(BF))
            others.append((h * count + w, lower, upper))
        gather_start(0, h)
        for at, lower, upper in others:
            mine[1, at] = jnp.where(low_lanes, swapped(lower).astype(BF), upper)
    grid_copy = pltpu.make_async_copy(grid_ref, grid_hbm, grid_sem)
    grid_copy.start()
    for q in range(2):
        values[q][pl.ds(z * PATCHES, PATCHES)] = mine[q]
    lax.fori_loop(2 * quarter, 3 * quarter, prepare, 0)
    gather_relay(0)
    gather_start(1, 0)
    gather_start(1, 1)
    lax.fori_loop(3 * quarter, tiles, prepare, 0)
    gather_finish(0)

    def swap_values(q):
        def one(p, carry):
            values_swapped[q, p] = swapped(values[q][p]).astype(BF)
            return carry

        lax.fori_loop(0, ORBITS * PATCHES, one, 0)

    def read(q, j, target_ref):
        a, b = [links_smem[2, j * MOST + i] for i in range(MOST)]
        right = jnp.concatenate([
            jnp.where(low_lanes, values[q][a], zero_block), jnp.where(low_lanes, values_swapped[q, a], zero_block),
            jnp.where(low_lanes, zero_block, values_swapped[q, b]), jnp.where(low_lanes, zero_block, values[q][b]),
        ], axis=0)
        target_ref[j] = (jnp.dot(turned[j], right, preferred_element_type=F32) * inverse[j]).astype(BF)

    back = (back0, back1)

    def back_copy(q, j):
        return pltpu.make_async_remote_copy(
            src_ref=back_out.at[q, j], dst_ref=back[q].at[j], send_sem=back_send.at[q, j], recv_sem=back_recv.at[q, j],
            device_id=(z, *source(j)), device_id_type=MESH,
        )

    def read_and_send(q):
        def step(p, carry):
            for u in range(2):
                read(q, 2 * p + u, back_out.at[q])
            for u in range(2):
                back_copy(q, 2 * p + u).start()
            return carry

        return step

    def read_first(q):
        read(q, 1, back_out.at[q])
        back_copy(q, 1).start()
        read(q, 0, back[q])

    swap_values(0)
    read_first(0)
    lax.fori_loop(1, quarter, read_and_send(0), 0)
    gather_relay(1)
    lax.fori_loop(quarter, tiles // 2, read_and_send(0), 0)
    gather_finish(1)
    swap_values(1)
    read_first(1)
    lax.fori_loop(1, tiles // 2, read_and_send(1), 0)

    def arrive(q):
        def step(j, carry):
            back_copy(q, j).wait_recv()
            return carry

        return step

    together = min(4, blocks)

    def combine(q):
        def step(i, carry):
            for u in range(together):
                b = i * together + u
                t = tile_of[b]
                k = (t // cols + rows - r) % rows * cols + (t % cols + cols - c) % cols
                j = jnp.where(k == 0, 0, (k - 1 + tiles - 1 - tiles // 2) % (tiles - 1) + 1)
                in_place = jnp.full((BLK, C), (table_smem[t, 0] == b).astype(jnp.int32)) == 1 - q
                x = back[q][j].astype(F32)
                value = (features[b].astype(F32) + jnp.where(in_place, x, swapped(x))).astype(BF)
                out_ref[b] = value if q == 0 else jnp.where(low_lanes, out_ref[b], value)
            if q == 1:
                store(i).start()
            return carry

        return step

    def store(i):
        some = pl.ds(i * together, together)
        return pltpu.make_async_copy(out_ref.at[some], out_hbm.at[some], store_sem.at[i])

    for q in range(2):
        lax.fori_loop(1, tiles, arrive(q), 0)
        lax.fori_loop(0, blocks // together, combine(q), 0)

    def stored(i, carry):
        store(i).wait()
        return carry

    def sent(j, carry):
        for q in range(2):
            out_copy(q, j).wait_send()
            back_copy(q, j).wait_send()
        return carry

    lax.fori_loop(1, tiles, sent, 0)
    lax.fori_loop(0, blocks // together, stored, 0)
    grid_copy.wait()
    for q in range(2):
        for copies in rings[q]:
            for copy in copies:
                copy.wait_send()
    for copy in gathers + edge_copies:
        copy.wait_send()


def local(
    obs_feat, obs_offset, obs_cells, block_tile, block_patch, w_embed, b_embed, w_proj, b_proj, density_weight,
    w_first, b_first, w_second, b_second,
):
    blocks = block_tile.shape[0]
    rows, cols = lax.axis_size("rows"), lax.axis_size("cols")
    tiles = rows * cols
    slots = tiles * MOST
    patches = ORBITS * PATCHES

    vm = pl.BlockSpec(memory_space=VMEM)
    sm = pl.BlockSpec(memory_space=SMEM)
    part_rows = PATCHES * FOLD + DENS
    dma = pltpu.SemaphoreType.DMA
    obs_out, grid_out = pl.pallas_call(
        functools.partial(main_kernel, rows, cols, blocks),
        grid=(1,),
        out_shape=(jax.ShapeDtypeStruct((blocks, BLK, C), BF), jax.ShapeDtypeStruct((SR, TC, C), BF)),
        in_specs=[sm, vm, vm] + [pl.BlockSpec(memory_space=pl.ANY)] * 5 + [vm] * 7,
        out_specs=(pl.BlockSpec(memory_space=pl.ANY),) * 2,
        scratch_shapes=[
            VMEM((blocks, BLK, C), BF),
            VMEM((SR, TC, C), BF),
            VMEM((blocks, BLK, C), BF),
            VMEM((2, blocks * BLK), BF),
            VMEM((8, blocks * BLK), jnp.int32),
            VMEM((3, 3 * C, C), BF),
            VMEM((3, 3 * C, C), BF),
            VMEM((tiles, C), jnp.int32),
            SMEM((tiles, C), jnp.int32),
            VMEM((blocks, BLK, C), BF),
            VMEM((blocks, BLK, C), BF),
            VMEM((blocks, 8, BLK), F32),
            VMEM((tiles, BLK + META, C), BF),
            VMEM((tiles, BLK, C), BF),
            VMEM((tiles, BLK + META, C), BF),
            VMEM((tiles, BLK, C), BF),
            VMEM((slots, CELLS, BLK), BF),
            VMEM((slots, 8, BLK), F32),
            VMEM((tiles, BLK, MOST * CELLS), BF),
            VMEM((tiles, BLK, C), F32),
            VMEM((slots + 1, FOLD, C), F32),
            VMEM((slots + 1, FOLD, C), F32),
            VMEM((slots + 1, 8, CELLS), F32),
            VMEM((8, C), jnp.int32),
            SMEM((8, C), jnp.int32),
            VMEM((ORBITS, DENS, C), F32),
            VMEM((ORBITS, part_rows, C), BF),
            VMEM((ORBITS, part_rows, C), BF),
            VMEM((ORBITS, DENS, C), BF),
            VMEM((2, part_rows, C), BF),
            VMEM((2, part_rows, C), BF),
            VMEM((2, 2, part_rows, C), BF),
            VMEM((PATCHES, FOLD, C), F32),
            VMEM((SR, TC, C), BF),
            VMEM((SR + 4, TC, 3 * C), BF),
            VMEM((SR + 2, TC, C), BF),
            VMEM((2, SR + 8, 3 * C), F32),
            VMEM((2, SR + 8, C), F32),
            VMEM((2, 2, SR, C), BF),
            VMEM((2, 2, TC, C), BF),
            VMEM((6, 2, SR, C), BF),
            VMEM((2, PATCHES, FOLD, C), BF),
            VMEM((patches, FOLD, C), BF),
            VMEM((patches, FOLD, C), BF),
            VMEM((2, patches, FOLD, C), BF),
            VMEM((2, tiles, BLK, C), BF),
            VMEM((tiles, BLK, C), BF),
            VMEM((tiles, BLK, C), BF),
            dma((2, tiles)),
            dma((2, tiles)),
            dma((2, 2, 3)),
            dma((2, 2, 3)),
            dma((8,)),
            dma((8,)),
            dma((2, 2, 3)),
            dma((2, 2, 3)),
            dma((2, tiles)),
            dma((2, tiles)),
            dma((2,)),
            dma((6,)),
            dma((blocks // min(4, blocks),)),
            dma,
        ],
        compiler_params=pltpu.CompilerParams(collective_id=0, has_side_effects=True, vmem_limit_bytes=63000000),
        name="encode",
    )(
        block_tile, block_tile[None, :], block_patch[None, :], obs_feat.reshape(blocks, BLK, C), obs_offset, obs_cells,
        w_first.reshape(3, 3 * C, C), w_second.reshape(3, 3 * C, C), w_embed, b_embed[None, :], w_proj, b_proj[None, :],
        density_weight[None, :], b_first[None, :], b_second[None, :],
    )
    return (obs_out.reshape(obs_feat.shape), grid_out)


def solution(mesh):
    by_device = P(("orbits", "rows", "cols"))
    in_specs = (
        P(("orbits", "rows", "cols"), None), P(None, ("orbits", "rows", "cols")), P(None, ("orbits", "rows", "cols")),
        by_device, by_device, P(), P(), P(), P(), P(), P(), P(), P(), P(),
    )
    out_specs = (P(("orbits", "rows", "cols"), None), P(("orbits", "rows"), "cols", None))
    return jax.shard_map(local, mesh=mesh, in_specs=in_specs, out_specs=out_specs, check_vma=False)
```

```python
import functools

import jax
import jax.numpy as jnp
from jax import lax
from jax.experimental import pallas as pl
from jax.experimental.pallas import tpu as pltpu
from jax.sharding import PartitionSpec as P

PH = 8
PW = 32
SR = 16
TC = 128
BLK = 128
C = 128
HALF = C // 2
MOST = 2
CELLS = PH * PW
FOLD = CELLS // 2
WIDE = TC // PW
PATCHES = SR // PH * WIDE
DENS = 2 * PATCHES
META = 8
DEAD = -128.0
ORBITS = 4
MESH = pl.DeviceIdType.MESH
VMEM = pltpu.VMEM
SMEM = pltpu.SMEM
BF = jnp.bfloat16
F32 = jnp.float32


def window_weights(meta_rows):
    off_r, off_c, anchor = meta_rows[0:1], meta_rows[1:2], meta_rows[2:3]
    anchor_r = jnp.floor(anchor * (1.0 / PW))
    anchor_c = anchor - anchor_r * PW
    tap_r = lax.broadcasted_iota(jnp.int32, (PH, BLK), 0).astype(F32) - anchor_r
    tap_c = lax.broadcasted_iota(jnp.int32, (PW, BLK), 0).astype(F32) - anchor_c
    delta_r = tap_r - 1.5 - off_r
    delta_c = tap_c - 1.5 - off_c
    weight_r = jnp.where((tap_r >= 0.0) & (tap_r < 4.0), jnp.exp(delta_r * delta_r * -0.5), 0.0)
    weight_c = jnp.where((tap_c >= 0.0) & (tap_c < 4.0), jnp.exp(delta_c * delta_c * -0.5), 0.0)
    return jnp.concatenate([(weight_r[r : r + 1] * weight_c).astype(BF) for r in range(PH)], axis=0)


def swapped(x):
    return pltpu.roll(x.astype(F32), HALF, 1)


def main_kernel(
    rows, cols, blocks,
    tile_of, tile_row, patch_row, feat_hbm, off_hbm, cells_hbm, w1_hbm, w2_hbm,
    we_ref, be_ref, wp_ref, bp_ref, dw_ref, b1_ref, b2_ref,
    out_hbm, grid_hbm,
    out_ref, grid_ref, feat_ref, off_ref, cells_ref, w1_ref, w2_ref, table, table_smem,
    features, swapped_features, block_meta, send0, send1, got0, got1, matrices, patch_rows,
    turned, inverse, sums0, sums1, density_sums, links, links_smem, density_rows, part0, part1, density_part, relay_in, relay_out, part_in,
    packed, tile, wide, first, side_in, side_first, col_out, row_in, col_in, mine, values0, values1, values_swapped, back_out, back0, back1,
    out_send, out_recv, ring_send, ring_recv, edge_send, edge_recv, gather_send, gather_recv, back_send, back_recv, link_sem, load_sem, store_sem, grid_sem,
):
    z, r, c = lax.axis_index("orbits"), lax.axis_index("rows"), lax.axis_index("cols")
    tiles = rows * cols
    slots = tiles * MOST
    stripes = ORBITS * rows
    stripe = z * rows + r
    after, before = (z + 1) % ORBITS, (z + ORBITS - 1) % ORBITS
    across = (z + 2) % ORBITS

    def offset_of(j):
        return (j - 1 + tiles // 2) % (tiles - 1) + 1

    def target(j):
        k = offset_of(j)
        return (r + k // cols) % rows, (c + k % cols) % cols

    def source(j):
        k = offset_of(j)
        return (r + rows - k // cols) % rows, (c + cols - k % cols) % cols

    def edge_device(up, side):
        other = (stripe + stripes + up) % stripes
        return (other // rows, other % rows, (c + cols + side) % cols)

    edges = ((-1, 0), (1, 0), (-1, -1), (0, -1), (1, -1), (-1, 1), (0, 1), (1, 1))
    barrier = pltpu.get_barrier_semaphore()

    def greet(j, carry):
        pl.semaphore_signal(barrier, inc=1, device_id=(z, *target(j)), device_id_type=MESH)
        return carry

    lax.fori_loop(1, tiles, greet, 0)
    for other in (after, before):
        pl.semaphore_signal(barrier, inc=1, device_id=(other, r, c), device_id_type=MESH)
    for up, side in edges:
        pl.semaphore_signal(barrier, inc=1, device_id=edge_device(up, side), device_id_type=MESH)

    half_blocks = blocks // 2
    loads = [
        pltpu.make_async_copy(feat_hbm.at[pl.ds(0, half_blocks)], feat_ref.at[pl.ds(0, half_blocks)], load_sem.at[0]),
        pltpu.make_async_copy(feat_hbm.at[pl.ds(half_blocks, half_blocks)], feat_ref.at[pl.ds(half_blocks, half_blocks)], load_sem.at[1]),
        pltpu.make_async_copy(off_hbm, off_ref, load_sem.at[2]),
        pltpu.make_async_copy(cells_hbm.at[pl.ds(0, 8)], cells_ref, load_sem.at[3]),
        pltpu.make_async_copy(w1_hbm, w1_ref, load_sem.at[4]),
        pltpu.make_async_copy(w2_hbm, w2_ref, load_sem.at[5]),
    ]
    for load in loads:
        load.start()

    square = (tiles, blocks)
    block_id = lax.broadcasted_iota(jnp.int32, square, 1).astype(F32)
    hit = tile_row[...] == lax.broadcasted_iota(jnp.int32, square, 0)
    lowest = jnp.min(jnp.where(hit, block_id, float(blocks)), axis=1, keepdims=True)
    highest = jnp.max(jnp.where(hit, block_id, -1.0), axis=1, keepdims=True)
    row_patches = patch_row[...].astype(F32)
    patch_low = jnp.max(jnp.where(block_id == lowest, row_patches, -1.0), axis=1, keepdims=True)
    patch_high = jnp.max(jnp.where((block_id == highest) & (highest > lowest), row_patches, -1.0), axis=1, keepdims=True)
    entry = lax.broadcasted_iota(jnp.int32, (tiles, C), 1)
    found = jnp.where(entry == 0, lowest, jnp.where(entry == 1, highest, jnp.where(entry == 2, patch_low, patch_high)))
    found = found.astype(jnp.int32)
    table[...] = jnp.where(entry < 2, jnp.clip(found, 0, blocks - 1), found)
    table_copy = pltpu.make_async_copy(table, table_smem, link_sem.at[1])
    table_copy.start()

    group = min(8, half_blocks)
    proj = jnp.concatenate([wp_ref[...], swapped(wp_ref[...]).astype(BF)], axis=1)
    proj_bias = jnp.concatenate([bp_ref[...], jnp.concatenate([bp_ref[:, HALF:], bp_ref[:, :HALF]], axis=1)], axis=1)

    def embed(i, carry):
        at = pl.ds(i * group, group)
        x = feat_ref[at].reshape(group * BLK, C)
        v = jnp.dot(x, we_ref[...], preferred_element_type=F32) + be_ref[...]
        hidden = (v / (1.0 + jnp.exp(-v))).astype(BF)
        both = (jnp.dot(hidden, proj, preferred_element_type=F32) + proj_bias).astype(BF)
        features[at] = both[:, :C].reshape(group, BLK, C)
        swapped_features[at] = both[:, C:].reshape(group, BLK, C)
        return carry

    loads[0].wait()
    lax.fori_loop(0, half_blocks // group, embed, 0)
    loads[1].wait()
    lax.fori_loop(half_blocks // group, blocks // group, embed, 0)
    loads[2].wait()
    loads[3].wait()
    row_id = lax.broadcasted_iota(jnp.int32, (8, BLK), 0)
    row_kind = row_id % 4
    for b in range(blocks):
        lanes = slice(b * BLK, (b + 1) * BLK)
        off = off_ref[:, lanes].astype(F32)
        meta = jnp.where(row_kind == 0, off[0:1], off[1:2])
        block_meta[b] = jnp.where(row_kind == 2, cells_ref[0:1, lanes].astype(F32), meta)
    table_copy.wait()

    low_lanes = lax.broadcasted_iota(jnp.int32, (BLK, C), 1) < HALF

    def pack(t, dst0, dst1, j):
        at = [table_smem[t, i] for i in range(MOST)]
        dst0[j, :BLK, :] = jnp.where(low_lanes, features[at[0]], swapped_features[at[1]])
        dst1[j] = jnp.where(low_lanes, swapped_features[at[0]], features[at[1]])
        patch = jnp.where(row_id < 4, table_smem[t, 2].astype(F32), table_smem[t, 3].astype(F32))
        meta = jnp.where(row_id < 4, block_meta[at[0]], block_meta[at[1]])
        meta = jnp.where((row_kind == 2) & (patch < 0.0), DEAD, meta)
        dst0[j, BLK:, :] = jnp.where(row_kind == 3, patch, meta).astype(BF)

    sends, gots = (send0, send1), (got0, got1)

    def out_copy(q, j):
        return pltpu.make_async_remote_copy(
            src_ref=sends[q].at[j], dst_ref=gots[q].at[j], send_sem=out_send.at[q, j], recv_sem=out_recv.at[q, j],
            device_id=(z, *target(j)), device_id_type=MESH,
        )

    pl.semaphore_wait(barrier, tiles - 1 + 2 + len(edges))

    def start_first(j, carry):
        tr, tc = target(j)
        pack(tr * cols + tc, send0, send1, j)
        out_copy(0, j).start()
        return carry

    def start_second(j, carry):
        out_copy(1, j).start()
        return carry

    lax.fori_loop(1, tiles, start_first, 0)
    lax.fori_loop(1, tiles, start_second, 0)
    pack(r * cols + c, got0, got1, 0)

    ones = jnp.ones((8, BLK), BF)
    zero_block = jnp.zeros((BLK, C), BF)
    sums0[0] = jnp.zeros((FOLD, C), F32)
    sums1[0] = jnp.zeros((FOLD, C), F32)
    density_sums[0] = jnp.zeros((8, CELLS), F32)

    def folded(matrix, stream, i):
        other = swapped(stream).astype(BF)
        low, high = (stream, other) if i == 0 else (other, stream)
        right = jnp.concatenate([jnp.where(low_lanes, low, zero_block), jnp.where(low_lanes, zero_block, high)], axis=0)
        left = jnp.concatenate([matrix[:FOLD], matrix[FOLD:]], axis=1)
        return jnp.dot(left, right, preferred_element_type=F32)

    def receive0(j):
        metas = got0[j, BLK:, :].astype(F32)
        stream = got0[j, :BLK, :]
        for i in range(MOST):
            meta = metas[4 * i : 4 * i + 4]
            matrix = window_weights(meta)
            matrices[j * MOST + i] = matrix
            patch_rows[j * MOST + i] = jnp.broadcast_to(meta[3:4], (8, BLK))
            sums0[1 + j * MOST + i] = folded(matrix, stream, i)
            density_sums[1 + j * MOST + i] = lax.dot_general(ones, matrix, (((1,), (1,)), ((), ())), preferred_element_type=F32)

    unroll = min(4, tiles // 2)

    def step0(p, carry):
        for u in range(unroll):
            out_copy(0, p * unroll + u).wait_recv()
        for u in range(unroll):
            receive0(p * unroll + u)
        return carry

    for u in range(1, unroll):
        out_copy(0, u).wait_recv()
    for u in range(unroll):
        receive0(u)
    lax.fori_loop(1, tiles // unroll, step0, 0)

    by_row = jnp.concatenate([patch_rows[s, 0:1, :] for s in range(slots)], axis=0)
    slot_row = lax.broadcasted_iota(jnp.int32, (slots, C), 0)
    lane = lax.broadcasted_iota(jnp.int32, (slots, C), 1)
    by_lane = jnp.sum(jnp.where(slot_row == lane, by_row, 0.0), axis=0, keepdims=True)
    earlier = jnp.max(jnp.where((by_row == by_lane) & (slot_row < lane), slot_row + 1, 0), axis=0, keepdims=True)
    latest = jnp.max(jnp.where(by_row == lane.astype(F32), slot_row + 1, 0), axis=0, keepdims=True)
    link_id = lax.broadcasted_iota(jnp.int32, (8, C), 0)
    ids = jnp.clip(by_lane.astype(jnp.int32), 0, ORBITS * PATCHES - 1)
    links[...] = jnp.where(link_id == 0, earlier, jnp.where(link_id == 1, latest, ids))
    link_copy = pltpu.make_async_copy(links, links_smem, link_sem.at[0])
    link_copy.start()
    link_copy.wait()

    def chain(s, carry):
        e = links_smem[0, s]
        sums0[s + 1] = sums0[s + 1] + sums0[e]
        density_sums[s + 1] = density_sums[s + 1] + density_sums[e]
        return carry

    lax.fori_loop(0, slots, chain, 0)

    for p in range(ORBITS * PATCHES):
        at = links_smem[1, p]
        owner, local_patch = p // PATCHES, p % PATCHES
        part0[owner, local_patch * FOLD : (local_patch + 1) * FOLD, :] = sums0[at].astype(BF)
        row = density_sums[at]
        density_rows[owner, local_patch : local_patch + 1, :] = row[0:1, :C]
        density_rows[owner, PATCHES + local_patch : PATCHES + local_patch + 1, :] = row[0:1, C:]
    for owner in range(ORBITS):
        density_part[owner] = density_rows[owner].astype(BF)
        part0[owner, PATCHES * FOLD :, :] = density_part[owner]

    cut = PATCHES * FOLD // 2
    parts = (part0, part1)

    def ring_copy(q, src, dst, way, step, other):
        return pltpu.make_async_remote_copy(
            src_ref=src, dst_ref=dst, send_sem=ring_send.at[q, way, step], recv_sem=ring_recv.at[q, way, step],
            device_id=(other, r, c), device_id_type=MESH,
        )

    def sides(q):
        low, high = pl.ds(0, cut), pl.ds(cut, cut + (DENS if q == 0 else 0))
        return ((0, after, low, high), (1, before, high, low))

    rings = {}

    def ring_start(q, which):
        if q not in rings:
            rings[q] = []
            for way, other, passed, direct in sides(q):
                relay = ring_copy(q, parts[q].at[across, passed], relay_in.at[q, passed], way, 0, other)
                straight = ring_copy(q, parts[q].at[other, direct], part_in.at[q, way, direct], way, 1, other)
                summed = ring_copy(q, relay_out.at[q, passed], part_in.at[q, way, passed], way, 2, other)
                rings[q].append((relay, straight, summed))
        for relay, straight, summed in rings[q]:
            (relay if which == "relay" else straight).start()

    def ring_relay(q):
        for way, other, passed, direct in sides(q):
            relay, straight, summed = rings[q][way]
            relay.wait_recv()
            total = parts[q][other, passed].astype(F32) + relay_in[q, passed].astype(F32)
            relay_out[q, passed] = total.astype(BF)
            summed.start()

    def ring_finish(q):
        for relay, straight, summed in rings[q]:
            straight.wait_recv()
        for relay, straight, summed in rings[q]:
            summed.wait_recv()

    ring_start(0, "relay")
    ring_start(0, "straight")

    def receive1(j):
        stream = got1[j]
        for i in range(MOST):
            s = j * MOST + i
            sums1[s + 1] = folded(matrices[s], stream, i) + sums1[links_smem[0, s]]

    def step1(p, carry):
        for j in (2 * p, 2 * p + 1):
            out_copy(1, j).wait_recv()
        for j in (2 * p, 2 * p + 1):
            receive1(j)
        return carry

    receive1(0)
    out_copy(1, 1).wait_recv()
    receive1(1)
    middle = max(1, tiles // 4)
    lax.fori_loop(1, middle, step1, 0)
    ring_relay(0)
    lax.fori_loop(middle, tiles // 2, step1, 0)
    def fill_part1(owner):
        for p in range(PATCHES):
            part1[owner, p * FOLD : (p + 1) * FOLD, :] = sums1[links_smem[1, owner * PATCHES + p]].astype(BF)

    fill_part1(across)
    ring_start(1, "relay")
    fill_part1(after)
    fill_part1(before)
    ring_start(1, "straight")
    fill_part1(z)
    ring_finish(0)

    zero_lanes = jnp.zeros((CELLS, C), BF)
    one_cells = jnp.ones((CELLS, C), BF)
    cell_low = lax.broadcasted_iota(jnp.int32, (CELLS, C), 1) < HALF
    one_pair = jnp.concatenate([jnp.where(cell_low, one_cells, zero_lanes), jnp.where(cell_low, zero_lanes, one_cells)], axis=0)

    def prepare(j, carry):
        turned[j] = jnp.concatenate([matrices[j * MOST].T, matrices[j * MOST + 1].T], axis=1)
        total = jnp.dot(turned[j], one_pair, preferred_element_type=F32)
        inverse[j] = 1.0 / jnp.where(total > 0.0, total, 1.0)
        return carry

    quarter = max(1, tiles // 4)

    tail = pl.ds(PATCHES * FOLD, DENS)
    dens_in = jnp.concatenate([part0[z, tail], part_in[0, 0, tail], part_in[0, 1, tail]], axis=0)
    pick_shape = (3 * DENS, DENS * C)
    picked = lax.broadcasted_iota(jnp.int32, pick_shape, 0) % DENS == lax.broadcasted_iota(jnp.int32, pick_shape, 1) // C
    density_all = lax.dot_general(dens_in, picked.astype(BF), (((0,), (0,)), ((), ())), preferred_element_type=F32)
    weight_swapped = jnp.concatenate([dw_ref[:, HALF:], dw_ref[:, :HALF]], axis=1)
    low_row = lax.broadcasted_iota(jnp.int32, (1, C), 1) < HALF
    weights = (jnp.where(low_row, dw_ref[...], weight_swapped), jnp.where(low_row, weight_swapped, dw_ref[...]))

    def grid_value(q, p):
        cells = pl.ds(p * FOLD, FOLD)
        density = jnp.where(
            low_lanes, density_all[:, p * C : (p + 1) * C], density_all[:, (PATCHES + p) * C : (PATCHES + p + 1) * C]
        )
        total = parts[q][z, cells].astype(F32) + part_in[q, 0, cells].astype(F32) + part_in[q, 1, cells].astype(F32)
        return total / jnp.maximum(density, 1.0) + weights[q] * (density / (1.0 + density))

    for p in range(PATCHES):
        packed[p] = grid_value(0, p)
    lax.fori_loop(0, quarter, prepare, 0)
    ring_relay(1)
    lax.fori_loop(quarter, 2 * quarter, prepare, 0)
    ring_finish(1)
    for p in range(PATCHES):
        x0, x1 = packed[p], grid_value(1, p)
        top, left = p // WIDE * PH, p % WIDE * PW
        lower = jnp.where(low_lanes, x0, swapped(x1)).astype(BF)
        upper = jnp.where(low_lanes, swapped(x0), x1).astype(BF)
        tile[top : top + PH // 2, left : left + PW, :] = lower.reshape(PH // 2, PW, C)
        tile[top + PH // 2 : top + PH, left : left + PW, :] = upper.reshape(PH // 2, PW, C)

    for i in range(SR):
        for k in range(2):
            col_out[0, k, i : i + 1, :] = tile[i, k : k + 1, :]
            col_out[1, k, i : i + 1, :] = tile[i, TC - 2 + k : TC - 1 + k, :]
    edge_copies = []
    for e, (up, side) in enumerate(edges):
        if side == 0:
            src, dst = tile.at[pl.ds(0 if up < 0 else SR - 2, 2)], row_in.at[e]
        else:
            src, dst = col_out.at[0 if side < 0 else 1], col_in.at[e - 2]
        edge_copies.append(pltpu.make_async_remote_copy(
            src_ref=src, dst_ref=dst, send_sem=edge_send.at[e], recv_sem=edge_recv.at[e],
            device_id=edge_device(up, side), device_id_type=MESH,
        ))
    for copy in edge_copies:
        copy.start()

    def shifts(row, centre):
        centre = centre.astype(F32)
        wide[row, :, 0:C] = pltpu.roll(centre, 1, 0).astype(BF)
        wide[row, :, C : 2 * C] = centre.astype(BF)
        wide[row, :, 2 * C :] = pltpu.roll(centre, TC - 1, 0).astype(BF)

    def convolved(i, height, w_ref, b_ref):
        total = None
        for a in range(3):
            x = wide[pl.ds(i + a, height)].reshape(height * TC, 3 * C)
            term = jnp.dot(x, w_ref[a], preferred_element_type=F32)
            total = term if total is None else total + term
        return total + b_ref[...]

    def silu(v):
        return v / (1.0 + jnp.exp(-v))

    for i in range(SR):
        shifts(i + 2, tile[i])
    loads[4].wait()
    loads[5].wait()
    for copy in edge_copies:
        copy.wait_recv()
    has_above, has_below = stripe > 0, stripe < stripes - 1
    for k in range(2):
        shifts(k, jnp.where(has_above, row_in[1, k].astype(F32), 0.0))
        shifts(SR + 2 + k, jnp.where(has_below, row_in[0, k].astype(F32), 0.0))
    for s, (first_edge, open_) in enumerate(((3, c > 0), (0, c < cols - 1))):
        own_at, own_lanes = (0, slice(2 * C, 3 * C)) if s == 0 else (TC - 1, slice(0, C))
        side_in[s, 2 : SR + 2, own_lanes] = col_out[s, s].astype(F32)
        for k in range(2):
            side_in[s, k : k + 1, own_lanes] = jnp.where(has_above, row_in[1, k, own_at : own_at + 1, :].astype(F32), 0.0)
            side_in[s, SR + 2 + k : SR + 3 + k, own_lanes] = jnp.where(has_below, row_in[0, k, own_at : own_at + 1, :].astype(F32), 0.0)
            lanes = slice((k + s) * C, (k + s + 1) * C)
            above = col_in[first_edge + 2, k].astype(F32)[SR - 2 :]
            below = col_in[first_edge, k].astype(F32)[:2]
            side_in[s, 0:2, lanes] = jnp.where(open_ & has_above, above, 0.0)
            side_in[s, 2 : SR + 2, lanes] = jnp.where(open_, col_in[first_edge + 1, k].astype(F32), 0.0)
            side_in[s, SR + 2 : SR + 4, lanes] = jnp.where(open_ & has_below, below, 0.0)
    for i in range(SR + 4):
        wide[i, 0:1, 0:C] = side_in[0, i : i + 1, C : 2 * C].astype(BF)
        wide[i, TC - 1 : TC, 2 * C :] = side_in[1, i : i + 1, C : 2 * C].astype(BF)

    tall = 6
    for i in range(0, SR + 2, tall):
        first[i : i + tall] = silu(convolved(i, tall, w1_ref, b1_ref)).astype(BF).reshape(tall, TC, C)
    side_row = lax.broadcasted_iota(jnp.int32, (SR + 2, C), 0)
    inside = ((side_row > 0) | has_above) & ((side_row < SR + 1) | has_below)
    for s, open_ in enumerate((c > 0, c < cols - 1)):
        total = None
        for a in range(3):
            term = jnp.dot(side_in[s, a : a + SR + 2, :].astype(BF), w1_ref[a], preferred_element_type=F32)
            total = term if total is None else total + term
        side_first[s, 0 : SR + 2, :] = jnp.where(inside & open_, silu(total + b1_ref[...]), 0.0)
    for i in range(SR + 2):
        row = first[i].astype(F32)
        if i == 0:
            row = jnp.where(has_above, row, 0.0)
        if i == SR + 1:
            row = jnp.where(has_below, row, 0.0)
        shifts(i, row)
    for i in range(SR + 2):
        wide[i, 0:1, 0:C] = side_first[0, i : i + 1, :].astype(BF)
        wide[i, TC - 1 : TC, 2 * C :] = side_first[1, i : i + 1, :].astype(BF)
    block_rows = PH // 2

    count = PATCHES // 2
    values = (values0, values1)

    def half_of(q, owner, h):
        return values[q].at[pl.ds(owner * PATCHES + h * count, count)]

    def gather_copy(q, owner, h, way, step, src):
        return pltpu.make_async_remote_copy(
            src_ref=src, dst_ref=half_of(q, owner, h), send_sem=gather_send.at[q, way, step],
            recv_sem=gather_recv.at[q, way, step], device_id=((after, before)[way], r, c), device_id_type=MESH,
        )

    gathers = []

    def gather_start(q, h):
        for way in range(2):
            copy = gather_copy(q, z, h, way, h, mine.at[q, pl.ds(h * count, count)])
            copy.start()
            gathers.append(copy)

    near = (before, after)

    def gather_relay(q):
        for way in range(2):
            gather_copy(q, near[way], way, way, way, half_of(q, near[way], way)).wait_recv()
            copy = gather_copy(q, near[way], way, way, 2, half_of(q, near[way], way))
            copy.start()
            gathers.append(copy)

    def gather_finish(q):
        for way in range(2):
            gather_copy(q, near[way], 1 - way, way, 1 - way, half_of(q, near[way], 1 - way)).wait_recv()
        for way in range(2):
            gather_copy(q, across, way, way, 2, half_of(q, across, way)).wait_recv()

    for h in range(2):
        halves, others = [], []
        for i in range(h * PH, (h + 1) * PH, block_rows):
            v = convolved(i, block_rows, w2_ref, b2_ref).reshape(block_rows, TC, C)
            v = (tile[i : i + block_rows].astype(F32) + v).astype(BF)
            grid_ref[i : i + block_rows] = v
            halves.append(v)
        for w in range(WIDE):
            lower = halves[0][:, w * PW : (w + 1) * PW, :].reshape(FOLD, C)
            upper = halves[1][:, w * PW : (w + 1) * PW, :].reshape(FOLD, C)
            mine[0, h * count + w] = jnp.where(low_lanes, lower, swapped(upper).astype(BF))
            others.append((h * count + w, lower, upper))
        gather_start(0, h)
        for at, lower, upper in others:
            mine[1, at] = jnp.where(low_lanes, swapped(lower).astype(BF), upper)
    grid_copy = pltpu.make_async_copy(grid_ref, grid_hbm, grid_sem)
    grid_copy.start()
    for q in range(2):
        values[q][pl.ds(z * PATCHES, PATCHES)] = mine[q]
    lax.fori_loop(2 * quarter, 3 * quarter, prepare, 0)
    gather_relay(0)
    gather_start(1, 0)
    gather_start(1, 1)
    lax.fori_loop(3 * quarter, tiles, prepare, 0)
    gather_finish(0)

    def swap_values(q):
        def some(i, carry):
            for u in range(PATCHES):
                values_swapped[q, i * PATCHES + u] = swapped(values[q][i * PATCHES + u]).astype(BF)
            return carry

        lax.fori_loop(0, ORBITS, some, 0)

    def read(q, j, target_ref):
        a, b = [links_smem[2, j * MOST + i] for i in range(MOST)]
        right = jnp.concatenate([
            jnp.where(low_lanes, values[q][a], zero_block), jnp.where(low_lanes, values_swapped[q, a], zero_block),
            jnp.where(low_lanes, zero_block, values_swapped[q, b]), jnp.where(low_lanes, zero_block, values[q][b]),
        ], axis=0)
        target_ref[j] = (jnp.dot(turned[j], right, preferred_element_type=F32) * inverse[j]).astype(BF)

    back = (back0, back1)

    def back_copy(q, j):
        return pltpu.make_async_remote_copy(
            src_ref=back_out.at[q, j], dst_ref=back[q].at[j], send_sem=back_send.at[q, j], recv_sem=back_recv.at[q, j],
            device_id=(z, *source(j)), device_id_type=MESH,
        )

    def read_and_send(q):
        def step(p, carry):
            for u in range(2):
                read(q, 2 * p + u, back_out.at[q])
            for u in range(2):
                back_copy(q, 2 * p + u).start()
            return carry

        return step

    def read_first(q):
        read(q, 1, back_out.at[q])
        back_copy(q, 1).start()
        read(q, 0, back[q])

    swap_values(0)
    read_first(0)
    lax.fori_loop(1, quarter, read_and_send(0), 0)
    gather_relay(1)
    lax.fori_loop(quarter, tiles // 2, read_and_send(0), 0)
    gather_finish(1)
    swap_values(1)
    read_first(1)
    lax.fori_loop(1, tiles // 2, read_and_send(1), 0)

    def arrive(q):
        def step(j, carry):
            back_copy(q, j).wait_recv()
            return carry

        return step

    together = min(4, blocks)

    def combine(q):
        def step(i, carry):
            for u in range(together):
                b = i * together + u
                t = tile_of[b]
                k = (t // cols + rows - r) % rows * cols + (t % cols + cols - c) % cols
                j = jnp.where(k == 0, 0, (k - 1 + tiles - 1 - tiles // 2) % (tiles - 1) + 1)
                in_place = jnp.full((BLK, C), (table_smem[t, 0] == b).astype(jnp.int32)) == 1 - q
                x = back[q][j].astype(F32)
                value = (features[b].astype(F32) + jnp.where(in_place, x, swapped(x))).astype(BF)
                out_ref[b] = value if q == 0 else jnp.where(low_lanes, out_ref[b], value)
            if q == 1:
                store(i).start()
            return carry

        return step

    def store(i):
        some = pl.ds(i * together, together)
        return pltpu.make_async_copy(out_ref.at[some], out_hbm.at[some], store_sem.at[i])

    for q in range(2):
        lax.fori_loop(1, tiles, arrive(q), 0)
        lax.fori_loop(0, blocks // together, combine(q), 0)

    def stored(i, carry):
        store(i).wait()
        return carry

    def sent(j, carry):
        for q in range(2):
            out_copy(q, j).wait_send()
            back_copy(q, j).wait_send()
        return carry

    lax.fori_loop(1, tiles, sent, 0)
    lax.fori_loop(0, blocks // together, stored, 0)
    grid_copy.wait()
    for q in range(2):
        for copies in rings[q]:
            for copy in copies:
                copy.wait_send()
    for copy in gathers + edge_copies:
        copy.wait_send()


def copy_kernel(pieces, out_main, grid_main, out_hbm, grid_hbm, out_v, grid_v, in_sem, to_sem):
    rows = out_v.shape[0] // pieces
    sets = [(out_main.at[pl.ds(i * rows, rows)], out_v.at[pl.ds(i * rows, rows)], out_hbm.at[pl.ds(i * rows, rows)]) for i in range(pieces)]
    sets.append((grid_main, grid_v, grid_hbm))
    ins = [pltpu.make_async_copy(a, b, in_sem.at[i]) for i, (a, b, _) in enumerate(sets)]
    outs = [pltpu.make_async_copy(b, d, to_sem.at[i]) for i, (_, b, d) in enumerate(sets)]
    for x in ins:
        x.start()
    for x, y in zip(ins, outs):
        x.wait()
        y.start()
    for y in outs:
        y.wait()


def local(
    obs_feat, obs_offset, obs_cells, block_tile, block_patch, w_embed, b_embed, w_proj, b_proj, density_weight,
    w_first, b_first, w_second, b_second,
):
    blocks = block_tile.shape[0]
    rows, cols = lax.axis_size("rows"), lax.axis_size("cols")
    tiles = rows * cols
    slots = tiles * MOST
    patches = ORBITS * PATCHES

    vm = pl.BlockSpec(memory_space=VMEM)
    sm = pl.BlockSpec(memory_space=SMEM)
    part_rows = PATCHES * FOLD + DENS
    dma = pltpu.SemaphoreType.DMA
    obs_out, grid_out = pl.pallas_call(
        functools.partial(main_kernel, rows, cols, blocks),
        grid=(1,),
        out_shape=(jax.ShapeDtypeStruct((blocks, BLK, C), BF), jax.ShapeDtypeStruct((SR, TC, C), BF)),
        in_specs=[sm, vm, vm] + [pl.BlockSpec(memory_space=pl.ANY)] * 5 + [vm] * 7,
        out_specs=(pl.BlockSpec(memory_space=pl.ANY),) * 2,
        scratch_shapes=[
            VMEM((blocks, BLK, C), BF),
            VMEM((SR, TC, C), BF),
            VMEM((blocks, BLK, C), BF),
            VMEM((2, blocks * BLK), BF),
            VMEM((8, blocks * BLK), jnp.int32),
            VMEM((3, 3 * C, C), BF),
            VMEM((3, 3 * C, C), BF),
            VMEM((tiles, C), jnp.int32),
            SMEM((tiles, C), jnp.int32),
            VMEM((blocks, BLK, C), BF),
            VMEM((blocks, BLK, C), BF),
            VMEM((blocks, 8, BLK), F32),
            VMEM((tiles, BLK + META, C), BF),
            VMEM((tiles, BLK, C), BF),
            VMEM((tiles, BLK + META, C), BF),
            VMEM((tiles, BLK, C), BF),
            VMEM((slots, CELLS, BLK), BF),
            VMEM((slots, 8, BLK), F32),
            VMEM((tiles, BLK, MOST * CELLS), BF),
            VMEM((tiles, BLK, C), F32),
            VMEM((slots + 1, FOLD, C), F32),
            VMEM((slots + 1, FOLD, C), F32),
            VMEM((slots + 1, 8, CELLS), F32),
            VMEM((8, C), jnp.int32),
            SMEM((8, C), jnp.int32),
            VMEM((ORBITS, DENS, C), F32),
            VMEM((ORBITS, part_rows, C), BF),
            VMEM((ORBITS, part_rows, C), BF),
            VMEM((ORBITS, DENS, C), BF),
            VMEM((2, part_rows, C), BF),
            VMEM((2, part_rows, C), BF),
            VMEM((2, 2, part_rows, C), BF),
            VMEM((PATCHES, FOLD, C), F32),
            VMEM((SR, TC, C), BF),
            VMEM((SR + 4, TC, 3 * C), BF),
            VMEM((SR + 2, TC, C), BF),
            VMEM((2, SR + 8, 3 * C), F32),
            VMEM((2, SR + 8, C), F32),
            VMEM((2, 2, SR, C), BF),
            VMEM((2, 2, TC, C), BF),
            VMEM((6, 2, SR, C), BF),
            VMEM((2, PATCHES, FOLD, C), BF),
            VMEM((patches, FOLD, C), BF),
            VMEM((patches, FOLD, C), BF),
            VMEM((2, patches, FOLD, C), BF),
            VMEM((2, tiles, BLK, C), BF),
            VMEM((tiles, BLK, C), BF),
            VMEM((tiles, BLK, C), BF),
            dma((2, tiles)),
            dma((2, tiles)),
            dma((2, 2, 3)),
            dma((2, 2, 3)),
            dma((8,)),
            dma((8,)),
            dma((2, 2, 3)),
            dma((2, 2, 3)),
            dma((2, tiles)),
            dma((2, tiles)),
            dma((2,)),
            dma((6,)),
            dma((blocks // min(4, blocks),)),
            dma,
        ],
        compiler_params=pltpu.CompilerParams(collective_id=0, has_side_effects=True, vmem_limit_bytes=63000000),
        name="encode",
    )(
        block_tile, block_tile[None, :], block_patch[None, :], obs_feat.reshape(blocks, BLK, C), obs_offset, obs_cells,
        w_first.reshape(3, 3 * C, C), w_second.reshape(3, 3 * C, C), w_embed, b_embed[None, :], w_proj, b_proj[None, :],
        density_weight[None, :], b_first[None, :], b_second[None, :],
    )
    pieces = 4
    obs_out, grid_out = pl.pallas_call(
        functools.partial(copy_kernel, pieces),
        out_shape=(jax.ShapeDtypeStruct((blocks, BLK, C), BF), jax.ShapeDtypeStruct((SR, TC, C), BF)),
        in_specs=[pl.BlockSpec(memory_space=pl.ANY)] * 2,
        out_specs=(pl.BlockSpec(memory_space=pl.ANY),) * 2,
        scratch_shapes=[VMEM((blocks, BLK, C), BF), VMEM((SR, TC, C), BF), dma((pieces + 1,)), dma((pieces + 1,))],
        name="copy_out",
    )(obs_out, grid_out)
    return (obs_out.reshape(obs_feat.shape), grid_out)


def solution(mesh):
    by_device = P(("orbits", "rows", "cols"))
    in_specs = (
        P(("orbits", "rows", "cols"), None), P(None, ("orbits", "rows", "cols")), P(None, ("orbits", "rows", "cols")),
        by_device, by_device, P(), P(), P(), P(), P(), P(), P(), P(), P(),
    )
    out_specs = (P(("orbits", "rows", "cols"), None), P(("orbits", "rows"), "cols", None))
    return jax.shard_map(local, mesh=mesh, in_specs=in_specs, out_specs=out_specs, check_vma=False)
```

```python
import functools

import jax
import jax.numpy as jnp
from jax import lax
from jax.experimental import pallas as pl
from jax.experimental.pallas import tpu as pltpu
from jax.sharding import PartitionSpec as P

PH = 8
PW = 32
SR = 16
TC = 128
BLK = 128
C = 128
HALF = C // 2
MOST = 2
CELLS = PH * PW
FOLD = CELLS // 2
WIDE = TC // PW
PATCHES = SR // PH * WIDE
DENS = 2 * PATCHES
META = 8
DEAD = -128.0
ORBITS = 4
MESH = pl.DeviceIdType.MESH
VMEM = pltpu.VMEM
SMEM = pltpu.SMEM
BF = jnp.bfloat16
F32 = jnp.float32


def window_weights(meta_rows):
    off_r, off_c, anchor = meta_rows[0:1], meta_rows[1:2], meta_rows[2:3]
    anchor_r = jnp.floor(anchor * (1.0 / PW))
    anchor_c = anchor - anchor_r * PW
    tap_r = lax.broadcasted_iota(jnp.int32, (PH, BLK), 0).astype(F32) - anchor_r
    tap_c = lax.broadcasted_iota(jnp.int32, (PW, BLK), 0).astype(F32) - anchor_c
    delta_r = tap_r - 1.5 - off_r
    delta_c = tap_c - 1.5 - off_c
    weight_r = jnp.where((tap_r >= 0.0) & (tap_r < 4.0), jnp.exp(delta_r * delta_r * -0.5), 0.0)
    weight_c = jnp.where((tap_c >= 0.0) & (tap_c < 4.0), jnp.exp(delta_c * delta_c * -0.5), 0.0)
    return jnp.concatenate([(weight_r[r : r + 1] * weight_c).astype(BF) for r in range(PH)], axis=0)


def swapped(x):
    return pltpu.roll(x.astype(F32), HALF, 1)


def main_kernel(
    rows, cols, blocks,
    tile_of, tile_row, patch_row, feat_hbm, off_hbm, cells_hbm, w1_hbm, w2_hbm,
    we_ref, be_ref, wp_ref, bp_ref, dw_ref, b1_ref, b2_ref,
    out_hbm, grid_hbm,
    out_ref, grid_ref, feat_ref, off_ref, cells_ref, w1_ref, w2_ref, table, table_smem,
    features, swapped_features, block_meta, send0, send1, got0, got1, matrices, patch_rows,
    turned, inverse, sums0, sums1, density_sums, links, links_smem, density_rows, part0, part1, density_part, relay_in, relay_out, part_in,
    packed, tile, wide, first, side_in, side_first, col_out, row_in, col_in, mine, values0, values1, values_swapped, back_out, back0, back1,
    out_send, out_recv, ring_send, ring_recv, edge_send, edge_recv, gather_send, gather_recv, back_send, back_recv, link_sem, load_sem, store_sem, grid_sem,
):
    z, r, c = lax.axis_index("orbits"), lax.axis_index("rows"), lax.axis_index("cols")
    tiles = rows * cols
    slots = tiles * MOST
    stripes = ORBITS * rows
    stripe = z * rows + r
    after, before = (z + 1) % ORBITS, (z + ORBITS - 1) % ORBITS
    across = (z + 2) % ORBITS

    def offset_of(j):
        return (j - 1 + tiles // 2) % (tiles - 1) + 1

    def target(j):
        k = offset_of(j)
        return (r + k // cols) % rows, (c + k % cols) % cols

    def source(j):
        k = offset_of(j)
        return (r + rows - k // cols) % rows, (c + cols - k % cols) % cols

    def edge_device(up, side):
        other = (stripe + stripes + up) % stripes
        return (other // rows, other % rows, (c + cols + side) % cols)

    edges = ((-1, 0), (1, 0), (-1, -1), (0, -1), (1, -1), (-1, 1), (0, 1), (1, 1))
    half_blocks = blocks // 2
    loads = [
        pltpu.make_async_copy(feat_hbm.at[pl.ds(0, half_blocks)], feat_ref.at[pl.ds(0, half_blocks)], load_sem.at[0]),
        pltpu.make_async_copy(feat_hbm.at[pl.ds(half_blocks, half_blocks)], feat_ref.at[pl.ds(half_blocks, half_blocks)], load_sem.at[1]),
        pltpu.make_async_copy(off_hbm, off_ref, load_sem.at[2]),
        pltpu.make_async_copy(cells_hbm.at[pl.ds(0, 8)], cells_ref, load_sem.at[3]),
        pltpu.make_async_copy(w1_hbm, w1_ref, load_sem.at[4]),
        pltpu.make_async_copy(w2_hbm, w2_ref, load_sem.at[5]),
    ]
    for load in loads:
        load.start()

    barrier = pltpu.get_barrier_semaphore()

    def greet(j, carry):
        pl.semaphore_signal(barrier, inc=1, device_id=(z, *target(j)), device_id_type=MESH)
        return carry

    lax.fori_loop(1, tiles, greet, 0)
    for other in (after, before):
        pl.semaphore_signal(barrier, inc=1, device_id=(other, r, c), device_id_type=MESH)
    for up, side in edges:
        pl.semaphore_signal(barrier, inc=1, device_id=edge_device(up, side), device_id_type=MESH)

    square = (tiles, blocks)
    block_id = lax.broadcasted_iota(jnp.int32, square, 1).astype(F32)
    hit = tile_row[...] == lax.broadcasted_iota(jnp.int32, square, 0)
    lowest = jnp.min(jnp.where(hit, block_id, float(blocks)), axis=1, keepdims=True)
    highest = jnp.max(jnp.where(hit, block_id, -1.0), axis=1, keepdims=True)
    row_patches = patch_row[...].astype(F32)
    patch_low = jnp.max(jnp.where(block_id == lowest, row_patches, -1.0), axis=1, keepdims=True)
    patch_high = jnp.max(jnp.where((block_id == highest) & (highest > lowest), row_patches, -1.0), axis=1, keepdims=True)
    entry = lax.broadcasted_iota(jnp.int32, (tiles, C), 1)
    found = jnp.where(entry == 0, lowest, jnp.where(entry == 1, highest, jnp.where(entry == 2, patch_low, patch_high)))
    found = found.astype(jnp.int32)
    table[...] = jnp.where(entry < 2, jnp.clip(found, 0, blocks - 1), found)
    table_copy = pltpu.make_async_copy(table, table_smem, link_sem.at[1])
    table_copy.start()

    group = min(8, half_blocks)
    proj = jnp.concatenate([wp_ref[...], swapped(wp_ref[...]).astype(BF)], axis=1)
    proj_bias = jnp.concatenate([bp_ref[...], jnp.concatenate([bp_ref[:, HALF:], bp_ref[:, :HALF]], axis=1)], axis=1)

    def embed(i, carry):
        at = pl.ds(i * group, group)
        x = feat_ref[at].reshape(group * BLK, C)
        v = jnp.dot(x, we_ref[...], preferred_element_type=F32) + be_ref[...]
        hidden = (v / (1.0 + jnp.exp(-v))).astype(BF)
        both = (jnp.dot(hidden, proj, preferred_element_type=F32) + proj_bias).astype(BF)
        features[at] = both[:, :C].reshape(group, BLK, C)
        swapped_features[at] = both[:, C:].reshape(group, BLK, C)
        return carry

    loads[0].wait()
    lax.fori_loop(0, half_blocks // group, embed, 0)
    loads[1].wait()
    lax.fori_loop(half_blocks // group, blocks // group, embed, 0)
    loads[2].wait()
    loads[3].wait()
    row_id = lax.broadcasted_iota(jnp.int32, (8, BLK), 0)
    row_kind = row_id % 4
    for b in range(blocks):
        lanes = slice(b * BLK, (b + 1) * BLK)
        off = off_ref[:, lanes].astype(F32)
        meta = jnp.where(row_kind == 0, off[0:1], off[1:2])
        block_meta[b] = jnp.where(row_kind == 2, cells_ref[0:1, lanes].astype(F32), meta)
    table_copy.wait()

    low_lanes = lax.broadcasted_iota(jnp.int32, (BLK, C), 1) < HALF

    def pack(t, dst0, dst1, j):
        at = [table_smem[t, i] for i in range(MOST)]
        dst0[j, :BLK, :] = jnp.where(low_lanes, features[at[0]], swapped_features[at[1]])
        dst1[j] = jnp.where(low_lanes, swapped_features[at[0]], features[at[1]])
        patch = jnp.where(row_id < 4, table_smem[t, 2].astype(F32), table_smem[t, 3].astype(F32))
        meta = jnp.where(row_id < 4, block_meta[at[0]], block_meta[at[1]])
        meta = jnp.where((row_kind == 2) & (patch < 0.0), DEAD, meta)
        dst0[j, BLK:, :] = jnp.where(row_kind == 3, patch, meta).astype(BF)

    sends, gots = (send0, send1), (got0, got1)

    def out_copy(q, j):
        return pltpu.make_async_remote_copy(
            src_ref=sends[q].at[j], dst_ref=gots[q].at[j], send_sem=out_send.at[q, j], recv_sem=out_recv.at[q, j],
            device_id=(z, *target(j)), device_id_type=MESH,
        )

    pl.semaphore_wait(barrier, tiles - 1 + 2 + len(edges))

    def start_first(j, carry):
        tr, tc = target(j)
        pack(tr * cols + tc, send0, send1, j)
        out_copy(0, j).start()
        return carry

    def start_second(j, carry):
        out_copy(1, j).start()
        return carry

    lax.fori_loop(1, tiles, start_first, 0)
    lax.fori_loop(1, tiles, start_second, 0)
    pack(r * cols + c, got0, got1, 0)

    ones = jnp.ones((8, BLK), BF)
    zero_block = jnp.zeros((BLK, C), BF)
    sums0[0] = jnp.zeros((FOLD, C), F32)
    sums1[0] = jnp.zeros((FOLD, C), F32)
    density_sums[0] = jnp.zeros((8, CELLS), F32)

    def folded(matrix, stream, i):
        other = swapped(stream).astype(BF)
        low, high = (stream, other) if i == 0 else (other, stream)
        right = jnp.concatenate([jnp.where(low_lanes, low, zero_block), jnp.where(low_lanes, zero_block, high)], axis=0)
        left = jnp.concatenate([matrix[:FOLD], matrix[FOLD:]], axis=1)
        return jnp.dot(left, right, preferred_element_type=F32)

    def receive0(j):
        metas = got0[j, BLK:, :].astype(F32)
        stream = got0[j, :BLK, :]
        for i in range(MOST):
            meta = metas[4 * i : 4 * i + 4]
            matrix = window_weights(meta)
            matrices[j * MOST + i] = matrix
            patch_rows[j * MOST + i] = jnp.broadcast_to(meta[3:4], (8, BLK))
            sums0[1 + j * MOST + i] = folded(matrix, stream, i)
            density_sums[1 + j * MOST + i] = lax.dot_general(ones, matrix, (((1,), (1,)), ((), ())), preferred_element_type=F32)

    unroll = min(4, tiles // 2)

    def step0(p, carry):
        for u in range(unroll):
            out_copy(0, p * unroll + u).wait_recv()
        for u in range(unroll):
            receive0(p * unroll + u)
        return carry

    for u in range(1, unroll):
        out_copy(0, u).wait_recv()
    for u in range(unroll):
        receive0(u)
    lax.fori_loop(1, tiles // unroll, step0, 0)

    by_row = jnp.concatenate([patch_rows[s, 0:1, :] for s in range(slots)], axis=0)
    slot_row = lax.broadcasted_iota(jnp.int32, (slots, C), 0)
    lane = lax.broadcasted_iota(jnp.int32, (slots, C), 1)
    by_lane = jnp.sum(jnp.where(slot_row == lane, by_row, 0.0), axis=0, keepdims=True)
    earlier = jnp.max(jnp.where((by_row == by_lane) & (slot_row < lane), slot_row + 1, 0), axis=0, keepdims=True)
    latest = jnp.max(jnp.where(by_row == lane.astype(F32), slot_row + 1, 0), axis=0, keepdims=True)
    link_id = lax.broadcasted_iota(jnp.int32, (8, C), 0)
    ids = jnp.clip(by_lane.astype(jnp.int32), 0, ORBITS * PATCHES - 1)
    links[...] = jnp.where(link_id == 0, earlier, jnp.where(link_id == 1, latest, ids))
    link_copy = pltpu.make_async_copy(links, links_smem, link_sem.at[0])
    link_copy.start()
    link_copy.wait()

    def chain(s, carry):
        e = links_smem[0, s]
        sums0[s + 1] = sums0[s + 1] + sums0[e]
        density_sums[s + 1] = density_sums[s + 1] + density_sums[e]
        return carry

    lax.fori_loop(0, slots, chain, 0)

    for p in range(ORBITS * PATCHES):
        at = links_smem[1, p]
        owner, local_patch = p // PATCHES, p % PATCHES
        part0[owner, local_patch * FOLD : (local_patch + 1) * FOLD, :] = sums0[at].astype(BF)
        row = density_sums[at]
        density_rows[owner, local_patch : local_patch + 1, :] = row[0:1, :C]
        density_rows[owner, PATCHES + local_patch : PATCHES + local_patch + 1, :] = row[0:1, C:]
    for owner in range(ORBITS):
        density_part[owner] = density_rows[owner].astype(BF)
        part0[owner, PATCHES * FOLD :, :] = density_part[owner]

    cut = PATCHES * FOLD // 2
    parts = (part0, part1)

    def ring_copy(q, src, dst, way, step, other):
        return pltpu.make_async_remote_copy(
            src_ref=src, dst_ref=dst, send_sem=ring_send.at[q, way, step], recv_sem=ring_recv.at[q, way, step],
            device_id=(other, r, c), device_id_type=MESH,
        )

    def sides(q):
        low, high = pl.ds(0, cut), pl.ds(cut, cut + (DENS if q == 0 else 0))
        return ((0, after, low, high), (1, before, high, low))

    rings = {}

    def ring_start(q, which):
        if q not in rings:
            rings[q] = []
            for way, other, passed, direct in sides(q):
                relay = ring_copy(q, parts[q].at[across, passed], relay_in.at[q, passed], way, 0, other)
                straight = ring_copy(q, parts[q].at[other, direct], part_in.at[q, way, direct], way, 1, other)
                summed = ring_copy(q, relay_out.at[q, passed], part_in.at[q, way, passed], way, 2, other)
                rings[q].append((relay, straight, summed))
        for relay, straight, summed in rings[q]:
            (relay if which == "relay" else straight).start()

    def ring_relay(q):
        for way, other, passed, direct in sides(q):
            relay, straight, summed = rings[q][way]
            relay.wait_recv()
            total = parts[q][other, passed].astype(F32) + relay_in[q, passed].astype(F32)
            relay_out[q, passed] = total.astype(BF)
            summed.start()

    def ring_finish(q):
        for relay, straight, summed in rings[q]:
            straight.wait_recv()
        for relay, straight, summed in rings[q]:
            summed.wait_recv()

    ring_start(0, "relay")
    ring_start(0, "straight")

    def receive1(j):
        stream = got1[j]
        for i in range(MOST):
            s = j * MOST + i
            sums1[s + 1] = folded(matrices[s], stream, i) + sums1[links_smem[0, s]]

    def step1(p, carry):
        for j in (2 * p, 2 * p + 1):
            out_copy(1, j).wait_recv()
        for j in (2 * p, 2 * p + 1):
            receive1(j)
        return carry

    receive1(0)
    out_copy(1, 1).wait_recv()
    receive1(1)
    middle = max(1, 3 * tiles // 8)
    lax.fori_loop(1, middle, step1, 0)
    ring_relay(0)
    lax.fori_loop(middle, tiles // 2, step1, 0)
    def fill_part1(owner):
        for p in range(PATCHES):
            part1[owner, p * FOLD : (p + 1) * FOLD, :] = sums1[links_smem[1, owner * PATCHES + p]].astype(BF)

    fill_part1(across)
    ring_start(1, "relay")
    fill_part1(after)
    fill_part1(before)
    ring_start(1, "straight")
    fill_part1(z)
    ring_finish(0)

    zero_lanes = jnp.zeros((CELLS, C), BF)
    one_cells = jnp.ones((CELLS, C), BF)
    cell_low = lax.broadcasted_iota(jnp.int32, (CELLS, C), 1) < HALF
    one_pair = jnp.concatenate([jnp.where(cell_low, one_cells, zero_lanes), jnp.where(cell_low, zero_lanes, one_cells)], axis=0)

    def prepare(j, carry):
        turned[j] = jnp.concatenate([matrices[j * MOST].T, matrices[j * MOST + 1].T], axis=1)
        total = jnp.dot(turned[j], one_pair, preferred_element_type=F32)
        inverse[j] = 1.0 / jnp.where(total > 0.0, total, 1.0)
        return carry

    quarter = max(1, tiles // 4)

    tail = pl.ds(PATCHES * FOLD, DENS)
    dens_in = jnp.concatenate([part0[z, tail], part_in[0, 0, tail], part_in[0, 1, tail]], axis=0)
    pick_shape = (3 * DENS, DENS * C)
    picked = lax.broadcasted_iota(jnp.int32, pick_shape, 0) % DENS == lax.broadcasted_iota(jnp.int32, pick_shape, 1) // C
    density_all = lax.dot_general(dens_in, picked.astype(BF), (((0,), (0,)), ((), ())), preferred_element_type=F32)
    weight_swapped = jnp.concatenate([dw_ref[:, HALF:], dw_ref[:, :HALF]], axis=1)
    low_row = lax.broadcasted_iota(jnp.int32, (1, C), 1) < HALF
    weights = (jnp.where(low_row, dw_ref[...], weight_swapped), jnp.where(low_row, weight_swapped, dw_ref[...]))

    def grid_value(q, p):
        cells = pl.ds(p * FOLD, FOLD)
        density = jnp.where(
            low_lanes, density_all[:, p * C : (p + 1) * C], density_all[:, (PATCHES + p) * C : (PATCHES + p + 1) * C]
        )
        total = parts[q][z, cells].astype(F32) + part_in[q, 0, cells].astype(F32) + part_in[q, 1, cells].astype(F32)
        return total / jnp.maximum(density, 1.0) + weights[q] * (density / (1.0 + density))

    for p in range(PATCHES):
        packed[p] = grid_value(0, p)
    lax.fori_loop(0, quarter, prepare, 0)
    ring_relay(1)
    lax.fori_loop(quarter, 2 * quarter, prepare, 0)
    ring_finish(1)
    for p in range(PATCHES):
        x0, x1 = packed[p], grid_value(1, p)
        top, left = p // WIDE * PH, p % WIDE * PW
        lower = jnp.where(low_lanes, x0, swapped(x1)).astype(BF)
        upper = jnp.where(low_lanes, swapped(x0), x1).astype(BF)
        tile[top : top + PH // 2, left : left + PW, :] = lower.reshape(PH // 2, PW, C)
        tile[top + PH // 2 : top + PH, left : left + PW, :] = upper.reshape(PH // 2, PW, C)

    for i in range(SR):
        for k in range(2):
            col_out[0, k, i : i + 1, :] = tile[i, k : k + 1, :]
            col_out[1, k, i : i + 1, :] = tile[i, TC - 2 + k : TC - 1 + k, :]
    edge_copies = []
    for e, (up, side) in enumerate(edges):
        if side == 0:
            src, dst = tile.at[pl.ds(0 if up < 0 else SR - 2, 2)], row_in.at[e]
        else:
            src, dst = col_out.at[0 if side < 0 else 1], col_in.at[e - 2]
        edge_copies.append(pltpu.make_async_remote_copy(
            src_ref=src, dst_ref=dst, send_sem=edge_send.at[e], recv_sem=edge_recv.at[e],
            device_id=edge_device(up, side), device_id_type=MESH,
        ))
    for copy in edge_copies:
        copy.start()

    def shifts(row, centre):
        centre = centre.astype(F32)
        wide[row, :, 0:C] = pltpu.roll(centre, 1, 0).astype(BF)
        wide[row, :, C : 2 * C] = centre.astype(BF)
        wide[row, :, 2 * C :] = pltpu.roll(centre, TC - 1, 0).astype(BF)

    def convolved(i, height, w_ref, b_ref):
        total = None
        for a in range(3):
            x = wide[pl.ds(i + a, height)].reshape(height * TC, 3 * C)
            term = jnp.dot(x, w_ref[a], preferred_element_type=F32)
            total = term if total is None else total + term
        return total + b_ref[...]

    def silu(v):
        return v / (1.0 + jnp.exp(-v))

    for i in range(SR):
        shifts(i + 2, tile[i])
    loads[4].wait()
    loads[5].wait()
    for copy in edge_copies:
        copy.wait_recv()
    has_above, has_below = stripe > 0, stripe < stripes - 1
    for k in range(2):
        shifts(k, jnp.where(has_above, row_in[1, k].astype(F32), 0.0))
        shifts(SR + 2 + k, jnp.where(has_below, row_in[0, k].astype(F32), 0.0))
    for s, (first_edge, open_) in enumerate(((3, c > 0), (0, c < cols - 1))):
        own_at, own_lanes = (0, slice(2 * C, 3 * C)) if s == 0 else (TC - 1, slice(0, C))
        side_in[s, 2 : SR + 2, own_lanes] = col_out[s, s].astype(F32)
        for k in range(2):
            side_in[s, k : k + 1, own_lanes] = jnp.where(has_above, row_in[1, k, own_at : own_at + 1, :].astype(F32), 0.0)
            side_in[s, SR + 2 + k : SR + 3 + k, own_lanes] = jnp.where(has_below, row_in[0, k, own_at : own_at + 1, :].astype(F32), 0.0)
            lanes = slice((k + s) * C, (k + s + 1) * C)
            above = col_in[first_edge + 2, k].astype(F32)[SR - 2 :]
            below = col_in[first_edge, k].astype(F32)[:2]
            side_in[s, 0:2, lanes] = jnp.where(open_ & has_above, above, 0.0)
            side_in[s, 2 : SR + 2, lanes] = jnp.where(open_, col_in[first_edge + 1, k].astype(F32), 0.0)
            side_in[s, SR + 2 : SR + 4, lanes] = jnp.where(open_ & has_below, below, 0.0)
    for i in range(SR + 4):
        wide[i, 0:1, 0:C] = side_in[0, i : i + 1, C : 2 * C].astype(BF)
        wide[i, TC - 1 : TC, 2 * C :] = side_in[1, i : i + 1, C : 2 * C].astype(BF)

    tall = 6
    for i in range(0, SR + 2, tall):
        first[i : i + tall] = silu(convolved(i, tall, w1_ref, b1_ref)).astype(BF).reshape(tall, TC, C)
    side_row = lax.broadcasted_iota(jnp.int32, (SR + 2, C), 0)
    inside = ((side_row > 0) | has_above) & ((side_row < SR + 1) | has_below)
    for s, open_ in enumerate((c > 0, c < cols - 1)):
        total = None
        for a in range(3):
            term = jnp.dot(side_in[s, a : a + SR + 2, :].astype(BF), w1_ref[a], preferred_element_type=F32)
            total = term if total is None else total + term
        side_first[s, 0 : SR + 2, :] = jnp.where(inside & open_, silu(total + b1_ref[...]), 0.0)
    for i in range(SR + 2):
        row = first[i].astype(F32)
        if i == 0:
            row = jnp.where(has_above, row, 0.0)
        if i == SR + 1:
            row = jnp.where(has_below, row, 0.0)
        shifts(i, row)
    for i in range(SR + 2):
        wide[i, 0:1, 0:C] = side_first[0, i : i + 1, :].astype(BF)
        wide[i, TC - 1 : TC, 2 * C :] = side_first[1, i : i + 1, :].astype(BF)
    block_rows = PH // 2

    count = PATCHES // 2
    values = (values0, values1)

    def half_of(q, owner, h):
        return values[q].at[pl.ds(owner * PATCHES + h * count, count)]

    def gather_copy(q, owner, h, way, step, src):
        return pltpu.make_async_remote_copy(
            src_ref=src, dst_ref=half_of(q, owner, h), send_sem=gather_send.at[q, way, step],
            recv_sem=gather_recv.at[q, way, step], device_id=((after, before)[way], r, c), device_id_type=MESH,
        )

    gathers = []

    def gather_start(q, h):
        for way in range(2):
            copy = gather_copy(q, z, h, way, h, mine.at[q, pl.ds(h * count, count)])
            copy.start()
            gathers.append(copy)

    near = (before, after)

    def gather_relay(q):
        for way in range(2):
            gather_copy(q, near[way], way, way, way, half_of(q, near[way], way)).wait_recv()
            copy = gather_copy(q, near[way], way, way, 2, half_of(q, near[way], way))
            copy.start()
            gathers.append(copy)

    def gather_finish(q):
        for way in range(2):
            gather_copy(q, near[way], 1 - way, way, 1 - way, half_of(q, near[way], 1 - way)).wait_recv()
        for way in range(2):
            gather_copy(q, across, way, way, 2, half_of(q, across, way)).wait_recv()

    for h in range(2):
        halves, others = [], []
        for i in range(h * PH, (h + 1) * PH, block_rows):
            v = convolved(i, block_rows, w2_ref, b2_ref).reshape(block_rows, TC, C)
            v = (tile[i : i + block_rows].astype(F32) + v).astype(BF)
            grid_ref[i : i + block_rows] = v
            halves.append(v)
        for w in range(WIDE):
            lower = halves[0][:, w * PW : (w + 1) * PW, :].reshape(FOLD, C)
            upper = halves[1][:, w * PW : (w + 1) * PW, :].reshape(FOLD, C)
            mine[0, h * count + w] = jnp.where(low_lanes, lower, swapped(upper).astype(BF))
            others.append((h * count + w, lower, upper))
        gather_start(0, h)
        for at, lower, upper in others:
            mine[1, at] = jnp.where(low_lanes, swapped(lower).astype(BF), upper)
    grid_copy = pltpu.make_async_copy(grid_ref, grid_hbm, grid_sem)
    grid_copy.start()
    for q in range(2):
        values[q][pl.ds(z * PATCHES, PATCHES)] = mine[q]
    lax.fori_loop(2 * quarter, 3 * quarter, prepare, 0)
    gather_relay(0)
    gather_start(1, 0)
    gather_start(1, 1)
    lax.fori_loop(3 * quarter, tiles, prepare, 0)
    gather_finish(0)

    def swap_values(q):
        def some(i, carry):
            for u in range(PATCHES):
                values_swapped[q, i * PATCHES + u] = swapped(values[q][i * PATCHES + u]).astype(BF)
            return carry

        lax.fori_loop(0, ORBITS, some, 0)

    def read(q, j, target_ref):
        a, b = [links_smem[2, j * MOST + i] for i in range(MOST)]
        right = jnp.concatenate([
            jnp.where(low_lanes, values[q][a], zero_block), jnp.where(low_lanes, values_swapped[q, a], zero_block),
            jnp.where(low_lanes, zero_block, values_swapped[q, b]), jnp.where(low_lanes, zero_block, values[q][b]),
        ], axis=0)
        target_ref[j] = (jnp.dot(turned[j], right, preferred_element_type=F32) * inverse[j]).astype(BF)

    back = (back0, back1)

    def back_copy(q, j):
        return pltpu.make_async_remote_copy(
            src_ref=back_out.at[q, j], dst_ref=back[q].at[j], send_sem=back_send.at[q, j], recv_sem=back_recv.at[q, j],
            device_id=(z, *source(j)), device_id_type=MESH,
        )

    def read_and_send(q):
        def step(p, carry):
            for u in range(2):
                read(q, 2 * p + u, back_out.at[q])
            for u in range(2):
                back_copy(q, 2 * p + u).start()
            return carry

        return step

    def read_first(q):
        read(q, 1, back_out.at[q])
        back_copy(q, 1).start()
        read(q, 0, back[q])

    swap_values(0)
    read_first(0)
    lax.fori_loop(1, quarter, read_and_send(0), 0)
    gather_relay(1)
    lax.fori_loop(quarter, tiles // 2, read_and_send(0), 0)
    gather_finish(1)
    swap_values(1)
    read_first(1)
    lax.fori_loop(1, tiles // 2, read_and_send(1), 0)

    def arrive(q):
        def step(j, carry):
            back_copy(q, j).wait_recv()
            return carry

        return step

    together = min(4, blocks)

    def combine(q):
        def step(i, carry):
            for u in range(together):
                b = i * together + u
                t = tile_of[b]
                k = (t // cols + rows - r) % rows * cols + (t % cols + cols - c) % cols
                j = jnp.where(k == 0, 0, (k - 1 + tiles - 1 - tiles // 2) % (tiles - 1) + 1)
                in_place = jnp.full((BLK, C), (table_smem[t, 0] == b).astype(jnp.int32)) == 1 - q
                x = back[q][j].astype(F32)
                value = (features[b].astype(F32) + jnp.where(in_place, x, swapped(x))).astype(BF)
                out_ref[b] = value if q == 0 else jnp.where(low_lanes, out_ref[b], value)
            if q == 1:
                store(i).start()
            return carry

        return step

    def store(i):
        some = pl.ds(i * together, together)
        return pltpu.make_async_copy(out_ref.at[some], out_hbm.at[some], store_sem.at[i])

    for q in range(2):
        lax.fori_loop(1, tiles, arrive(q), 0)
        lax.fori_loop(0, blocks // together, combine(q), 0)

    def stored(i, carry):
        store(i).wait()
        return carry

    def sent(j, carry):
        for q in range(2):
            out_copy(q, j).wait_send()
            back_copy(q, j).wait_send()
        return carry

    lax.fori_loop(1, tiles, sent, 0)
    lax.fori_loop(0, blocks // together, stored, 0)
    grid_copy.wait()
    for q in range(2):
        for copies in rings[q]:
            for copy in copies:
                copy.wait_send()
    for copy in gathers + edge_copies:
        copy.wait_send()


def copy_kernel(pieces, out_main, grid_main, out_hbm, grid_hbm, out_v, grid_v, in_sem, to_sem):
    rows = out_v.shape[0] // pieces
    sets = [(out_main.at[pl.ds(i * rows, rows)], out_v.at[pl.ds(i * rows, rows)], out_hbm.at[pl.ds(i * rows, rows)]) for i in range(pieces)]
    sets.append((grid_main, grid_v, grid_hbm))
    ins = [pltpu.make_async_copy(a, b, in_sem.at[i]) for i, (a, b, _) in enumerate(sets)]
    outs = [pltpu.make_async_copy(b, d, to_sem.at[i]) for i, (_, b, d) in enumerate(sets)]
    for x in ins:
        x.start()
    for x, y in zip(ins, outs):
        x.wait()
        y.start()
    for y in outs:
        y.wait()


def local(
    obs_feat, obs_offset, obs_cells, block_tile, block_patch, w_embed, b_embed, w_proj, b_proj, density_weight,
    w_first, b_first, w_second, b_second,
):
    blocks = block_tile.shape[0]
    rows, cols = lax.axis_size("rows"), lax.axis_size("cols")
    tiles = rows * cols
    slots = tiles * MOST
    patches = ORBITS * PATCHES

    vm = pl.BlockSpec(memory_space=VMEM)
    sm = pl.BlockSpec(memory_space=SMEM)
    part_rows = PATCHES * FOLD + DENS
    dma = pltpu.SemaphoreType.DMA
    obs_out, grid_out = pl.pallas_call(
        functools.partial(main_kernel, rows, cols, blocks),
        grid=(1,),
        out_shape=(jax.ShapeDtypeStruct((blocks, BLK, C), BF), jax.ShapeDtypeStruct((SR, TC, C), BF)),
        in_specs=[sm, vm, vm] + [pl.BlockSpec(memory_space=pl.ANY)] * 5 + [vm] * 7,
        out_specs=(pl.BlockSpec(memory_space=pl.ANY),) * 2,
        scratch_shapes=[
            VMEM((blocks, BLK, C), BF),
            VMEM((SR, TC, C), BF),
            VMEM((blocks, BLK, C), BF),
            VMEM((2, blocks * BLK), BF),
            VMEM((8, blocks * BLK), jnp.int32),
            VMEM((3, 3 * C, C), BF),
            VMEM((3, 3 * C, C), BF),
            VMEM((tiles, C), jnp.int32),
            SMEM((tiles, C), jnp.int32),
            VMEM((blocks, BLK, C), BF),
            VMEM((blocks, BLK, C), BF),
            VMEM((blocks, 8, BLK), F32),
            VMEM((tiles, BLK + META, C), BF),
            VMEM((tiles, BLK, C), BF),
            VMEM((tiles, BLK + META, C), BF),
            VMEM((tiles, BLK, C), BF),
            VMEM((slots, CELLS, BLK), BF),
            VMEM((slots, 8, BLK), F32),
            VMEM((tiles, BLK, MOST * CELLS), BF),
            VMEM((tiles, BLK, C), F32),
            VMEM((slots + 1, FOLD, C), F32),
            VMEM((slots + 1, FOLD, C), F32),
            VMEM((slots + 1, 8, CELLS), F32),
            VMEM((8, C), jnp.int32),
            SMEM((8, C), jnp.int32),
            VMEM((ORBITS, DENS, C), F32),
            VMEM((ORBITS, part_rows, C), BF),
            VMEM((ORBITS, part_rows, C), BF),
            VMEM((ORBITS, DENS, C), BF),
            VMEM((2, part_rows, C), BF),
            VMEM((2, part_rows, C), BF),
            VMEM((2, 2, part_rows, C), BF),
            VMEM((PATCHES, FOLD, C), F32),
            VMEM((SR, TC, C), BF),
            VMEM((SR + 4, TC, 3 * C), BF),
            VMEM((SR + 2, TC, C), BF),
            VMEM((2, SR + 8, 3 * C), F32),
            VMEM((2, SR + 8, C), F32),
            VMEM((2, 2, SR, C), BF),
            VMEM((2, 2, TC, C), BF),
            VMEM((6, 2, SR, C), BF),
            VMEM((2, PATCHES, FOLD, C), BF),
            VMEM((patches, FOLD, C), BF),
            VMEM((patches, FOLD, C), BF),
            VMEM((2, patches, FOLD, C), BF),
            VMEM((2, tiles, BLK, C), BF),
            VMEM((tiles, BLK, C), BF),
            VMEM((tiles, BLK, C), BF),
            dma((2, tiles)),
            dma((2, tiles)),
            dma((2, 2, 3)),
            dma((2, 2, 3)),
            dma((8,)),
            dma((8,)),
            dma((2, 2, 3)),
            dma((2, 2, 3)),
            dma((2, tiles)),
            dma((2, tiles)),
            dma((2,)),
            dma((6,)),
            dma((blocks // min(4, blocks),)),
            dma,
        ],
        compiler_params=pltpu.CompilerParams(collective_id=0, has_side_effects=True, vmem_limit_bytes=63000000),
        name="encode",
    )(
        block_tile, block_tile[None, :], block_patch[None, :], obs_feat.reshape(blocks, BLK, C), obs_offset, obs_cells,
        w_first.reshape(3, 3 * C, C), w_second.reshape(3, 3 * C, C), w_embed, b_embed[None, :], w_proj, b_proj[None, :],
        density_weight[None, :], b_first[None, :], b_second[None, :],
    )
    pieces = 4
    obs_out, grid_out = pl.pallas_call(
        functools.partial(copy_kernel, pieces),
        out_shape=(jax.ShapeDtypeStruct((blocks, BLK, C), BF), jax.ShapeDtypeStruct((SR, TC, C), BF)),
        in_specs=[pl.BlockSpec(memory_space=pl.ANY)] * 2,
        out_specs=(pl.BlockSpec(memory_space=pl.ANY),) * 2,
        scratch_shapes=[VMEM((blocks, BLK, C), BF), VMEM((SR, TC, C), BF), dma((pieces + 1,)), dma((pieces + 1,))],
        name="copy_out",
    )(obs_out, grid_out)
    return (obs_out.reshape(obs_feat.shape), grid_out)


def solution(mesh):
    by_device = P(("orbits", "rows", "cols"))
    in_specs = (
        P(("orbits", "rows", "cols"), None), P(None, ("orbits", "rows", "cols")), P(None, ("orbits", "rows", "cols")),
        by_device, by_device, P(), P(), P(), P(), P(), P(), P(), P(), P(),
    )
    out_specs = (P(("orbits", "rows", "cols"), None), P(("orbits", "rows"), "cols", None))
    return jax.shard_map(local, mesh=mesh, in_specs=in_specs, out_specs=out_specs, check_vma=False)
```
